32 devices in a mesh: group: 2 (over x), lon: 8 (over z, y), lat: 2 (over core).
Axes of the slice: x: 2, y: 2, z: 4, core: 2. Of those that a mesh axis runs over, the one named last changes fastest.
Arguments:
- tokens: bfloat16 [128, 256, 384], P(('group', 'lat'), 'lon'), parts along dimension 0, may hold values from -6 to 6
- visible: int32 [128, 256], P(('group', 'lat'), 'lon'), parts along dimension 0, may hold values 0 or 1
- mask_token: bfloat16 [384], replicated, may hold values from -4 to 4
- norm_gain_table: float32 [2, 384], replicated, may hold values from 0.25 to 1.75
- query_key_value_weight: bfloat16 [2, 384, 1152], replicated, may hold values from -0.3125 to 0.3125
- output_weight: bfloat16 [2, 384, 384], replicated, may hold values from -0.3125 to 0.3125
- cotangent: float32 [128, 256, 384], P(('group', 'lat'), 'lon'), parts along dimension 0, may hold values from -6 to 6
Outputs:
- grad_tokens: float32 [128, 256, 384], P(('group', 'lat'), 'lon'), parts along dimension 0
- grad_qkv: float32 [4, 384, 1152], P('group'), parts along dimension 0
- grad_out: float32 [4, 384, 384], P('group'), parts along dimension 0
- grad_gain: float32 [4, 384], P('group'), parts along dimension 0
The draws below stay inside these ranges and needn't reach their ends.
There are 2 independent parts, one for each index of `group`. The reference program is written for one: setup_inputs(seed, part) draws one part's arguments, and reference() takes and returns one part's arrays. A program takes and returns all parts, laid end to end along the dimension named above; an argument that names none is the same for every part. Nothing has to cross between parts.
Inputs may be any that keep to these rules, and one draw needn't show every extreme that they name: 1 marks a visible token.
All inputs are finite; a program needn't handle non-finite values. No bound on the sum of `visible` on one device may be relied on, other than what follows from the above.
Results may differ from the reference program's by a relative error of at most 0.01.
Values may be sent and summed in bfloat16 or wider, within the bound.
No kernel may reach another device: no remote copies, remote signals or barrier semaphores. Data moves between devices by JAX's collectives and lax.ppermute only.
A program may use at most 320 MiB of HBM per device.

```python
import jax
import jax.numpy as jnp
from jax import lax

D = 384
HEADS = 6
DILATION_STEP = 32
LAYERS = 2
LAT_CELLS = 64
LON_CELLS = 256


def place_ends(entries, own_key, least, largest):
    dims = entries.shape
    place = [jax.random.randint(jax.random.fold_in(own_key, axis), (), 0, dims[axis]) for axis in range(len(dims))]
    entries = entries.at[tuple(place)].set(least)
    longest = dims.index(max(dims))
    place[longest] = (place[longest] + 1) % dims[longest]
    return entries.at[tuple(place)].set(largest)


def level_of(stream_key, shape, shards, least, largest):
    def one(dim, parts):
        heights = jax.random.uniform(jax.random.fold_in(jax.random.fold_in(stream_key, 6), dim), (parts,), jnp.float32, least / len(shards), largest / len(shards))
        return jnp.repeat(jnp.exp(heights), shape[dim] // parts).reshape((-1,) + (1,) * (len(shape) - dim - 1))

    gain = one(*shards[0])
    for cut in shards[1:]:
        gain = gain * one(*cut)
    return gain


def gaussian(stream_key, shape, scale, bound, pieces=(), kind=jnp.bfloat16):
    loudness = level_of(stream_key, shape, pieces, -0.22, 0.18) if pieces else 1.0
    values = jax.random.normal(stream_key, shape, jnp.float32) * scale * loudness
    return jnp.minimum(jnp.maximum(values, -bound), bound).astype(kind)


def setup_inputs(seed: int = 0, part: int = 0) -> dict:
    arg_keys = jax.random.split(jax.random.key(seed), 8)
    part_keys = jax.random.split(jax.random.fold_in(arg_keys[7], part), 8)
    tokens = gaussian(part_keys[0], (LAT_CELLS, LON_CELLS, D), 1.0, 6.0, ((0, 2), (1, 8)))
    visible = place_ends((jax.random.randint(part_keys[1], (LAT_CELLS, LON_CELLS), 0, 4) < 1).astype(jnp.int32), jax.random.fold_in(part_keys[1], 1), 0, 1)
    mask_token = gaussian(arg_keys[2], (D,), 1.0, 4.0)
    norm_gain_table = jnp.clip(1.0 + 0.15 * jax.random.normal(arg_keys[3], (LAYERS, D), jnp.float32), 0.25, 1.75)
    query_key_value_weight = gaussian(arg_keys[4], (LAYERS, D, 3 * D), D ** -0.5, 0.3125)
    output_weight = gaussian(arg_keys[5], (LAYERS, D, D), D ** -0.5, 0.3125)
    cotangent = gaussian(part_keys[6], (LAT_CELLS, LON_CELLS, D), 1.0, 6.0, ((0, 2), (1, 8)), jnp.float32)
    return {"tokens": tokens, "visible": visible, "mask_token": mask_token, "norm_gain_table": norm_gain_table, "query_key_value_weight": query_key_value_weight, "output_weight": output_weight, "cotangent": cotangent}


def rounded_down(value_in):
    lowered = lax.optimization_barrier(value_in.astype(jnp.bfloat16)).astype(jnp.float32)
    return value_in + lax.stop_gradient(lowered - value_in)

def normed(values_in, gain_row):
    mean_value = lax.optimization_barrier(jnp.mean(values_in, axis=-1, keepdims=True))
    centred = values_in - mean_value
    spread = lax.optimization_barrier(jnp.mean(centred * centred, axis=-1, keepdims=True))
    return centred * lax.rsqrt(spread + 1e-05) * gain_row

def attend_whole(query, keyval, dilation):
    row_count, col_count, model = query.shape
    head_size = model // HEADS
    padded = jnp.pad(keyval, ((dilation, dilation), (0, 0), (0, 0)))
    shaped_query = query.reshape(row_count, col_count, HEADS, head_size)
    weights = []
    values = []
    for lat_step in (-1, 0, 1):
        row_start = dilation + lat_step * dilation
        key_band = padded[row_start:row_start + row_count]
        lat_line = jnp.arange(row_count) + lat_step * dilation
        inside = jnp.where((lat_line >= 0) & (lat_line < row_count), 1.0, 0.0).astype(jnp.float32)[:, None, None]
        for lon_step in (-1, 0, 1):
            key_cols = jnp.roll(key_band, -lon_step * dilation, axis=1)
            key_part = key_cols[..., :model].reshape(row_count, col_count, HEADS, head_size)
            score = lax.optimization_barrier(jnp.sum(shaped_query * key_part, axis=-1)) * head_size ** (-0.5)
            weights.append(jnp.exp(score) * inside)
            values.append(key_cols[..., model:].reshape(row_count, col_count, HEADS, head_size))
    weight_sum = sum(weights)
    result = jnp.zeros_like(shaped_query)
    for weight_one, value_one in zip(weights, values):
        result = result + (weight_one / weight_sum)[..., None] * value_one
    return result.reshape(row_count, col_count, model)

def layer_number(layer_in, gain_row, weight_qkv, weight_out, dilation):
    model = layer_in.shape[2]
    normal_part = rounded_down(normed(layer_in, gain_row))
    query_key_value_stacked = rounded_down(jnp.dot(normal_part, weight_qkv, precision=lax.Precision.HIGHEST))
    attend_checked = jax.checkpoint(attend_whole, static_argnums=(2,))
    mixed = rounded_down(attend_checked(query_key_value_stacked[..., :model], query_key_value_stacked[..., model:], dilation))
    return layer_in + jnp.dot(mixed, weight_out, precision=lax.Precision.HIGHEST)

def reference(tokens, visible, mask_token, norm_gain_table, query_key_value_weight, output_weight, cotangent):
    token_full = tokens.astype(jnp.float32)
    shown = visible[..., None] == 1

    def forward(token_in, gain_stacked, query_key_value_stacked, output_stacked):
        starting_tokens = jnp.where(shown, token_in, mask_token.astype(jnp.float32)[None, None, :])
        between_tokens = rounded_down(layer_number(starting_tokens, gain_stacked[0], query_key_value_stacked[0], output_stacked[0], DILATION_STEP))
        return layer_number(between_tokens, gain_stacked[1], query_key_value_stacked[1], output_stacked[1], 1)
    final, pullback = jax.vjp(forward, token_full, norm_gain_table, query_key_value_weight.astype(jnp.float32), output_weight.astype(jnp.float32))
    grad_tok, grad_gain, grad_qkv, grad_out = pullback(cotangent)
    factor = (tokens.shape[0] * tokens.shape[1]) ** (-0.5)
    return (grad_tok, grad_qkv * factor, grad_out * factor, grad_gain * factor)
```

```python
import jax
import jax.numpy as jnp
from jax import lax
from jax.experimental import pallas as pl
from jax.experimental.pallas import tpu as pltpu
from jax.sharding import PartitionSpec as P

HEADS = 6
EPS = 1e-05
F32 = jnp.float32
BF16 = jnp.bfloat16
VMEM_BYTES = 56 * 1024 * 1024
HALO = 128
COLS_AT = 32
RIGHT_AT = 72
HALO_COLS = 80


def nn(a, b):
    return lax.dot_general(a, b, (((1,), (0,)), ((), ())), preferred_element_type=F32)


def nt(a, b):
    return lax.dot_general(a, b, (((1,), (1,)), ((), ())), preferred_element_type=F32)


def tn(a, b):
    return lax.dot_general(a, b, (((0,), (0,)), ((), ())), preferred_element_type=F32)


def iota(shape, dim):
    return lax.broadcasted_iota(jnp.int32, shape, dim)


def one_hot(condition):
    return jnp.where(condition, 1.0, 0.0).astype(BF16)


def permuted(value, axis, target):
    count = lax.axis_size(axis)
    return lax.ppermute(value, axis, [(i, target(i) % count) for i in range(count)])


def lat_swap(value):
    return permuted(value, "lat", lambda i: i ^ 1)


def lon_swap(value):
    return permuted(value, "lon", lambda i: i ^ 1)


def lon_forward(value):
    return permuted(value, "lon", lambda i: i + 2 if i % 2 == 0 else i - 2)


def lon_backward(value):
    return permuted(value, "lon", lambda i: i - 2 if i % 2 == 0 else i + 2)


def from_left(value):
    return permuted(value, "lon", lambda i: i + 1)


def from_right(value):
    return permuted(value, "lon", lambda i: i - 1)


def around(pack):
    left, right = from_left(pack), from_right(pack)
    return [lat_swap(pack), left, right, lat_swap(left), lat_swap(right)]


def norm_parts(x):
    mean = jnp.mean(x, axis=-1, keepdims=True)
    centred = x - mean
    spread = jnp.mean(centred * centred, axis=-1, keepdims=True)
    rstd = lax.rsqrt(spread + EPS)
    return centred * rstd, rstd


def norm_back(x, gain, grad_normal):
    xhat, rstd = norm_parts(x)
    g = grad_normal * gain
    return rstd * (
        g - jnp.mean(g, axis=-1, keepdims=True) - xhat * jnp.mean(g * xhat, axis=-1, keepdims=True)
    )


def visible_columns(visible):
    side = visible.shape[1]
    eye = jnp.where(iota((side, side), 0) == iota((side, side), 1), 1.0, 0.0)
    return nt(eye, visible.astype(F32))


def start_kernel(tok_ref, vis_ref, mask_ref, gain_ref, start_ref, normal_ref):
    rows, cols, width = tok_ref.shape
    shown = visible_columns(vis_ref[...])
    mask_row = mask_ref[...].astype(F32)
    gain = gain_ref[...]
    for r in range(rows):
        x = jnp.where(shown[:, r : r + 1] > 0.5, tok_ref[r].astype(F32), mask_row)
        start_ref[r] = x.astype(BF16)
        xhat, _ = norm_parts(x)
        normal_ref[r] = (xhat * gain).astype(BF16)


def first_kernel(
    lat_ref, n0, n1, n2, n3, n4, n5, start_ref, wt_ref, wo_ref, gain_ref,
    q_ref, kv_ref, p_ref, mixed_ref, h_ref, normal_ref, pack_ref,
    w_s, pack_s,
):
    width, tile = q_ref.shape
    head = width // HEADS
    blocks = (n0, n1, n2, n3, n4, n5)
    q_ref[...] = nt(wt_ref[0:width], n0[...]).astype(BF16)
    for b, ref in enumerate(blocks):
        kv_ref[b] = nt(wt_ref[width : 3 * width], ref[...]).astype(BF16)
    for h in range(HEADS):
        lo, hi = h * head, (h + 1) * head
        q = q_ref[lo:hi, :].astype(F32) * (head**-0.5)
        total = jnp.zeros((1, tile), F32)
        out = jnp.zeros((head, tile), F32)
        for b in range(len(blocks)):
            k = kv_ref[b, lo:hi, :].astype(F32)
            w = jnp.exp(jnp.sum(q * k, axis=0, keepdims=True))
            w_s[b, h : h + 1, :] = w
            total = total + w
            out = out + w * kv_ref[b, width + lo : width + hi, :].astype(F32)
        inverse = 1.0 / total
        for b in range(len(blocks)):
            p_ref[b, h : h + 1, :] = w_s[b, h : h + 1, :] * inverse
        mixed_ref[lo:hi, :] = (out * inverse).astype(BF16)
    h1 = start_ref[...].astype(F32) + tn(mixed_ref[...], wo_ref[...])
    h1 = h1.astype(BF16)
    h_ref[...] = h1
    xhat, _ = norm_parts(h1.astype(F32))
    normal = (xhat * gain_ref[...]).astype(BF16)
    normal_ref[...] = normal
    step = pl.program_id(0)
    brow = jnp.where(lat_ref[0] == 0, 31, 0)
    slot = iota((HALO, tile), 0)
    token = step * tile + iota((HALO, tile), 1)
    r, c = token // 32, token % 32
    pick = one_hot(
        ((slot < 32) & (r == brow) & (c == slot))
        | ((slot >= 32) & (slot < 64) & (c == 0) & (r == slot - 32))
        | ((slot >= 64) & (slot < 96) & (c == 31) & (r == slot - 64))
    )

    @pl.when(step == 0)
    def _():
        pack_s[...] = jnp.zeros_like(pack_s)

    pack_s[...] += nn(pick, normal)

    @pl.when(step == pl.num_programs(0) - 1)
    def _():
        pack_ref[...] = pack_s[...].astype(BF16)


def second_kernel(
    lat_ref, n_ref, pv, pl_, pr, pdl, pdr, w_ref, wo_ref, cot_ref,
    dn_ref, back_ref, dw_ref, dwo_ref,
    q_s, k_s, v_s, kc_s, vc_s, dq_s, dk_s, dv_s, dkc_s, dvc_s, do_s, mixed_s, halo_s, mask_s,
):
    points, width = n_ref.shape
    head = width // HEADS
    lat = lat_ref[0]
    upper = lat == 0
    a, b = iota((HALO, HALO), 0), iota((HALO, HALO), 1)
    corner = jnp.where(upper, 33, 0)
    halo = nn(one_hot((a < 32) & (a == b)), pv[...])
    halo += nn(one_hot((b >= 64) & (b < 96) & (a == COLS_AT + 1 + b - 64)), pl_[...])
    halo += nn(one_hot((b >= 32) & (b < 64) & (a == RIGHT_AT + 1 + b - 32)), pr[...])
    halo += nn(one_hot((b == 31) & (a == COLS_AT + corner)), pdl[...])
    halo += nn(one_hot((b == 0) & (a == RIGHT_AT + corner)), pdr[...])
    halo = halo.astype(BF16)
    halo_s[...] = halo

    normal = n_ref[...]
    scale = head**-0.5
    q_s[...] = (nn(normal, w_ref[:, 0:width]).astype(BF16).astype(F32) * scale).astype(BF16)
    k_s[32 : 32 + points, :] = nn(normal, w_ref[:, width : 2 * width]).astype(BF16)
    v_s[32 : 32 + points, :] = nn(normal, w_ref[:, 2 * width : 3 * width]).astype(BF16)
    kh = nn(halo, w_ref[:, width : 2 * width]).astype(BF16)
    vh = nn(halo, w_ref[:, 2 * width : 3 * width]).astype(BF16)
    for at in (0, 32 + points):
        k_s[at : at + 32, :] = kh[0:32]
        v_s[at : at + 32, :] = vh[0:32]
    kc_s[...] = kh[COLS_AT : COLS_AT + HALO_COLS]
    vc_s[...] = vh[COLS_AT : COLS_AT + HALO_COLS]
    dk_s[...] = jnp.zeros_like(dk_s)
    dv_s[...] = jnp.zeros_like(dv_s)
    dkc_s[...] = jnp.zeros_like(dkc_s)
    dvc_s[...] = jnp.zeros_like(dvc_s)
    cot = cot_ref[...].astype(BF16)
    do_s[...] = nt(cot, wo_ref[...]).astype(BF16)

    key, query = iota((192, 256), 0), iota((192, 256), 1) % 128
    drow = key // 32 - 1 - query // 32
    dcol = key % 32 - query % 32
    mask_s[...] = jnp.where((jnp.abs(drow) <= 1) & (jnp.abs(dcol) <= 1), 1.0, 0.0)

    tiles = points // 128

    def tile_step(t, carry):
        base = pl.multiple_of(t * 128, 128)
        key = iota((192, 256), 0)
        first = jnp.where(upper & (t == 0), 32, 0)
        last = jnp.where(jnp.logical_not(upper) & (t == tiles - 1), 160, 192)
        mask1 = (mask_s[...] > 0.5) & (key >= first) & (key < last)
        e, query = iota((HALO_COLS, 256), 0), iota((HALO_COLS, 256), 1) % 128
        is_right = e >= 40
        ext = jnp.where(is_right, e - 40, e)
        near = jnp.abs(ext - 1 - (4 * t + query // 32)) <= 1
        side = query % 32 == jnp.where(is_right, 31, 0)
        real = (ext < 34) & (ext != jnp.where(upper, 0, 33))
        mask2 = near & side & real
        lane = iota((128, 128), 1)
        even = lane < 64
        for pair in range(HEADS // 2):
            lanes = slice(pair * 128, pair * 128 + 128)
            win = pl.ds(base, 192)
            here = pl.ds(base, 128)
            q = q_s[here, lanes]
            do = do_s[here, lanes]
            zero = jnp.zeros_like(q)
            qm = jnp.concatenate([jnp.where(even, q, zero), jnp.where(even, zero, q)], 0)
            dom = jnp.concatenate([jnp.where(even, do, zero), jnp.where(even, zero, do)], 0)
            k1, v1 = k_s[win, lanes], v_s[win, lanes]
            k2, v2 = kc_s[:, lanes], vc_s[:, lanes]
            w1 = jnp.where(mask1, jnp.exp(nt(k1, qm)), 0.0)
            w2 = jnp.where(mask2, jnp.exp(nt(k2, qm)), 0.0)
            total = jnp.sum(w1, axis=0, keepdims=True) + jnp.sum(w2, axis=0, keepdims=True)
            inverse = 1.0 / total
            p1, p2 = w1 * inverse, w2 * inverse
            dp1, dp2 = nt(v1, dom), nt(v2, dom)
            delta = jnp.sum(p1 * dp1, axis=0, keepdims=True) + jnp.sum(
                p2 * dp2, axis=0, keepdims=True
            )
            ds1, ds2 = (p1 * (dp1 - delta)).astype(BF16), (p2 * (dp2 - delta)).astype(BF16)
            p1, p2 = p1.astype(BF16), p2.astype(BF16)
            out = tn(p1, v1) + tn(p2, v2)
            mixed_s[here, lanes] = jnp.where(even, out[0:128], out[128:256]).astype(BF16)
            dq = (tn(ds1, k1) + tn(ds2, k2)) * scale
            dq_s[here, lanes] = jnp.where(even, dq[0:128], dq[128:256]).astype(BF16)
            dk_s[win, lanes] += nn(ds1, qm)
            dv_s[win, lanes] += nn(p1, dom)
            dkc_s[:, lanes] += nn(ds2, qm)
            dvc_s[:, lanes] += nn(p2, dom)
        return carry

    lax.fori_loop(0, tiles, tile_step, 0)

    dwo_ref[...] = tn(mixed_s[...], cot).astype(BF16)
    row_at = pl.multiple_of(jnp.where(upper, 32 + points, 0), 32)
    pad = jnp.zeros((HALO - COLS_AT - HALO_COLS, width), F32)
    dkh = jnp.concatenate([dk_s[pl.ds(row_at, 32), :], dkc_s[...], pad], 0).astype(BF16)
    dvh = jnp.concatenate([dv_s[pl.ds(row_at, 32), :], dvc_s[...], pad], 0).astype(BF16)
    dq = dq_s[...]
    dk = dk_s[32 : 32 + points, :].astype(BF16)
    dv = dv_s[32 : 32 + points, :].astype(BF16)
    halo = halo_s[...]
    wq, wk, wv = (w_ref[:, i * width : (i + 1) * width] for i in range(3))
    dn_ref[...] = nt(dq, wq) + nt(dk, wk) + nt(dv, wv)
    back_ref[...] = (nt(dkh, wk) + nt(dvh, wv)).astype(BF16)
    dw_ref[:, 0:width] = tn(normal, dq).astype(BF16)
    dw_ref[:, width : 2 * width] = (tn(normal, dk) + tn(halo, dkh)).astype(BF16)
    dw_ref[:, 2 * width : 3 * width] = (tn(normal, dv) + tn(halo, dvh)).astype(BF16)


def third_kernel(
    lat_ref, n0, n1, n2, n3, n4, n5, q_ref, kv_ref, p_ref, mixed_ref, h_ref, dn1_ref, cot_ref,
    packs_ref, wt_ref, wo_ref, gain_ref,
    dh_ref, d0, d1, d2, d3, d4, d5, dw_ref, dwo_ref,
    dw_s, dwo_s, dmix_s, dkv_s, dq_s, dp_s,
):
    width, tile = q_ref.shape
    head = width // HEADS
    scale = head**-0.5
    blocks = (n0, n1, n2, n3, n4, n5)
    outs = (d0, d1, d2, d3, d4, d5)
    step = pl.program_id(0)

    @pl.when(step == 0)
    def _():
        dw_s[...] = jnp.zeros_like(dw_s)
        dwo_s[...] = jnp.zeros_like(dwo_s)

    upper = lat_ref[0] == 0
    brow = jnp.where(upper, 31, 0)
    corner = jnp.where(upper, 0, 33)
    shape = (tile, 5 * HALO)
    token = step * tile + iota(shape, 0)
    r, c = token // 32, token % 32
    which, slot = iota(shape, 1) // HALO, iota(shape, 1) % HALO
    border = r == brow
    place = one_hot(
        ((which == 0) & border & (slot < 32) & (slot == c))
        | ((which == 1) & (c == 0) & (slot == RIGHT_AT + 1 + r))
        | ((which == 2) & (c == 31) & (slot == COLS_AT + 1 + r))
        | ((which == 3) & border & (c == 0) & (slot == RIGHT_AT + corner))
        | ((which == 4) & border & (c == 31) & (slot == COLS_AT + corner))
    )
    dn = dn1_ref[...] + nn(place, packs_ref[...])
    dh = cot_ref[...] + norm_back(h_ref[...].astype(F32), gain_ref[...], dn)
    dh_ref[...] = dh
    dhb = dh.astype(BF16)
    dmix_s[...] = nt(wo_ref[...], dhb)
    dwo_s[...] += nn(mixed_ref[...], dhb)
    for h in range(HEADS):
        lo, hi = h * head, (h + 1) * head
        dmix = dmix_s[lo:hi, :]
        delta = jnp.zeros((1, tile), F32)
        for b in range(len(blocks)):
            dp = jnp.sum(
                dmix * kv_ref[b, width + lo : width + hi, :].astype(F32), axis=0, keepdims=True
            )
            dp_s[b : b + 1, :] = dp
            delta = delta + p_ref[b, h : h + 1, :] * dp
        q = q_ref[lo:hi, :].astype(F32)
        dq = jnp.zeros((head, tile), F32)
        for b in range(len(blocks)):
            p = p_ref[b, h : h + 1, :]
            ds = p * (dp_s[b : b + 1, :] - delta) * scale
            dq = dq + ds * kv_ref[b, lo:hi, :].astype(F32)
            dkv_s[b, lo:hi, :] = (ds * q).astype(BF16)
            dkv_s[b, width + lo : width + hi, :] = (p * dmix).astype(BF16)
        dq_s[lo:hi, :] = dq.astype(BF16)
    dq = dq_s[...]
    dw_s[0:width, :] += nn(dq, n0[...])
    for b, (ref, out) in enumerate(zip(blocks, outs)):
        dkv = dkv_s[b]
        grad = tn(dkv, wt_ref[width : 3 * width])
        if b == 0:
            grad = grad + tn(dq, wt_ref[0:width])
        out[...] = grad.astype(out.dtype)
        dw_s[width : 3 * width, :] += nn(dkv, ref[...])

    @pl.when(step == pl.num_programs(0) - 1)
    def _():
        dw_ref[...] = dw_s[...].astype(BF16)
        dwo_ref[...] = dwo_s[...].astype(BF16)


def last_kernel(start_ref, vis_ref, gain_ref, dh_ref, own_ref, far_ref, out_ref):
    rows, cols, width = start_ref.shape
    shown = visible_columns(vis_ref[...])
    gain = gain_ref[...]
    for r in range(rows):
        dn = own_ref[r] + far_ref[r].astype(F32)
        grad = dh_ref[r] + norm_back(start_ref[r].astype(F32), gain, dn)
        out_ref[r] = jnp.where(shown[:, r : r + 1] > 0.5, grad, 0.0)


def call(kernel, out_shape, scratch=(), grid=None, in_specs=None, out_specs=None):
    return pl.pallas_call(
        kernel,
        out_shape=out_shape,
        grid_spec=pltpu.PrefetchScalarGridSpec(
            num_scalar_prefetch=0,
            grid=grid or (),
            in_specs=in_specs,
            out_specs=out_specs,
            scratch_shapes=list(scratch),
        ),
        compiler_params=pltpu.CompilerParams(vmem_limit_bytes=VMEM_BYTES),
    )


def whole():
    return pl.BlockSpec(memory_space=pltpu.VMEM)


def scalar():
    return pl.BlockSpec(memory_space=pltpu.SMEM)


def fixed(shape):
    return pl.BlockSpec(shape, lambda i: (0,) * len(shape))


def local(
    tokens, visible, mask_token, norm_gain_table, query_key_value_weight, output_weight, cotangent
):
    rows, cols, width = tokens.shape
    points = rows * cols
    lat_count, lon_count = lax.axis_size("lat"), lax.axis_size("lon")
    lat = lax.axis_index("lat").astype(jnp.int32).reshape(1)
    gain0, gain1 = norm_gain_table[0:1], norm_gain_table[1:2]
    w0, w1 = query_key_value_weight[0], query_key_value_weight[1]
    wo0, wo1 = output_weight[0], output_weight[1]
    wt0 = w0.T
    struct = jax.ShapeDtypeStruct

    start, normal0 = call(
        start_kernel,
        (struct((rows, cols, width), BF16), struct((rows, cols, width), BF16)),
        in_specs=[whole()] * 4,
        out_specs=(whole(), whole()),
    )(tokens, visible, mask_token.reshape(1, width), gain0)
    flat = lambda x: x.reshape(points, width)

    own = flat(normal0)
    swapped = lon_swap(own)
    beyond = lon_forward(swapped)
    blocks = [own, lat_swap(own), swapped, beyond, lat_swap(swapped), lat_swap(beyond)]

    tile = 256
    steps = points // tile
    tok_spec = pl.BlockSpec((tile, width), lambda i: (i, 0))
    feat_spec = pl.BlockSpec((width, tile), lambda i: (0, i))
    kv_spec = pl.BlockSpec((6, 2 * width, tile), lambda i: (0, 0, i))
    p_spec = pl.BlockSpec((6, 8, tile), lambda i: (0, 0, i))
    q0, kv0, p0, mixed0, h1, normal1, pack = call(
        first_kernel,
        (
            struct((width, points), BF16),
            struct((6, 2 * width, points), BF16),
            struct((6, 8, points), F32),
            struct((width, points), BF16),
            struct((points, width), BF16),
            struct((points, width), BF16),
            struct((HALO, width), BF16),
        ),
        grid=(steps,),
        in_specs=[scalar()]
        + [tok_spec] * 7
        + [fixed((3 * width, width)), fixed((width, width)), fixed((1, width))],
        out_specs=(
            feat_spec, kv_spec, p_spec, feat_spec, tok_spec, tok_spec, fixed((HALO, width)),
        ),
        scratch=[pltpu.VMEM((6, 8, tile), F32), pltpu.VMEM((HALO, width), F32)],
    )(lat, *blocks, flat(start), wt0, wo0, gain1)

    halos = around(pack)
    cot = flat(cotangent)
    ext = points + 64
    dn1, back, dw1, dwo1 = call(
        second_kernel,
        (
            struct((points, width), F32),
            struct((HALO, width), BF16),
            struct((width, 3 * width), BF16),
            struct((width, width), BF16),
        ),
        in_specs=[scalar()] + [whole()] * 9,
        out_specs=(whole(),) * 4,
        scratch=[
            pltpu.VMEM((points, width), BF16),
            pltpu.VMEM((ext, width), BF16),
            pltpu.VMEM((ext, width), BF16),
            pltpu.VMEM((HALO_COLS, width), BF16),
            pltpu.VMEM((HALO_COLS, width), BF16),
            pltpu.VMEM((points, width), BF16),
            pltpu.VMEM((ext, width), F32),
            pltpu.VMEM((ext, width), F32),
            pltpu.VMEM((HALO_COLS, width), F32),
            pltpu.VMEM((HALO_COLS, width), F32),
            pltpu.VMEM((points, width), BF16),
            pltpu.VMEM((points, width), BF16),
            pltpu.VMEM((HALO, width), BF16),
            pltpu.VMEM((192, 256), F32),
        ],
    )(lat, normal1, *halos, w1, wo1, cot)

    packs = jnp.concatenate(around(back), 0)
    dh1, d0, d1, d2, d3, d4, d5, dw0t, dwo0 = call(
        third_kernel,
        (
            struct((points, width), F32),
            struct((points, width), F32),
            *[struct((points, width), BF16)] * 5,
            struct((3 * width, width), BF16),
            struct((width, width), BF16),
        ),
        grid=(steps,),
        in_specs=[scalar()]
        + [tok_spec] * 6
        + [feat_spec, kv_spec, p_spec, feat_spec, tok_spec, tok_spec, tok_spec]
        + [
            fixed((5 * HALO, width)),
            fixed((3 * width, width)),
            fixed((width, width)),
            fixed((1, width)),
        ],
        out_specs=(
            *[tok_spec] * 7, fixed((3 * width, width)), fixed((width, width)),
        ),
        scratch=[
            pltpu.VMEM((3 * width, width), F32),
            pltpu.VMEM((width, width), F32),
            pltpu.VMEM((width, tile), F32),
            pltpu.VMEM((6, 2 * width, tile), BF16),
            pltpu.VMEM((width, tile), BF16),
            pltpu.VMEM((8, tile), F32),
        ],
    )(lat, *blocks, q0, kv0, p0, mixed0, h1, dn1, cot, packs, wt0, wo0, gain1)

    def plus(a, b):
        return (a.astype(F32) + b.astype(F32)).astype(BF16)

    d3 = plus(d3, lat_swap(d5))
    d2 = plus(d2, lat_swap(d4))
    d2 = plus(d2, lon_backward(d3))
    far = plus(lon_swap(d2), lat_swap(d1))

    cube = lambda x: x.reshape(rows, cols, width)
    grad_tokens = call(
        last_kernel,
        struct((rows, cols, width), F32),
        in_specs=[whole()] * 6,
        out_specs=whole(),
    )(start, visible, gain0, cube(dh1), cube(d0), cube(far))

    factor = (points * lat_count * lon_count) ** (-0.5)
    s1, so1 = lax.psum((dw1.astype(F32), dwo1.astype(F32)), ("lon", "lat"))
    s0, so0 = lax.psum((dw0t.astype(F32), dwo0.astype(F32)), ("lon", "lat"))
    g_qkv = jnp.stack([s0.T, s1]) * factor
    g_out = jnp.stack([so0, so1]) * factor
    g_gain = (
        jnp.sum(query_key_value_weight.astype(F32) * g_qkv, axis=-1) / norm_gain_table
    )
    return grad_tokens, g_qkv, g_out, g_gain


def solution(mesh):
    return jax.shard_map(
        local,
        mesh=mesh,
        in_specs=(
            P(("group", "lat"), "lon", None),
            P(("group", "lat"), "lon"),
            P(),
            P(),
            P(),
            P(),
            P(("group", "lat"), "lon", None),
        ),
        out_specs=(
            P(("group", "lat"), "lon", None),
            P("group", None, None),
            P("group", None, None),
            P("group", None),
        ),
        check_vma=False,
    )
```

```python
import functools

import jax
import jax.numpy as jnp
from jax import lax
from jax.experimental import pallas as pl
from jax.experimental.pallas import tpu as pltpu
from jax.sharding import PartitionSpec as P

HEADS = 6
EPS = 1e-05
F32 = jnp.float32
BF16 = jnp.bfloat16
VMEM_BYTES = 56 * 1024 * 1024
HALO = 112
CORNER = 96
RETURNED = 224


def nn(a, b):
    return lax.dot_general(a, b, (((1,), (0,)), ((), ())), preferred_element_type=F32)


def nt(a, b):
    return lax.dot_general(a, b, (((1,), (1,)), ((), ())), preferred_element_type=F32)


def tn(a, b):
    return lax.dot_general(a, b, (((0,), (0,)), ((), ())), preferred_element_type=F32)


def iota(shape, dim):
    return lax.broadcasted_iota(jnp.int32, shape, dim)


def one_hot(condition):
    return jnp.where(condition, 1.0, 0.0).astype(BF16)


def permuted(value, axis, target):
    count = lax.axis_size(axis)
    return lax.ppermute(value, axis, [(i, target(i) % count) for i in range(count)])


def lat_swap(value):
    return permuted(value, "lat", lambda i: i ^ 1)


def lon_swap(value):
    return permuted(value, "lon", lambda i: i ^ 1)


def lon_forward(value):
    return permuted(value, "lon", lambda i: i + 2 if i % 2 == 0 else i - 2)


def lon_backward(value):
    return permuted(value, "lon", lambda i: i - 2 if i % 2 == 0 else i + 2)


def from_left(value):
    return permuted(value, "lon", lambda i: i + 1)


def from_right(value):
    return permuted(value, "lon", lambda i: i - 1)


def chained(value, after):
    return lax.optimization_barrier((value, after))


def exchanged(parts, axis_stride, factor):
    count = lax.axis_size("lon")
    digit = (lax.axis_index("lon") // axis_stride) % factor
    moved = []
    for d in range(1, factor):
        pairs = [(i, shifted(i, axis_stride, factor, d)) for i in range(count)]
        moved.append(lax.ppermute(parts(lax.rem(digit + d, factor)), "lon", pairs))
    total = parts(digit).astype(F32)
    for piece in moved:
        total = total + piece.astype(F32)
    return total.astype(BF16)


def shifted(i, stride, factor, d):
    digit = (i // stride) % factor
    return i + ((digit + d) % factor - digit) * stride


def spread(value, axis_stride, factor):
    count = lax.axis_size("lon")
    digit = (lax.axis_index("lon") // axis_stride) % factor
    rows = value.shape[0]
    full = jnp.zeros((factor * rows,) + value.shape[1:], value.dtype)
    full = lax.dynamic_update_slice(full, value, (digit * rows, 0))
    for d in range(1, factor):
        pairs = [(i, shifted(i, axis_stride, factor, d)) for i in range(count)]
        got = lax.ppermute(value, "lon", pairs)
        at = lax.rem(digit - d + factor, factor) * rows
        full = lax.dynamic_update_slice(full, got, (at, 0))
    return full


def lon_factors():
    left = lax.axis_size("lon")
    stride, out = 1, []
    for factor in [2] + [4] * 10:
        if left == 1:
            break
        factor = min(factor, left)
        out.append((stride, factor))
        stride, left = stride * factor, left // factor
    return out


def summed(value):
    lat = lax.axis_index("lat")
    half = value.shape[0] // 2
    mine = lax.dynamic_slice_in_dim(value, lat * half, half, 0)
    other = lat_swap(lax.dynamic_slice_in_dim(value, (1 - lat) * half, half, 0))
    value = (mine.astype(F32) + other.astype(F32)).astype(BF16)
    factors = lon_factors()
    for stride, factor in factors:
        size = value.shape[0] // factor
        take = lambda k, v=value, n=size: lax.dynamic_slice_in_dim(v, k * n, n, 0)
        value = exchanged(take, stride, factor)
    for stride, factor in factors[::-1]:
        value = spread(value, stride, factor)
    other = lat_swap(value)
    return jnp.where(
        lat == 0, jnp.concatenate([value, other], 0), jnp.concatenate([other, value], 0)
    )


def norm_parts(x):
    mean = jnp.mean(x, axis=-1, keepdims=True)
    centred = x - mean
    spread = jnp.mean(centred * centred, axis=-1, keepdims=True)
    rstd = lax.rsqrt(spread + EPS)
    return centred * rstd, rstd


def norm_back(x, gain, grad_normal):
    xhat, rstd = norm_parts(x)
    g = grad_normal * gain
    return rstd * (
        g - jnp.mean(g, axis=-1, keepdims=True) - xhat * jnp.mean(g * xhat, axis=-1, keepdims=True)
    )


def shown_column(visible, base, tile):
    rows, cols = visible.shape
    token = base + iota((tile, rows), 0)
    of_row = nn(one_hot(token // cols == iota((tile, rows), 1)), visible.astype(F32).astype(BF16))
    token = base + iota((tile, cols), 0)
    mine = token % cols == iota((tile, cols), 1)
    return jnp.sum(jnp.where(mine, of_row, 0.0), axis=1, keepdims=True)


def start_kernel(first, tok_ref, vis_ref, mask_ref, gain_ref, start_ref, normal_ref):
    tile, width = tok_ref.shape
    base = first + pl.program_id(0) * tile
    shown = shown_column(vis_ref[...], base, tile)
    x = jnp.where(shown > 0.5, tok_ref[...].astype(F32), mask_ref[...].astype(F32))
    start_ref[...] = x.astype(BF16)
    xhat, _ = norm_parts(x)
    normal_ref[...] = (xhat * gain_ref[...]).astype(BF16)


def first_kernel(
    first, lat_ref, n0, n1, n2, n3, n4, n5, start_ref, row_in, left_in, right_in,
    wt_ref, wo_ref, gain_ref,
    q_ref, kv_ref, p_ref, mixed_ref, h_ref, normal_ref, row_ref, left_ref, right_ref,
    w_s, pack_s,
):
    width, tile = q_ref.shape
    head = width // HEADS
    blocks = (n0, n1, n2, n3, n4, n5)
    q_ref[...] = nt(wt_ref[0:width], n0[...]).astype(BF16)
    for b, ref in enumerate(blocks):
        kv_ref[b] = nt(wt_ref[width : 3 * width], ref[...]).astype(BF16)
    for h in range(HEADS):
        lo, hi = h * head, (h + 1) * head
        q = q_ref[lo:hi, :].astype(F32) * (head**-0.5)
        total = jnp.zeros((1, tile), F32)
        out = jnp.zeros((head, tile), F32)
        for b in range(len(blocks)):
            k = kv_ref[b, lo:hi, :].astype(F32)
            w = jnp.exp(jnp.sum(q * k, axis=0, keepdims=True))
            w_s[b, h : h + 1, :] = w
            total = total + w
            out = out + w * kv_ref[b, width + lo : width + hi, :].astype(F32)
        inverse = 1.0 / total
        for b in range(len(blocks)):
            p_ref[b, h : h + 1, :] = w_s[b, h : h + 1, :] * inverse
        mixed_ref[lo:hi, :] = (out * inverse).astype(BF16)
    h1 = start_ref[...].astype(F32) + tn(mixed_ref[...], wo_ref[...])
    h1 = h1.astype(BF16)
    h_ref[...] = h1
    xhat, _ = norm_parts(h1.astype(F32))
    normal = (xhat * gain_ref[...]).astype(BF16)
    normal_ref[...] = normal
    step = pl.program_id(0)
    brow = jnp.where(lat_ref[0] == 0, 31, 0)
    slot = iota((96, tile), 0)
    token = first + step * tile + iota((96, tile), 1)
    r, c = token // 32, token % 32
    pick = one_hot(
        ((slot < 32) & (r == brow) & (c == slot))
        | ((slot >= 32) & (slot < 64) & (c == 0) & (r == slot - 32))
        | ((slot >= 64) & (c == 31) & (r == slot - 64))
    )

    @pl.when(step == 0)
    def _():
        for i, ref in enumerate((row_in, left_in, right_in)):
            pack_s[i * 32 : i * 32 + 32, :] = ref[...].astype(F32)

    pack_s[...] += nn(pick, normal)

    @pl.when(step == pl.num_programs(0) - 1)
    def _():
        for i, ref in enumerate((row_ref, left_ref, right_ref)):
            ref[...] = pack_s[i * 32 : i * 32 + 32, :].astype(BF16)


def second_kernel(
    lat_ref, na_ref, nb_ref, row_ref, left_ref, right_ref, dleft_ref, dright_ref,
    w_ref, wo_ref, cot_ref,
    dn_ref, brow_ref, bleft_ref, bright_ref, dw_ref,
    q_s, k_s, v_s, kc_s, vc_s, dq_s, dk_s, dv_s, dkc_s, dvc_s, do_s, mixed_s, halo_s, mask_s, normal_s,
):
    points, width = cot_ref.shape
    head = width // HEADS
    upper = lat_ref[0] == 0
    halo_s[0:32, :] = row_ref[...]
    halo_s[32:64, :] = left_ref[...]
    halo_s[64:96, :] = right_ref[...]
    a, b = iota((16, 32), 0), iota((16, 32), 1)
    sent = b == jnp.where(upper, 0, 31)
    corners = nn(one_hot(sent & (a == 0)), dleft_ref[...])
    corners += nn(one_hot(sent & (a == 1)), dright_ref[...])
    halo_s[CORNER:HALO, :] = corners.astype(BF16)
    halo = halo_s[...]
    normal_s[0 : points // 2, :] = na_ref[...]
    normal_s[points // 2 : points, :] = nb_ref[...]
    normal = normal_s[...]
    scale = head**-0.5
    q_s[...] = (nn(normal, w_ref[:, 0:width]).astype(BF16).astype(F32) * scale).astype(BF16)
    k_s[32 : 32 + points, :] = nn(normal, w_ref[:, width : 2 * width]).astype(BF16)
    v_s[32 : 32 + points, :] = nn(normal, w_ref[:, 2 * width : 3 * width]).astype(BF16)
    kh = nn(halo, w_ref[:, width : 2 * width]).astype(BF16)
    vh = nn(halo, w_ref[:, 2 * width : 3 * width]).astype(BF16)
    for at in (0, 32 + points):
        k_s[at : at + 32, :] = kh[0:32]
        v_s[at : at + 32, :] = vh[0:32]
    kc_s[...] = kh[32:HALO]
    vc_s[...] = vh[32:HALO]
    dk_s[...] = jnp.zeros_like(dk_s)
    dv_s[...] = jnp.zeros_like(dv_s)
    dkc_s[...] = jnp.zeros_like(dkc_s)
    dvc_s[...] = jnp.zeros_like(dvc_s)
    cot = cot_ref[...].astype(BF16)
    do_s[...] = nt(cot, wo_ref[...]).astype(BF16)

    key, query = iota((192, 256), 0), iota((192, 256), 1) % 128
    drow = key // 32 - 1 - query // 32
    dcol = key % 32 - query % 32
    mask_s[...] = jnp.where((jnp.abs(drow) <= 1) & (jnp.abs(dcol) <= 1), 1.0, 0.0)

    tiles = points // 128

    def tile_step(t, carry):
        base = pl.multiple_of(t * 128, 128)
        key = iota((192, 256), 0)
        first = jnp.where(upper & (t == 0), 32, 0)
        last = jnp.where(jnp.logical_not(upper) & (t == tiles - 1), 160, 192)
        mask1 = (mask_s[...] > 0.5) & (key >= first) & (key < last)
        e, query = iota((HALO - 32, 256), 0), iota((HALO - 32, 256), 1) % 128
        corner = e >= 64
        key_row = jnp.where(corner, jnp.where(upper, 32, -1), e % 32)
        is_left = (e < 32) | (e == 64)
        near = jnp.abs(key_row - (4 * t + query // 32)) <= 1
        side = query % 32 == jnp.where(is_left, 0, 31)
        mask2 = near & side & (e < 66)
        lane = iota((128, 128), 1)
        even = lane < 64
        for pair in range(HEADS // 2):
            lanes = slice(pair * 128, pair * 128 + 128)
            win = pl.ds(base, 192)
            here = pl.ds(base, 128)
            q = q_s[here, lanes]
            do = do_s[here, lanes]
            zero = jnp.zeros_like(q)
            qm = jnp.concatenate([jnp.where(even, q, zero), jnp.where(even, zero, q)], 0)
            dom = jnp.concatenate([jnp.where(even, do, zero), jnp.where(even, zero, do)], 0)
            k1, v1 = k_s[win, lanes], v_s[win, lanes]
            k2, v2 = kc_s[:, lanes], vc_s[:, lanes]
            w1 = jnp.where(mask1, jnp.exp(nt(k1, qm)), 0.0)
            w2 = jnp.where(mask2, jnp.exp(nt(k2, qm)), 0.0)
            total = jnp.sum(w1, axis=0, keepdims=True) + jnp.sum(w2, axis=0, keepdims=True)
            inverse = 1.0 / total
            p1, p2 = w1 * inverse, w2 * inverse
            dp1, dp2 = nt(v1, dom), nt(v2, dom)
            delta = jnp.sum(p1 * dp1, axis=0, keepdims=True) + jnp.sum(
                p2 * dp2, axis=0, keepdims=True
            )
            ds1, ds2 = (p1 * (dp1 - delta)).astype(BF16), (p2 * (dp2 - delta)).astype(BF16)
            p1, p2 = p1.astype(BF16), p2.astype(BF16)
            out = tn(p1, v1) + tn(p2, v2)
            mixed_s[here, lanes] = jnp.where(even, out[0:128], out[128:256]).astype(BF16)
            dq = (tn(ds1, k1) + tn(ds2, k2)) * scale
            dq_s[here, lanes] = jnp.where(even, dq[0:128], dq[128:256]).astype(BF16)
            dk_s[win, lanes] += nn(ds1, qm)
            dv_s[win, lanes] += nn(p1, dom)
            dkc_s[:, lanes] += nn(ds2, qm)
            dvc_s[:, lanes] += nn(p2, dom)
        return carry

    lax.fori_loop(0, tiles, tile_step, 0)

    row_at = pl.multiple_of(jnp.where(upper, 32 + points, 0), 32)
    dkh = jnp.concatenate([dk_s[pl.ds(row_at, 32), :], dkc_s[...]], 0).astype(BF16)
    dvh = jnp.concatenate([dv_s[pl.ds(row_at, 32), :], dvc_s[...]], 0).astype(BF16)
    dq = dq_s[...]
    dk = dk_s[32 : 32 + points, :].astype(BF16)
    dv = dv_s[32 : 32 + points, :].astype(BF16)
    wq, wk, wv = (w_ref[:, i * width : (i + 1) * width] for i in range(3))
    dn_ref[...] = nt(dq, wq) + nt(dk, wk) + nt(dv, wv)
    back = (nt(dkh, wk) + nt(dvh, wv)).astype(BF16)
    brow_ref[...] = back[0:32]
    for ref, at in ((bleft_ref, 32), (bright_ref, 64)):
        ref[0:32, :] = back[at : at + 32]
        ref[32:48, :] = back[CORNER:HALO]
    dw_ref[0:width, :] = tn(dq, normal).astype(BF16)
    dw_ref[width : 2 * width, :] = (tn(dk, normal) + tn(dkh, halo)).astype(BF16)
    dw_ref[2 * width : 3 * width, :] = (tn(dv, normal) + tn(dvh, halo)).astype(BF16)
    dw_ref[3 * width : 4 * width, :] = tn(mixed_s[...], cot).astype(BF16)


def third_kernel(
    first, lat_ref, n0, n1, n2, n3, n4, n5, q_ref, kv_ref, p_ref, mixed_ref, h_ref, dn1_ref, cot_ref,
    packs_ref, wt_ref, wo_ref, gain_ref, dw_in,
    dh_ref, d0, d1, d2, d3, d4, d5, dw_ref,
    dw_s, dmix_s, dkv_s, dq_s, dp_s,
):
    width, tile = q_ref.shape
    head = width // HEADS
    scale = head**-0.5
    blocks = (n0, n1, n2, n3, n4, n5)
    outs = (d0, d1, d2, d3, d4, d5)
    step = pl.program_id(0)

    @pl.when(step == 0)
    def _():
        dw_s[...] = jnp.zeros_like(dw_s) if dw_in is None else dw_in[...]

    brow = jnp.where(lat_ref[0] == 0, 31, 0)
    shape = (tile, RETURNED)
    token = first + step * tile + iota(shape, 0)
    r, c, slot = token // 32, token % 32, iota(shape, 1)
    border = r == brow
    place = one_hot(
        (border & (slot < 32) & (slot == c))
        | ((c == 0) & (slot < 64) & (slot == 32 + r))
        | ((c == 31) & (slot < 112) & (slot == 80 + r))
        | (border & (c == 0) & (slot == 128 + 33))
        | (border & (c == 31) & (slot == 176 + 32))
    )
    dn = dn1_ref[...] + nn(place, packs_ref[...])
    dh = cot_ref[...] + norm_back(h_ref[...].astype(F32), gain_ref[...], dn)
    dh_ref[...] = dh
    dhb = dh.astype(BF16)
    dmix_s[...] = nt(wo_ref[...], dhb)
    dw_s[3 * width : 4 * width, :] += nn(mixed_ref[...], dhb)
    for h in range(HEADS):
        lo, hi = h * head, (h + 1) * head
        dmix = dmix_s[lo:hi, :]
        delta = jnp.zeros((1, tile), F32)
        for b in range(len(blocks)):
            dp = jnp.sum(
                dmix * kv_ref[b, width + lo : width + hi, :].astype(F32), axis=0, keepdims=True
            )
            dp_s[b : b + 1, :] = dp
            delta = delta + p_ref[b, h : h + 1, :] * dp
        q = q_ref[lo:hi, :].astype(F32)
        dq = jnp.zeros((head, tile), F32)
        for b in range(len(blocks)):
            p = p_ref[b, h : h + 1, :]
            ds = p * (dp_s[b : b + 1, :] - delta) * scale
            dq = dq + ds * kv_ref[b, lo:hi, :].astype(F32)
            dkv_s[b, lo:hi, :] = (ds * q).astype(BF16)
            dkv_s[b, width + lo : width + hi, :] = (p * dmix).astype(BF16)
        dq_s[lo:hi, :] = dq.astype(BF16)
    dq = dq_s[...]
    dw_s[0:width, :] += nn(dq, n0[...])
    for b, (ref, out) in enumerate(zip(blocks, outs)):
        dkv = dkv_s[b]
        grad = tn(dkv, wt_ref[width : 3 * width])
        if b == 0:
            grad = grad + tn(dq, wt_ref[0:width])
        out[...] = grad.astype(out.dtype)
        dw_s[width : 3 * width, :] += nn(dkv, ref[...])

    @pl.when(step == pl.num_programs(0) - 1)
    def _():
        dw_ref[...] = dw_s[...].astype(dw_ref.dtype)


def last_kernel(
    first, start_ref, vis_ref, gain_ref, dh_ref, own_ref, far_ref, near_ref, prev_ref, out_ref
):
    tile, width = start_ref.shape
    shown = shown_column(vis_ref[...], first + pl.program_id(0) * tile, tile)
    dn = own_ref[...] + far_ref[...].astype(F32) + near_ref[...].astype(F32)
    grad = dh_ref[...] + norm_back(start_ref[...].astype(F32), gain_ref[...], dn)
    out_ref[...] = jnp.where(shown > 0.5, grad, 0.0)


def weights_kernel(factor, r0_ref, r1_ref, wt_ref, gain_ref, qkv_ref, out_ref, gain_out_ref):
    width = r0_ref.shape[1]
    for layer, ref in enumerate((r0_ref, r1_ref)):
        acc = jnp.zeros((1, width), F32)
        for i in range(3):
            lo, hi = i * width, (i + 1) * width
            grad = ref[lo:hi, :].astype(F32) * factor
            weight = wt_ref[layer, lo:hi, :].astype(F32)
            acc = acc + jnp.sum(weight * grad, axis=0, keepdims=True)
            qkv_ref[layer, :, lo:hi] = grad.T
        out_ref[layer] = ref[3 * width : 4 * width, :].astype(F32) * factor
        gain_out_ref[layer : layer + 1, :] = acc / gain_ref[layer : layer + 1, :]


def call(
    kernel, out_shape, scratch=(), grid=None, in_specs=None, out_specs=None, us=1, aliases=None
):
    return pl.pallas_call(
        kernel,
        out_shape=out_shape,
        grid_spec=pltpu.PrefetchScalarGridSpec(
            num_scalar_prefetch=0,
            grid=grid or (),
            in_specs=in_specs,
            out_specs=out_specs,
            scratch_shapes=list(scratch),
        ),
        input_output_aliases=aliases or {},
        cost_estimate=pl.CostEstimate(
            flops=int(us * 1e6 * 800), bytes_accessed=int(us * 1e6), transcendentals=0
        ),
        compiler_params=pltpu.CompilerParams(vmem_limit_bytes=VMEM_BYTES),
    )


def whole():
    return pl.BlockSpec(memory_space=pltpu.VMEM)


def scalar():
    return pl.BlockSpec(memory_space=pltpu.SMEM)


def fixed(shape):
    return pl.BlockSpec(shape, lambda i: (0,) * len(shape))


def token_spec(tile, width, first=0):
    at = first // tile
    return pl.BlockSpec((tile, width), lambda i: (i + at, 0))


CHUNKS = 2


def local(
    tokens, visible, mask_token, norm_gain_table, query_key_value_weight, output_weight, cotangent
):
    rows, cols, width = tokens.shape
    points = rows * cols
    size = points // CHUNKS
    firsts = [c * size for c in range(CHUNKS)]
    lat_count, lon_count = lax.axis_size("lat"), lax.axis_size("lon")
    lat = lax.axis_index("lat").astype(jnp.int32).reshape(1)
    gain0, gain1 = norm_gain_table[0:1], norm_gain_table[1:2]
    w1 = query_key_value_weight[1]
    wo0, wo1 = output_weight[0], output_weight[1]
    wt = jnp.swapaxes(query_key_value_weight, 1, 2)
    wt0 = wt[0]
    struct = jax.ShapeDtypeStruct
    tokens = tokens.reshape(points, width)
    cot = cotangent.reshape(points, width)
    mask_row = mask_token.reshape(1, width)
    part = struct((size, width), BF16)

    small = 128
    starts, normals = [], []
    for first in firsts:
        start, normal = call(
            functools.partial(start_kernel, first),
            (part, part),
            grid=(size // small,),
            in_specs=[
                token_spec(small, width, first),
                fixed((rows, cols)),
                fixed((1, width)),
                fixed((1, width)),
            ],
            out_specs=(token_spec(small, width),) * 2,
            us=2,
        )(tokens, visible, mask_row, gain0)
        starts.append(start)
        normals.append(normal)

    blocks = []
    before = None
    for c in range(CHUNKS):
        own = normals[c]
        if before is not None:
            own, before = chained(own, before)
        swapped = lon_swap(own)
        beyond = lon_forward(swapped)
        before = swapped
        blocks.append(
            [own, lat_swap(own), swapped, beyond, lat_swap(swapped), lat_swap(beyond)]
        )

    tile = 256
    steps = size // tile
    tok_spec = token_spec(tile, width)
    feat_spec = pl.BlockSpec((width, tile), lambda i: (0, i))
    kv_spec = pl.BlockSpec((6, 2 * width, tile), lambda i: (0, 0, i))
    p_spec = pl.BlockSpec((6, 8, tile), lambda i: (0, 0, i))
    packs = [jnp.zeros((32, width), BF16)] * 3
    kept = []
    for c in range(CHUNKS):
        *keep, normal1, row, left, right = call(
            functools.partial(first_kernel, firsts[c]),
            (
                struct((width, size), BF16),
                struct((6, 2 * width, size), BF16),
                struct((6, 8, size), F32),
                struct((width, size), BF16),
                part,
                part,
                *[struct((32, width), BF16)] * 3,
            ),
            grid=(steps,),
            in_specs=[scalar()]
            + [tok_spec] * 7
            + [fixed((32, width))] * 3
            + [fixed((3 * width, width)), fixed((width, width)), fixed((1, width))],
            out_specs=(
                feat_spec, kv_spec, p_spec, feat_spec, tok_spec, tok_spec,
                *[fixed((32, width))] * 3,
            ),
            scratch=[pltpu.VMEM((6, 8, tile), F32), pltpu.VMEM((96, width), F32)],
            us=7,
        )(lat, *blocks[c], starts[c], *packs, wt0, wo0, gain1)
        packs = [row, left, right]
        kept.append((keep, normal1))

    row, left, right = packs
    from_l, from_r = from_left(right), from_right(left)
    ext = points + 64
    halo_cols = HALO - 32
    dn1, brow, bleft, bright, dw1 = call(
        second_kernel,
        (
            struct((points, width), F32),
            struct((32, width), BF16),
            struct((48, width), BF16),
            struct((48, width), BF16),
            struct((4 * width, width), BF16),
        ),
        in_specs=[scalar()] + [whole()] * 10,
        out_specs=(whole(),) * 5,
        scratch=[
            pltpu.VMEM((points, width), BF16),
            pltpu.VMEM((ext, width), BF16),
            pltpu.VMEM((ext, width), BF16),
            pltpu.VMEM((halo_cols, width), BF16),
            pltpu.VMEM((halo_cols, width), BF16),
            pltpu.VMEM((points, width), BF16),
            pltpu.VMEM((ext, width), F32),
            pltpu.VMEM((ext, width), F32),
            pltpu.VMEM((halo_cols, width), F32),
            pltpu.VMEM((halo_cols, width), F32),
            pltpu.VMEM((points, width), BF16),
            pltpu.VMEM((points, width), BF16),
            pltpu.VMEM((HALO, width), BF16),
            pltpu.VMEM((192, 256), F32),
            pltpu.VMEM((points, width), BF16),
        ],
        us=22,
    )(
        lat, kept[0][1], kept[1][1], lat_swap(row), from_l, from_r, lat_swap(from_l),
        lat_swap(from_r), w1, wo1, cot,
    )

    sum1 = summed(dw1)

    from_l, from_r = from_left(bright), from_right(bleft)
    packs = jnp.concatenate(
        [lat_swap(brow), from_l, from_r, lat_swap(from_l), lat_swap(from_r)], 0
    )
    weights = None
    backs = []
    for c in range(CHUNKS):
        q0, kv0, p0, mixed0, h1 = kept[c][0]
        final = c == CHUNKS - 1
        kernel = functools.partial(third_kernel, firsts[c])
        extra = [] if weights is None else [weights]
        if weights is None:
            kernel = functools.partial(without_weights, kernel)
        *back, weights = call(
            kernel,
            (
                struct((size, width), F32),
                struct((size, width), F32),
                *[part] * 5,
                struct((4 * width, width), BF16 if final else F32),
            ),
            grid=(steps,),
            in_specs=[scalar()]
            + [tok_spec] * 6
            + [feat_spec, kv_spec, p_spec, feat_spec, tok_spec]
            + [token_spec(tile, width, firsts[c])] * 2
            + [
                fixed((RETURNED, width)),
                fixed((3 * width, width)),
                fixed((width, width)),
                fixed((1, width)),
            ]
            + [fixed((4 * width, width))] * len(extra),
            out_specs=(*[tok_spec] * 7, fixed((4 * width, width))),
            scratch=[
                pltpu.VMEM((4 * width, width), F32),
                pltpu.VMEM((width, tile), F32),
                pltpu.VMEM((6, 2 * width, tile), BF16),
                pltpu.VMEM((width, tile), BF16),
                pltpu.VMEM((8, tile), F32),
            ],
            us=11,
        )(
            lat, *blocks[c], q0, kv0, p0, mixed0, h1, dn1, cot, packs, wt0, wo0, gain1, *extra
        )
        backs.append(back)

    sum0 = summed(weights)

    def plus(a, b):
        return (a.astype(F32) + b.astype(F32)).astype(BF16)

    grad_tokens = None
    for c in range(CHUNKS):
        dh1, d0, d1, d2, d3, d4, d5 = backs[c]
        d3 = plus(d3, lat_swap(d5))
        d2 = plus(d2, lat_swap(d4))
        d2 = plus(d2, lon_backward(d3))
        extra = [] if grad_tokens is None else [grad_tokens]
        kernel = functools.partial(last_kernel, firsts[c])
        grad_tokens = call(
            kernel if extra else functools.partial(without_previous, kernel),
            struct((points, width), F32),
            grid=(size // small,),
            in_specs=[
                token_spec(small, width),
                fixed((rows, cols)),
                fixed((1, width)),
                *[token_spec(small, width)] * 4,
            ]
            + [pl.BlockSpec(memory_space=pl.ANY)] * len(extra),
            out_specs=token_spec(small, width, firsts[c]),
            aliases={7: 0} if extra else {},
            us=2,
        )(starts[c], visible, gain0, dh1, d0, lon_swap(d2), lat_swap(d1), *extra)

    factor = (points * lat_count * lon_count) ** (-0.5)
    g_qkv, g_out, g_gain = call(
        functools.partial(weights_kernel, factor),
        (
            struct((2, width, 3 * width), F32),
            struct((2, width, width), F32),
            struct((2, width), F32),
        ),
        in_specs=[whole()] * 4,
        out_specs=(whole(),) * 3,
        us=4,
    )(sum0, sum1, wt, norm_gain_table)
    return grad_tokens.reshape(rows, cols, width), g_qkv, g_out, g_gain


def without_weights(kernel, *refs):
    kernel(*refs[:18], None, *refs[18:])


def without_previous(kernel, *refs):
    kernel(*refs[:7], None, *refs[7:])


def solution(mesh):
    return jax.shard_map(
        local,
        mesh=mesh,
        in_specs=(
            P(("group", "lat"), "lon", None),
            P(("group", "lat"), "lon"),
            P(),
            P(),
            P(),
            P(),
            P(("group", "lat"), "lon", None),
        ),
        out_specs=(
            P(("group", "lat"), "lon", None),
            P("group", None, None),
            P("group", None, None),
            P("group", None),
        ),
        check_vma=False,
    )
```

```python
import functools

import jax
import jax.numpy as jnp
from jax import lax
from jax.experimental import pallas as pl
from jax.experimental.pallas import tpu as pltpu
from jax.sharding import PartitionSpec as P

HEADS = 6
EPS = 1e-05
F32 = jnp.float32
BF16 = jnp.bfloat16
VMEM_BYTES = 56 * 1024 * 1024
HALO = 112
CORNER = 96
RETURNED = 224


def nn(a, b):
    return lax.dot_general(a, b, (((1,), (0,)), ((), ())), preferred_element_type=F32)


def nt(a, b):
    return lax.dot_general(a, b, (((1,), (1,)), ((), ())), preferred_element_type=F32)


def tn(a, b):
    return lax.dot_general(a, b, (((0,), (0,)), ((), ())), preferred_element_type=F32)


def iota(shape, dim):
    return lax.broadcasted_iota(jnp.int32, shape, dim)


def one_hot(condition):
    return jnp.where(condition, 1.0, 0.0).astype(BF16)


def permuted(value, axis, target):
    count = lax.axis_size(axis)
    return lax.ppermute(value, axis, [(i, target(i) % count) for i in range(count)])


def lat_swap(value):
    return permuted(value, "lat", lambda i: i ^ 1)


def lon_swap(value):
    return permuted(value, "lon", lambda i: i ^ 1)


def lon_forward(value):
    return permuted(value, "lon", lambda i: i + 2 if i % 2 == 0 else i - 2)


def lon_backward(value):
    return permuted(value, "lon", lambda i: i - 2 if i % 2 == 0 else i + 2)


def from_left(value):
    return permuted(value, "lon", lambda i: i + 1)


def from_right(value):
    return permuted(value, "lon", lambda i: i - 1)


def chained(value, after):
    return lax.optimization_barrier((value, after))


def exchanged(parts, axis_stride, factor):
    count = lax.axis_size("lon")
    digit = (lax.axis_index("lon") // axis_stride) % factor
    moved = []
    for d in range(1, factor):
        pairs = [(i, shifted(i, axis_stride, factor, d)) for i in range(count)]
        moved.append(lax.ppermute(parts(lax.rem(digit + d, factor)), "lon", pairs))
    total = parts(digit).astype(F32)
    for piece in moved:
        total = total + piece.astype(F32)
    return total.astype(BF16)


def shifted(i, stride, factor, d):
    digit = (i // stride) % factor
    return i + ((digit + d) % factor - digit) * stride


def spread(value, axis_stride, factor):
    count = lax.axis_size("lon")
    digit = (lax.axis_index("lon") // axis_stride) % factor
    rows = value.shape[0]
    full = jnp.zeros((factor * rows,) + value.shape[1:], value.dtype)
    full = lax.dynamic_update_slice(full, value, (digit * rows, 0))
    for d in range(1, factor):
        pairs = [(i, shifted(i, axis_stride, factor, d)) for i in range(count)]
        got = lax.ppermute(value, "lon", pairs)
        at = lax.rem(digit - d + factor, factor) * rows
        full = lax.dynamic_update_slice(full, got, (at, 0))
    return full


def lon_factors():
    left = lax.axis_size("lon")
    stride, out = 1, []
    for factor in [2] + [4] * 10:
        if left == 1:
            break
        factor = min(factor, left)
        out.append((stride, factor))
        stride, left = stride * factor, left // factor
    return out


def halves_summed(value):
    lat = lax.axis_index("lat")
    half = value.shape[0] // 2
    mine = lax.dynamic_slice_in_dim(value, lat * half, half, 0)
    other = lat_swap(lax.dynamic_slice_in_dim(value, (1 - lat) * half, half, 0))
    return (mine.astype(F32) + other.astype(F32)).astype(BF16)


def stage_summed(value, stage):
    stride, factor = stage
    size = value.shape[0] // factor
    return exchanged(
        lambda k: lax.dynamic_slice_in_dim(value, k * size, size, 0), stride, factor
    )


def norm_parts(x):
    mean = jnp.mean(x, axis=-1, keepdims=True)
    centred = x - mean
    spread = jnp.mean(centred * centred, axis=-1, keepdims=True)
    rstd = lax.rsqrt(spread + EPS)
    return centred * rstd, rstd


def norm_back(x, gain, grad_normal):
    xhat, rstd = norm_parts(x)
    g = grad_normal * gain
    return rstd * (
        g - jnp.mean(g, axis=-1, keepdims=True) - xhat * jnp.mean(g * xhat, axis=-1, keepdims=True)
    )


def shown_column(visible, base, tile):
    rows, cols = visible.shape
    token = base + iota((tile, rows), 0)
    of_row = nn(one_hot(token // cols == iota((tile, rows), 1)), visible.astype(F32).astype(BF16))
    token = base + iota((tile, cols), 0)
    mine = token % cols == iota((tile, cols), 1)
    return jnp.sum(jnp.where(mine, of_row, 0.0), axis=1, keepdims=True)


def start_kernel(first, tok_ref, vis_ref, mask_ref, gain_ref, start_ref, normal_ref):
    tile, width = tok_ref.shape
    base = first + pl.program_id(0) * tile
    shown = shown_column(vis_ref[...], base, tile)
    x = jnp.where(shown > 0.5, tok_ref[...].astype(F32), mask_ref[...].astype(F32).reshape(1, width))
    start_ref[...] = x.astype(BF16)
    xhat, _ = norm_parts(x)
    normal_ref[...] = (xhat * gain_ref[0:1, :]).astype(BF16)


def first_kernel(
    first, lat_ref, n0, n1, n2, n3, n4, n5, start_ref, row_in, left_in, right_in,
    wt_ref, wo_ref, gain_ref,
    q_ref, kv_ref, p_ref, mixed_ref, h_ref, normal_ref, row_ref, left_ref, right_ref,
    w_s, pack_s,
):
    width, tile = q_ref.shape
    head = width // HEADS
    blocks = (n0, n1, n2, n3, n4, n5)
    q_ref[...] = nt(wt_ref[0:width], n0[...]).astype(BF16)
    for b, ref in enumerate(blocks):
        kv_ref[b] = nt(wt_ref[width : 3 * width], ref[...]).astype(BF16)
    for h in range(HEADS):
        lo, hi = h * head, (h + 1) * head
        q = q_ref[lo:hi, :].astype(F32) * (head**-0.5)
        total = jnp.zeros((1, tile), F32)
        out = jnp.zeros((head, tile), F32)
        for b in range(len(blocks)):
            k = kv_ref[b, lo:hi, :].astype(F32)
            w = jnp.exp(jnp.sum(q * k, axis=0, keepdims=True))
            w_s[b, h : h + 1, :] = w
            total = total + w
            out = out + w * kv_ref[b, width + lo : width + hi, :].astype(F32)
        inverse = 1.0 / total
        for b in range(len(blocks)):
            p_ref[b, h : h + 1, :] = w_s[b, h : h + 1, :] * inverse
        mixed_ref[lo:hi, :] = (out * inverse).astype(BF16)
    h1 = start_ref[...].astype(F32) + tn(mixed_ref[...], wo_ref[...])
    h1 = h1.astype(BF16)
    h_ref[...] = h1
    xhat, _ = norm_parts(h1.astype(F32))
    normal = (xhat * gain_ref[1:2, :]).astype(BF16)
    normal_ref[...] = normal
    step = pl.program_id(0)
    brow = jnp.where(lat_ref[0] == 0, 31, 0)
    slot = iota((96, tile), 0)
    token = first + step * tile + iota((96, tile), 1)
    r, c = token // 32, token % 32
    pick = one_hot(
        ((slot < 32) & (r == brow) & (c == slot))
        | ((slot >= 32) & (slot < 64) & (c == 0) & (r == slot - 32))
        | ((slot >= 64) & (c == 31) & (r == slot - 64))
    )

    @pl.when(step == 0)
    def _():
        for i, ref in enumerate((row_in, left_in, right_in)):
            known = jnp.zeros((32, width), F32) if ref is None else ref[...].astype(F32)
            pack_s[i * 32 : i * 32 + 32, :] = known

    pack_s[...] += nn(pick, normal)

    @pl.when(step == pl.num_programs(0) - 1)
    def _():
        for i, ref in enumerate((row_ref, left_ref, right_ref)):
            ref[...] = pack_s[i * 32 : i * 32 + 32, :].astype(BF16)


def second_kernel(
    lat_ref, na_ref, nb_ref, row_ref, left_ref, right_ref, dleft_ref, dright_ref,
    w_all, wo_all, cot_ref,
    dq_ref, dk_ref, dv_ref, mixed_s, dkh_ref, dvh_ref, halo_s, brow_ref, bleft_ref, bright_ref,
    q_s, k_s, v_s, kc_s, vc_s, dk_s, dv_s, dkc_s, dvc_s, do_s, mask_s, normal_s,
):
    points, width = cot_ref.shape
    head = width // HEADS
    w_ref, wo_ref = w_all.at[1], wo_all.at[1]
    upper = lat_ref[0] == 0
    halo_s[0:32, :] = row_ref[...]
    halo_s[32:64, :] = left_ref[...]
    halo_s[64:96, :] = right_ref[...]
    a, b = iota((16, 32), 0), iota((16, 32), 1)
    sent = b == jnp.where(upper, 0, 31)
    corners = nn(one_hot(sent & (a == 0)), dleft_ref[...])
    corners += nn(one_hot(sent & (a == 1)), dright_ref[...])
    halo_s[CORNER:HALO, :] = corners.astype(BF16)
    halo = halo_s[...]
    normal_s[0 : points // 2, :] = na_ref[...]
    normal_s[points // 2 : points, :] = nb_ref[...]
    normal = normal_s[...]
    scale = head**-0.5
    q_s[...] = (nn(normal, w_ref[:, 0:width]).astype(BF16).astype(F32) * scale).astype(BF16)
    k_s[32 : 32 + points, :] = nn(normal, w_ref[:, width : 2 * width]).astype(BF16)
    v_s[32 : 32 + points, :] = nn(normal, w_ref[:, 2 * width : 3 * width]).astype(BF16)
    kh = nn(halo, w_ref[:, width : 2 * width]).astype(BF16)
    vh = nn(halo, w_ref[:, 2 * width : 3 * width]).astype(BF16)
    for at in (0, 32 + points):
        k_s[at : at + 32, :] = kh[0:32]
        v_s[at : at + 32, :] = vh[0:32]
    kc_s[...] = kh[32:HALO]
    vc_s[...] = vh[32:HALO]
    dk_s[...] = jnp.zeros_like(dk_s)
    dv_s[...] = jnp.zeros_like(dv_s)
    dkc_s[...] = jnp.zeros_like(dkc_s)
    dvc_s[...] = jnp.zeros_like(dvc_s)
    cot = cot_ref[...].astype(BF16)
    do_s[...] = nt(cot, wo_ref[...]).astype(BF16)

    key, query = iota((192, 256), 0), iota((192, 256), 1) % 128
    drow = key // 32 - 1 - query // 32
    dcol = key % 32 - query % 32
    mask_s[...] = jnp.where((jnp.abs(drow) <= 1) & (jnp.abs(dcol) <= 1), 1.0, 0.0)

    tiles = points // 128

    def tile_step(t, carry):
        base = pl.multiple_of(t * 128, 128)
        key = iota((192, 256), 0)
        first = jnp.where(upper & (t == 0), 32, 0)
        last = jnp.where(jnp.logical_not(upper) & (t == tiles - 1), 160, 192)
        mask1 = (mask_s[...] > 0.5) & (key >= first) & (key < last)
        e, query = iota((HALO - 32, 256), 0), iota((HALO - 32, 256), 1) % 128
        corner = e >= 64
        key_row = jnp.where(corner, jnp.where(upper, 32, -1), e % 32)
        is_left = (e < 32) | (e == 64)
        near = jnp.abs(key_row - (4 * t + query // 32)) <= 1
        side = query % 32 == jnp.where(is_left, 0, 31)
        mask2 = near & side & (e < 66)
        lane = iota((128, 128), 1)
        even = lane < 64
        for pair in range(HEADS // 2):
            lanes = slice(pair * 128, pair * 128 + 128)
            win = pl.ds(base, 192)
            here = pl.ds(base, 128)
            q = q_s[here, lanes]
            do = do_s[here, lanes]
            zero = jnp.zeros_like(q)
            qm = jnp.concatenate([jnp.where(even, q, zero), jnp.where(even, zero, q)], 0)
            dom = jnp.concatenate([jnp.where(even, do, zero), jnp.where(even, zero, do)], 0)
            k1, v1 = k_s[win, lanes], v_s[win, lanes]
            k2, v2 = kc_s[:, lanes], vc_s[:, lanes]
            w1 = jnp.where(mask1, jnp.exp(nt(k1, qm)), 0.0)
            w2 = jnp.where(mask2, jnp.exp(nt(k2, qm)), 0.0)
            total = jnp.sum(w1, axis=0, keepdims=True) + jnp.sum(w2, axis=0, keepdims=True)
            inverse = 1.0 / total
            p1, p2 = w1 * inverse, w2 * inverse
            dp1, dp2 = nt(v1, dom), nt(v2, dom)
            delta = jnp.sum(p1 * dp1, axis=0, keepdims=True) + jnp.sum(
                p2 * dp2, axis=0, keepdims=True
            )
            ds1, ds2 = (p1 * (dp1 - delta)).astype(BF16), (p2 * (dp2 - delta)).astype(BF16)
            p1, p2 = p1.astype(BF16), p2.astype(BF16)
            out = tn(p1, v1) + tn(p2, v2)
            mixed_s[here, lanes] = jnp.where(even, out[0:128], out[128:256]).astype(BF16)
            dq = (tn(ds1, k1) + tn(ds2, k2)) * scale
            dq_ref[here, lanes] = jnp.where(even, dq[0:128], dq[128:256]).astype(BF16)
            dk_s[win, lanes] += nn(ds1, qm)
            dv_s[win, lanes] += nn(p1, dom)
            dkc_s[:, lanes] += nn(ds2, qm)
            dvc_s[:, lanes] += nn(p2, dom)
        return carry

    lax.fori_loop(0, tiles, tile_step, 0)

    row_at = pl.multiple_of(jnp.where(upper, 32 + points, 0), 32)
    dkh = jnp.concatenate([dk_s[pl.ds(row_at, 32), :], dkc_s[...]], 0).astype(BF16)
    dvh = jnp.concatenate([dv_s[pl.ds(row_at, 32), :], dvc_s[...]], 0).astype(BF16)
    dkh_ref[...] = dkh
    dvh_ref[...] = dvh
    dk_ref[...] = dk_s[32 : 32 + points, :].astype(BF16)
    dv_ref[...] = dv_s[32 : 32 + points, :].astype(BF16)
    wk, wv = (w_ref[:, i * width : (i + 1) * width] for i in (1, 2))
    back = (nt(dkh, wk) + nt(dvh, wv)).astype(BF16)
    brow_ref[...] = back[0:32]
    for ref, at in ((bleft_ref, 32), (bright_ref, 64)):
        ref[0:32, :] = back[at : at + 32]
        ref[32:48, :] = back[CORNER:HALO]


def second_weights_kernel(
    na_ref, nb_ref, halo_ref, dq_ref, dk_ref, dv_ref, mixed_ref, dkh_ref, dvh_ref,
    w_all, cot_ref, dn_ref, dw_ref, normal_s,
):
    points, width = cot_ref.shape
    normal_s[0 : points // 2, :] = na_ref[...]
    normal_s[points // 2 : points, :] = nb_ref[...]
    normal, halo = normal_s[...], halo_ref[...]
    wq, wk, wv = (w_all[1, :, i * width : (i + 1) * width] for i in range(3))
    dw_ref[0:width, :] = tn(dq_ref[...], normal).astype(BF16)
    dw_ref[width : 2 * width, :] = (tn(dk_ref[...], normal) + tn(dkh_ref[...], halo)).astype(BF16)
    dw_ref[2 * width : 3 * width, :] = (
        tn(dv_ref[...], normal) + tn(dvh_ref[...], halo)
    ).astype(BF16)
    dw_ref[3 * width : 4 * width, :] = tn(mixed_ref[...], cot_ref[...].astype(BF16)).astype(BF16)
    dn_ref[...] = nt(dq_ref[...], wq) + nt(dk_ref[...], wk) + nt(dv_ref[...], wv)


def third_kernel(
    first, lat_ref, n0, n1, n2, n3, n4, n5, q_ref, kv_ref, p_ref, mixed_ref, h_ref, dn1_ref, cot_ref,
    packs_ref, wt_ref, wo_ref, gain_ref, dw_in,
    dh_ref, d0, d1, d2, d3, d4, d5, dw_ref,
    dw_s, dmix_s, dkv_s, dq_s, dp_s,
):
    width, tile = q_ref.shape
    head = width // HEADS
    scale = head**-0.5
    blocks = (n0, n1, n2, n3, n4, n5)
    outs = (d0, d1, d2, d3, d4, d5)
    step = pl.program_id(0)

    @pl.when(step == 0)
    def _():
        dw_s[...] = jnp.zeros_like(dw_s) if dw_in is None else dw_in[...]

    brow = jnp.where(lat_ref[0] == 0, 31, 0)
    shape = (tile, RETURNED)
    token = first + step * tile + iota(shape, 0)
    r, c, slot = token // 32, token % 32, iota(shape, 1)
    border = r == brow
    place = one_hot(
        (border & (slot < 32) & (slot == c))
        | ((c == 0) & (slot < 64) & (slot == 32 + r))
        | ((c == 31) & (slot < 112) & (slot == 80 + r))
        | (border & (c == 0) & (slot == 128 + 33))
        | (border & (c == 31) & (slot == 176 + 32))
    )
    dn = dn1_ref[...] + nn(place, packs_ref[...])
    dh = cot_ref[...] + norm_back(h_ref[...].astype(F32), gain_ref[1:2, :], dn)
    dh_ref[...] = dh
    dhb = dh.astype(BF16)
    dmix_s[...] = nt(wo_ref[...], dhb)
    dw_s[3 * width : 4 * width, :] += nn(mixed_ref[...], dhb)
    for h in range(HEADS):
        lo, hi = h * head, (h + 1) * head
        dmix = dmix_s[lo:hi, :]
        delta = jnp.zeros((1, tile), F32)
        for b in range(len(blocks)):
            dp = jnp.sum(
                dmix * kv_ref[b, width + lo : width + hi, :].astype(F32), axis=0, keepdims=True
            )
            dp_s[b : b + 1, :] = dp
            delta = delta + p_ref[b, h : h + 1, :] * dp
        q = q_ref[lo:hi, :].astype(F32)
        dq = jnp.zeros((head, tile), F32)
        for b in range(len(blocks)):
            p = p_ref[b, h : h + 1, :]
            ds = p * (dp_s[b : b + 1, :] - delta) * scale
            dq = dq + ds * kv_ref[b, lo:hi, :].astype(F32)
            dkv_s[b, lo:hi, :] = (ds * q).astype(BF16)
            dkv_s[b, width + lo : width + hi, :] = (p * dmix).astype(BF16)
        dq_s[lo:hi, :] = dq.astype(BF16)
    dq = dq_s[...]
    dw_s[0:width, :] += nn(dq, n0[...])
    for b, (ref, out) in enumerate(zip(blocks, outs)):
        dkv = dkv_s[b]
        grad = tn(dkv, wt_ref[width : 3 * width])
        if b == 0:
            grad = grad + tn(dq, wt_ref[0:width])
        out[...] = grad.astype(out.dtype)
        dw_s[width : 3 * width, :] += nn(dkv, ref[...])

    @pl.when(step == pl.num_programs(0) - 1)
    def _():
        dw_ref[...] = dw_s[...].astype(dw_ref.dtype)


def last_kernel(
    first, start_ref, vis_ref, gain_ref, dh_ref, own_ref, far_ref, near_ref, prev_ref, out_ref
):
    tile, width = start_ref.shape
    shown = shown_column(vis_ref[...], first + pl.program_id(0) * tile, tile)
    dn = own_ref[...] + far_ref[...].astype(F32) + near_ref[...].astype(F32)
    grad = dh_ref[...] + norm_back(start_ref[...].astype(F32), gain_ref[0:1, :], dn)
    out_ref[...] = jnp.where(shown > 0.5, grad, 0.0)


def weights_kernel(
    factor, pieces, lat_ref, mine_ref, other_ref, wt_ref, gain_ref,
    qkv_ref, out_ref, gain_out_ref, rows_s,
):
    total, width = mine_ref.shape
    piece = total // pieces // 2
    lat = lat_ref[0]
    for ref, band in ((mine_ref, lat), (other_ref, 1 - lat)):
        for k in range(pieces):
            at = pl.multiple_of(band * (total // 2) + k * piece, 8)
            for layer in range(2):
                lo = (2 * k + layer) * piece
                rows_s[layer, pl.ds(at, piece), :] = ref[lo : lo + piece, :].astype(F32) * factor
    for layer in range(2):
        acc = jnp.zeros((1, width), F32)
        for i in range(3):
            lo, hi = i * width, (i + 1) * width
            grad = rows_s[layer, lo:hi, :]
            weight = wt_ref[layer, lo:hi, :].astype(F32)
            acc = acc + jnp.sum(weight * grad, axis=0, keepdims=True)
            qkv_ref[layer, :, lo:hi] = grad.T
        out_ref[layer] = rows_s[layer, 3 * width : 4 * width, :]
        gain_out_ref[layer : layer + 1, :] = acc / gain_ref[layer : layer + 1, :]


def call(
    kernel, out_shape, scratch=(), grid=None, in_specs=None, out_specs=None, us=1, aliases=None
):
    return pl.pallas_call(
        kernel,
        out_shape=out_shape,
        grid_spec=pltpu.PrefetchScalarGridSpec(
            num_scalar_prefetch=0,
            grid=grid or (),
            in_specs=in_specs,
            out_specs=out_specs,
            scratch_shapes=list(scratch),
        ),
        input_output_aliases=aliases or {},
        cost_estimate=pl.CostEstimate(
            flops=int(us * 1e6 * 800), bytes_accessed=int(us * 1e6), transcendentals=0
        ),
        compiler_params=pltpu.CompilerParams(vmem_limit_bytes=VMEM_BYTES),
    )


def whole():
    return pl.BlockSpec(memory_space=pltpu.VMEM)


def scalar():
    return pl.BlockSpec(memory_space=pltpu.SMEM)


def fixed(shape):
    return pl.BlockSpec(shape, lambda i: (0,) * len(shape))


def token_spec(tile, width, first=0):
    at = first // tile
    return pl.BlockSpec((tile, width), lambda i: (i + at, 0))


def layer_spec(layer, rows, width):
    return pl.BlockSpec((None, rows, width), lambda i: (layer, 0, 0))


CHUNKS = 2


def local(
    tokens, visible, mask_token, norm_gain_table, query_key_value_weight, output_weight, cotangent
):
    rows, cols, width = tokens.shape
    points = rows * cols
    size = points // CHUNKS
    firsts = [c * size for c in range(CHUNKS)]
    lat_count, lon_count = lax.axis_size("lat"), lax.axis_size("lon")
    lat = lax.axis_index("lat").astype(jnp.int32).reshape(1)
    wt = jnp.swapaxes(query_key_value_weight, 1, 2)
    struct = jax.ShapeDtypeStruct
    tokens = tokens.reshape(points, width)
    cot = cotangent.reshape(points, width)
    part = struct((size, width), BF16)
    every = struct((points, width), BF16)
    gain_spec = fixed((2, width))
    wt_spec, wo_spec = layer_spec(0, 3 * width, width), layer_spec(0, width, width)

    small = 256
    starts, normals = [], []
    for first in firsts:
        start, normal = call(
            functools.partial(start_kernel, first),
            (part, part),
            grid=(size // small,),
            in_specs=[
                token_spec(small, width, first),
                fixed((rows, cols)),
                fixed((width,)),
                gain_spec,
            ],
            out_specs=(token_spec(small, width),) * 2,
            us=2,
        )(tokens, visible, mask_token, norm_gain_table)
        starts.append(start)
        normals.append(normal)

    swapped0 = lon_swap(normals[0])
    own1, swapped0 = chained(normals[1], swapped0)
    swapped1 = lon_swap(own1)
    beyond0, beyond1 = lon_forward(swapped0), lon_forward(swapped1)
    near0, near1 = lat_swap(normals[0]), lat_swap(own1)

    def blocks_of(own, near, swapped, beyond):
        return [own, near, swapped, beyond, lat_swap(swapped), lat_swap(beyond)]

    blocks = [blocks_of(normals[0], near0, swapped0, beyond0), None]

    tile = 256
    steps = size // tile
    tok_spec = token_spec(tile, width)
    feat_spec = pl.BlockSpec((width, tile), lambda i: (0, i))
    kv_spec = pl.BlockSpec((6, 2 * width, tile), lambda i: (0, 0, i))
    p_spec = pl.BlockSpec((6, 8, tile), lambda i: (0, 0, i))
    packs = []
    kept = []
    for c in range(CHUNKS):
        kernel = functools.partial(first_kernel, firsts[c])
        *keep, normal1, row, left, right = call(
            kernel if packs else functools.partial(without, kernel, 8, 3),
            (
                struct((width, size), BF16),
                struct((6, 2 * width, size), BF16),
                struct((6, 8, size), F32),
                struct((width, size), BF16),
                part,
                part,
                *[struct((32, width), BF16)] * 3,
            ),
            grid=(steps,),
            in_specs=[scalar()]
            + [tok_spec] * 7
            + [fixed((32, width))] * len(packs)
            + [wt_spec, wo_spec, gain_spec],
            out_specs=(
                feat_spec, kv_spec, p_spec, feat_spec, tok_spec, tok_spec,
                *[fixed((32, width))] * 3,
            ),
            scratch=[pltpu.VMEM((6, 8, tile), F32), pltpu.VMEM((96, width), F32)],
            us=8,
        )(lat, *blocks[c], starts[c], *packs, wt, output_weight, norm_gain_table)
        packs = [row, left, right]
        kept.append((keep, normal1))
        if c == 0:
            beyond1, row, left, right = lax.optimization_barrier((beyond1, *packs))
            packs = [row, left, right]
            blocks[1] = blocks_of(own1, near1, swapped1, beyond1)

    row, left, right = packs
    from_l, from_r = from_left(right), from_right(left)
    ext = points + 64
    halo_cols = HALO - 32
    halo_struct = struct((HALO, width), BF16)
    dq1, dk1, dv1, mixed1, dkh, dvh, halo, brow, bleft, bright = call(
        second_kernel,
        (
            every, every, every, every, halo_struct, halo_struct, halo_struct,
            struct((32, width), BF16),
            struct((48, width), BF16),
            struct((48, width), BF16),
        ),
        in_specs=[scalar()] + [whole()] * 10,
        out_specs=(whole(),) * 10,
        scratch=[
            pltpu.VMEM((points, width), BF16),
            pltpu.VMEM((ext, width), BF16),
            pltpu.VMEM((ext, width), BF16),
            pltpu.VMEM((halo_cols, width), BF16),
            pltpu.VMEM((halo_cols, width), BF16),
            pltpu.VMEM((ext, width), F32),
            pltpu.VMEM((ext, width), F32),
            pltpu.VMEM((halo_cols, width), F32),
            pltpu.VMEM((halo_cols, width), F32),
            pltpu.VMEM((points, width), BF16),
            pltpu.VMEM((192, 256), F32),
            pltpu.VMEM((points, width), BF16),
        ],
        us=17,
    )(
        lat, kept[0][1], kept[1][1], lat_swap(row), from_l, from_r, lat_swap(from_l),
        lat_swap(from_r), query_key_value_weight, output_weight, cot,
    )

    dn1, dw1 = call(
        second_weights_kernel,
        (struct((points, width), F32), struct((4 * width, width), BF16)),
        in_specs=[whole()] * 11,
        out_specs=(whole(),) * 2,
        scratch=[pltpu.VMEM((points, width), BF16)],
        us=5,
    )(
        kept[0][1], kept[1][1], halo, dq1, dk1, dv1, mixed1, dkh, dvh,
        query_key_value_weight, cot,
    )

    from_l, from_r = from_left(bright), from_right(bleft)
    packs = jnp.concatenate(
        [lat_swap(brow), from_l, from_r, lat_swap(from_l), lat_swap(from_r)], 0
    )
    stages = lon_factors()
    sum1 = halves_summed(dw1)
    packs, sum1 = chained(packs, sum1)

    def plus(a, b):
        return (a.astype(F32) + b.astype(F32)).astype(BF16)

    weights = None
    backs = []
    for c in range(CHUNKS):
        q0, kv0, p0, mixed0, h1 = kept[c][0]
        final = c == CHUNKS - 1
        kernel = functools.partial(third_kernel, firsts[c])
        extra = [] if weights is None else [weights]
        if weights is None:
            kernel = functools.partial(without, kernel, 18, 1)
        dh1, d0, d1, d2, d3, d4, d5, weights = call(
            kernel,
            (
                struct((size, width), F32),
                struct((size, width), F32),
                *[part] * 5,
                struct((4 * width, width), BF16 if final else F32),
            ),
            grid=(steps,),
            in_specs=[scalar()]
            + [tok_spec] * 6
            + [feat_spec, kv_spec, p_spec, feat_spec, tok_spec]
            + [token_spec(tile, width, firsts[c])] * 2
            + [fixed((RETURNED, width)), wt_spec, wo_spec, gain_spec]
            + [fixed((4 * width, width))] * len(extra),
            out_specs=(*[tok_spec] * 7, fixed((4 * width, width))),
            scratch=[
                pltpu.VMEM((4 * width, width), F32),
                pltpu.VMEM((width, tile), F32),
                pltpu.VMEM((6, 2 * width, tile), BF16),
                pltpu.VMEM((width, tile), BF16),
                pltpu.VMEM((8, tile), F32),
            ],
            us=13,
        )(
            lat, *blocks[c], q0, kv0, p0, mixed0, h1, dn1, cot, packs, wt, output_weight,
            norm_gain_table, *extra,
        )
        d3 = plus(d3, lat_swap(d5))
        d2 = plus(d2, lat_swap(d4))
        d1 = lat_swap(d1)
        if c == 0:
            sum1 = stage_summed(sum1, stages[0])
            weights, sum1, d1, d2, d3 = lax.optimization_barrier((weights, sum1, d1, d2, d3))
            for stage in stages[1:]:
                sum1 = stage_summed(sum1, stage)
        d2 = plus(d2, lon_backward(d3))
        if c == 0:
            held = d2
        backs.append((dh1, d0, d1, d2))

    weights, sum1, held = lax.optimization_barrier((weights, sum1, held))
    backs[0] = backs[0][:3] + (held,)
    sum0 = halves_summed(weights)
    for stage in stages:
        sum0 = stage_summed(sum0, stage)
    sums = jnp.concatenate([sum0, sum1], 0)
    for stage in stages[::-1]:
        sums = spread(sums, *stage)
    other = lat_swap(sums)

    grad_tokens = None
    for c in range(CHUNKS):
        dh1, d0, d1, d2 = backs[c]
        extra = [] if grad_tokens is None else [grad_tokens]
        kernel = functools.partial(last_kernel, firsts[c])
        grad_tokens = call(
            kernel if extra else functools.partial(without, kernel, 7, 1),
            struct((points, width), F32),
            grid=(size // small,),
            in_specs=[token_spec(small, width), fixed((rows, cols)), gain_spec]
            + [token_spec(small, width)] * 4
            + [pl.BlockSpec(memory_space=pl.ANY)] * len(extra),
            out_specs=token_spec(small, width, firsts[c]),
            aliases={7: 0} if extra else {},
            us=4,
        )(starts[c], visible, norm_gain_table, dh1, d0, lon_swap(d2), d1, *extra)

    factor = (points * lat_count * lon_count) ** (-0.5)
    g_qkv, g_out, g_gain = call(
        functools.partial(weights_kernel, factor, lon_count),
        (
            struct((2, width, 3 * width), F32),
            struct((2, width, width), F32),
            struct((2, width), F32),
        ),
        in_specs=[scalar()] + [whole()] * 4,
        out_specs=(whole(),) * 3,
        scratch=[pltpu.VMEM((2, 4 * width, width), F32)],
        us=5,
    )(lat, sums, other, wt, norm_gain_table)
    return grad_tokens.reshape(rows, cols, width), g_qkv, g_out, g_gain


def without(kernel, at, count, *refs):
    kernel(*refs[:at], *[None] * count, *refs[at:])


def solution(mesh):
    return jax.shard_map(
        local,
        mesh=mesh,
        in_specs=(
            P(("group", "lat"), "lon", None),
            P(("group", "lat"), "lon"),
            P(),
            P(),
            P(),
            P(),
            P(("group", "lat"), "lon", None),
        ),
        out_specs=(
            P(("group", "lat"), "lon", None),
            P("group", None, None),
            P("group", None, None),
            P("group", None),
        ),
        check_vma=False,
    )
```

```python
import functools

import jax
import jax.numpy as jnp
from jax import lax
from jax.experimental import pallas as pl
from jax.experimental.pallas import tpu as pltpu
from jax.sharding import PartitionSpec as P

HEADS = 6
EPS = 1e-05
F32 = jnp.float32
BF16 = jnp.bfloat16
VMEM_BYTES = 56 * 1024 * 1024
HALO = 112
CORNER = 96
RETURNED = 224


def nn(a, b):
    return lax.dot_general(a, b, (((1,), (0,)), ((), ())), preferred_element_type=F32)


def nt(a, b):
    return lax.dot_general(a, b, (((1,), (1,)), ((), ())), preferred_element_type=F32)


def tn(a, b):
    return lax.dot_general(a, b, (((0,), (0,)), ((), ())), preferred_element_type=F32)


def iota(shape, dim):
    return lax.broadcasted_iota(jnp.int32, shape, dim)


def one_hot(condition):
    return jnp.where(condition, 1.0, 0.0).astype(BF16)


def permuted(value, axis, target):
    count = lax.axis_size(axis)
    return lax.ppermute(value, axis, [(i, target(i) % count) for i in range(count)])


def lat_swap(value):
    return permuted(value, "lat", lambda i: i ^ 1)


def lon_swap(value):
    return permuted(value, "lon", lambda i: i ^ 1)


def lon_forward(value):
    return permuted(value, "lon", lambda i: i + 2 if i % 2 == 0 else i - 2)


def lon_backward(value):
    return permuted(value, "lon", lambda i: i - 2 if i % 2 == 0 else i + 2)


def from_left(value):
    return permuted(value, "lon", lambda i: i + 1)


def from_right(value):
    return permuted(value, "lon", lambda i: i - 1)


def chained(value, after):
    return lax.optimization_barrier((value, after))


def exchanged(parts, axis_stride, factor):
    count = lax.axis_size("lon")
    digit = (lax.axis_index("lon") // axis_stride) % factor
    moved = []
    for d in range(1, factor):
        pairs = [(i, shifted(i, axis_stride, factor, d)) for i in range(count)]
        moved.append(lax.ppermute(parts(lax.rem(digit + d, factor)), "lon", pairs))
    total = parts(digit).astype(F32)
    for piece in moved:
        total = total + piece.astype(F32)
    return total.astype(BF16)


def shifted(i, stride, factor, d):
    digit = (i // stride) % factor
    return i + ((digit + d) % factor - digit) * stride


def spread(value, axis_stride, factor):
    count = lax.axis_size("lon")
    digit = (lax.axis_index("lon") // axis_stride) % factor
    rows = value.shape[0]
    full = jnp.zeros((factor * rows,) + value.shape[1:], value.dtype)
    full = lax.dynamic_update_slice(full, value, (digit * rows, 0))
    for d in range(1, factor):
        pairs = [(i, shifted(i, axis_stride, factor, d)) for i in range(count)]
        got = lax.ppermute(value, "lon", pairs)
        at = lax.rem(digit - d + factor, factor) * rows
        full = lax.dynamic_update_slice(full, got, (at, 0))
    return full


def lon_factors():
    left = lax.axis_size("lon")
    stride, out = 1, []
    for factor in [2] + [4] * 10:
        if left == 1:
            break
        factor = min(factor, left)
        out.append((stride, factor))
        stride, left = stride * factor, left // factor
    return out


def halves_summed(value):
    lat = lax.axis_index("lat")
    half = value.shape[0] // 2
    mine = lax.dynamic_slice_in_dim(value, lat * half, half, 0)
    other = lat_swap(lax.dynamic_slice_in_dim(value, (1 - lat) * half, half, 0))
    return (mine.astype(F32) + other.astype(F32)).astype(BF16)


def stage_summed(value, stage):
    stride, factor = stage
    size = value.shape[0] // factor
    return exchanged(
        lambda k: lax.dynamic_slice_in_dim(value, k * size, size, 0), stride, factor
    )


def norm_parts(x):
    mean = jnp.mean(x, axis=-1, keepdims=True)
    centred = x - mean
    spread = jnp.mean(centred * centred, axis=-1, keepdims=True)
    rstd = lax.rsqrt(spread + EPS)
    return centred * rstd, rstd


def norm_back(x, gain, grad_normal):
    xhat, rstd = norm_parts(x)
    g = grad_normal * gain
    return rstd * (
        g - jnp.mean(g, axis=-1, keepdims=True) - xhat * jnp.mean(g * xhat, axis=-1, keepdims=True)
    )


def shown_column(visible, base, tile):
    rows, cols = visible.shape
    token = base + iota((tile, rows), 0)
    of_row = nn(one_hot(token // cols == iota((tile, rows), 1)), visible.astype(F32).astype(BF16))
    token = base + iota((tile, cols), 0)
    mine = token % cols == iota((tile, cols), 1)
    return jnp.sum(jnp.where(mine, of_row, 0.0), axis=1, keepdims=True)


def start_kernel(first, tok_ref, vis_ref, mask_ref, gain_ref, start_ref, normal_ref):
    tile, width = tok_ref.shape
    base = first + pl.program_id(0) * tile
    shown = shown_column(vis_ref[...], base, tile)
    x = jnp.where(shown > 0.5, tok_ref[...].astype(F32), mask_ref[...].astype(F32).reshape(1, width))
    start_ref[...] = x.astype(BF16)
    xhat, _ = norm_parts(x)
    normal_ref[...] = (xhat * gain_ref[0:1, :]).astype(BF16)


def first_kernel(
    first, lat_ref, n0, n1, n2, n3, n4, n5, start_ref, row_in, left_in, right_in,
    wt_ref, wo_ref, gain_ref,
    q_ref, kv_ref, p_ref, mixed_ref, h_ref, normal_ref, row_ref, left_ref, right_ref,
    w_s, pack_s,
):
    width, tile = q_ref.shape
    head = width // HEADS
    blocks = (n0, n1, n2, n3, n4, n5)
    q_ref[...] = nt(wt_ref[0:width], n0[...]).astype(BF16)
    for b, ref in enumerate(blocks):
        kv_ref[b] = nt(wt_ref[width : 3 * width], ref[...]).astype(BF16)
    for h in range(HEADS):
        lo, hi = h * head, (h + 1) * head
        q = q_ref[lo:hi, :].astype(F32) * (head**-0.5)
        total = jnp.zeros((1, tile), F32)
        out = jnp.zeros((head, tile), F32)
        for b in range(len(blocks)):
            k = kv_ref[b, lo:hi, :].astype(F32)
            w = jnp.exp(jnp.sum(q * k, axis=0, keepdims=True))
            w_s[b, h : h + 1, :] = w
            total = total + w
            out = out + w * kv_ref[b, width + lo : width + hi, :].astype(F32)
        inverse = 1.0 / total
        for b in range(len(blocks)):
            p_ref[b, h : h + 1, :] = w_s[b, h : h + 1, :] * inverse
        mixed_ref[lo:hi, :] = (out * inverse).astype(BF16)
    h1 = start_ref[...].astype(F32) + tn(mixed_ref[...], wo_ref[...])
    h1 = h1.astype(BF16)
    h_ref[...] = h1
    xhat, _ = norm_parts(h1.astype(F32))
    normal = (xhat * gain_ref[1:2, :]).astype(BF16)
    normal_ref[...] = normal
    step = pl.program_id(0)
    brow = jnp.where(lat_ref[0] == 0, 31, 0)
    slot = iota((96, tile), 0)
    token = first + step * tile + iota((96, tile), 1)
    r, c = token // 32, token % 32
    pick = one_hot(
        ((slot < 32) & (r == brow) & (c == slot))
        | ((slot >= 32) & (slot < 64) & (c == 0) & (r == slot - 32))
        | ((slot >= 64) & (c == 31) & (r == slot - 64))
    )

    @pl.when(step == 0)
    def _():
        for i, ref in enumerate((row_in, left_in, right_in)):
            known = jnp.zeros((32, width), F32) if ref is None else ref[...].astype(F32)
            pack_s[i * 32 : i * 32 + 32, :] = known

    pack_s[...] += nn(pick, normal)

    @pl.when(step == pl.num_programs(0) - 1)
    def _():
        for i, ref in enumerate((row_ref, left_ref, right_ref)):
            ref[...] = pack_s[i * 32 : i * 32 + 32, :].astype(BF16)


def second_kernel(
    lat_ref, na_ref, nb_ref, row_ref, left_ref, right_ref, dleft_ref, dright_ref,
    w_all, wo_all, cot_ref,
    dn_ref, dw_ref, brow_ref, bleft_ref, bright_ref,
    dq_ref, dk_ref, dv_ref, mixed_s, dkh_ref, dvh_ref, halo_s,
    q_s, k_s, v_s, kc_s, vc_s, dk_s, dv_s, dkc_s, dvc_s, do_s, mask_s, normal_s,
):
    points, width = cot_ref.shape
    head = width // HEADS
    w_ref, wo_ref = w_all.at[1], wo_all.at[1]
    upper = lat_ref[0] == 0
    halo_s[0:32, :] = row_ref[...]
    halo_s[32:64, :] = left_ref[...]
    halo_s[64:96, :] = right_ref[...]
    a, b = iota((16, 32), 0), iota((16, 32), 1)
    sent = b == jnp.where(upper, 0, 31)
    corners = nn(one_hot(sent & (a == 0)), dleft_ref[...])
    corners += nn(one_hot(sent & (a == 1)), dright_ref[...])
    halo_s[CORNER:HALO, :] = corners.astype(BF16)
    halo = halo_s[...]
    normal_s[0 : points // 2, :] = na_ref[...]
    normal_s[points // 2 : points, :] = nb_ref[...]
    normal = normal_s[...]
    scale = head**-0.5
    q_s[...] = (nn(normal, w_ref[:, 0:width]).astype(BF16).astype(F32) * scale).astype(BF16)
    k_s[32 : 32 + points, :] = nn(normal, w_ref[:, width : 2 * width]).astype(BF16)
    v_s[32 : 32 + points, :] = nn(normal, w_ref[:, 2 * width : 3 * width]).astype(BF16)
    kh = nn(halo, w_ref[:, width : 2 * width]).astype(BF16)
    vh = nn(halo, w_ref[:, 2 * width : 3 * width]).astype(BF16)
    for at in (0, 32 + points):
        k_s[at : at + 32, :] = kh[0:32]
        v_s[at : at + 32, :] = vh[0:32]
    kc_s[...] = kh[32:HALO]
    vc_s[...] = vh[32:HALO]
    dk_s[...] = jnp.zeros_like(dk_s)
    dv_s[...] = jnp.zeros_like(dv_s)
    dkc_s[...] = jnp.zeros_like(dkc_s)
    dvc_s[...] = jnp.zeros_like(dvc_s)
    cot = cot_ref[...].astype(BF16)
    do_s[...] = nt(cot, wo_ref[...]).astype(BF16)

    key, query = iota((192, 256), 0), iota((192, 256), 1) % 128
    drow = key // 32 - 1 - query // 32
    dcol = key % 32 - query % 32
    mask_s[...] = jnp.where((jnp.abs(drow) <= 1) & (jnp.abs(dcol) <= 1), 1.0, 0.0)

    tiles = points // 128

    def tile_step(t, carry):
        base = pl.multiple_of(t * 128, 128)
        key = iota((192, 256), 0)
        first = jnp.where(upper & (t == 0), 32, 0)
        last = jnp.where(jnp.logical_not(upper) & (t == tiles - 1), 160, 192)
        mask1 = (mask_s[...] > 0.5) & (key >= first) & (key < last)
        e, query = iota((HALO - 32, 256), 0), iota((HALO - 32, 256), 1) % 128
        corner = e >= 64
        key_row = jnp.where(corner, jnp.where(upper, 32, -1), e % 32)
        is_left = (e < 32) | (e == 64)
        near = jnp.abs(key_row - (4 * t + query // 32)) <= 1
        side = query % 32 == jnp.where(is_left, 0, 31)
        mask2 = near & side & (e < 66)
        lane = iota((128, 128), 1)
        even = lane < 64
        for pair in range(HEADS // 2):
            lanes = slice(pair * 128, pair * 128 + 128)
            win = pl.ds(base, 192)
            here = pl.ds(base, 128)
            q = q_s[here, lanes]
            do = do_s[here, lanes]
            zero = jnp.zeros_like(q)
            qm = jnp.concatenate([jnp.where(even, q, zero), jnp.where(even, zero, q)], 0)
            dom = jnp.concatenate([jnp.where(even, do, zero), jnp.where(even, zero, do)], 0)
            k1, v1 = k_s[win, lanes], v_s[win, lanes]
            k2, v2 = kc_s[:, lanes], vc_s[:, lanes]
            w1 = jnp.where(mask1, jnp.exp(nt(k1, qm)), 0.0)
            w2 = jnp.where(mask2, jnp.exp(nt(k2, qm)), 0.0)
            total = jnp.sum(w1, axis=0, keepdims=True) + jnp.sum(w2, axis=0, keepdims=True)
            inverse = 1.0 / total
            p1, p2 = w1 * inverse, w2 * inverse
            dp1, dp2 = nt(v1, dom), nt(v2, dom)
            delta = jnp.sum(p1 * dp1, axis=0, keepdims=True) + jnp.sum(
                p2 * dp2, axis=0, keepdims=True
            )
            ds1, ds2 = (p1 * (dp1 - delta)).astype(BF16), (p2 * (dp2 - delta)).astype(BF16)
            p1, p2 = p1.astype(BF16), p2.astype(BF16)
            out = tn(p1, v1) + tn(p2, v2)
            mixed_s[here, lanes] = jnp.where(even, out[0:128], out[128:256]).astype(BF16)
            dq = (tn(ds1, k1) + tn(ds2, k2)) * scale
            dq_ref[here, lanes] = jnp.where(even, dq[0:128], dq[128:256]).astype(BF16)
            dk_s[win, lanes] += nn(ds1, qm)
            dv_s[win, lanes] += nn(p1, dom)
            dkc_s[:, lanes] += nn(ds2, qm)
            dvc_s[:, lanes] += nn(p2, dom)
        return carry

    lax.fori_loop(0, tiles, tile_step, 0)

    row_at = pl.multiple_of(jnp.where(upper, 32 + points, 0), 32)
    dkh = jnp.concatenate([dk_s[pl.ds(row_at, 32), :], dkc_s[...]], 0).astype(BF16)
    dvh = jnp.concatenate([dv_s[pl.ds(row_at, 32), :], dvc_s[...]], 0).astype(BF16)
    dkh_ref[...] = dkh
    dvh_ref[...] = dvh
    dk_ref[...] = dk_s[32 : 32 + points, :].astype(BF16)
    dv_ref[...] = dv_s[32 : 32 + points, :].astype(BF16)
    wk, wv = (w_ref[:, i * width : (i + 1) * width] for i in (1, 2))
    back = (nt(dkh, wk) + nt(dvh, wv)).astype(BF16)
    brow_ref[...] = back[0:32]
    for ref, at in ((bleft_ref, 32), (bright_ref, 64)):
        ref[0:32, :] = back[at : at + 32]
        ref[32:48, :] = back[CORNER:HALO]
    wq, wk, wv = (w_all[1, :, i * width : (i + 1) * width] for i in range(3))
    dw_ref[0:width, :] = tn(dq_ref[...], normal).astype(BF16)
    dw_ref[width : 2 * width, :] = (tn(dk_ref[...], normal) + tn(dkh_ref[...], halo)).astype(BF16)
    dw_ref[2 * width : 3 * width, :] = (
        tn(dv_ref[...], normal) + tn(dvh_ref[...], halo)
    ).astype(BF16)
    dw_ref[3 * width : 4 * width, :] = tn(mixed_s[...], cot).astype(BF16)
    dn_ref[...] = nt(dq_ref[...], wq) + nt(dk_ref[...], wk) + nt(dv_ref[...], wv)


def third_kernel(
    first, lat_ref, n0, n1, n2, n3, n4, n5, q_ref, kv_ref, p_ref, mixed_ref, h_ref, dn1_ref, cot_ref,
    packs_ref, wt_ref, wo_ref, gain_ref, dw_in,
    dh_ref, d0, d1, d2, d3, d4, d5, dw_ref,
    dw_s, dmix_s, dkv_s, dq_s, dp_s,
):
    width, tile = q_ref.shape
    head = width // HEADS
    scale = head**-0.5
    blocks = (n0, n1, n2, n3, n4, n5)
    outs = (d0, d1, d2, d3, d4, d5)
    step = pl.program_id(0)

    @pl.when(step == 0)
    def _():
        dw_s[...] = jnp.zeros_like(dw_s) if dw_in is None else dw_in[...]

    brow = jnp.where(lat_ref[0] == 0, 31, 0)
    shape = (tile, RETURNED)
    token = first + step * tile + iota(shape, 0)
    r, c, slot = token // 32, token % 32, iota(shape, 1)
    border = r == brow
    place = one_hot(
        (border & (slot < 32) & (slot == c))
        | ((c == 0) & (slot < 64) & (slot == 32 + r))
        | ((c == 31) & (slot < 112) & (slot == 80 + r))
        | (border & (c == 0) & (slot == 128 + 33))
        | (border & (c == 31) & (slot == 176 + 32))
    )
    dn = dn1_ref[...] + nn(place, packs_ref[...])
    dh = cot_ref[...] + norm_back(h_ref[...].astype(F32), gain_ref[1:2, :], dn)
    dh_ref[...] = dh
    dhb = dh.astype(BF16)
    dmix_s[...] = nt(wo_ref[...], dhb)
    dw_s[3 * width : 4 * width, :] += nn(mixed_ref[...], dhb)
    for h in range(HEADS):
        lo, hi = h * head, (h + 1) * head
        dmix = dmix_s[lo:hi, :]
        delta = jnp.zeros((1, tile), F32)
        for b in range(len(blocks)):
            dp = jnp.sum(
                dmix * kv_ref[b, width + lo : width + hi, :].astype(F32), axis=0, keepdims=True
            )
            dp_s[b : b + 1, :] = dp
            delta = delta + p_ref[b, h : h + 1, :] * dp
        q = q_ref[lo:hi, :].astype(F32)
        dq = jnp.zeros((head, tile), F32)
        for b in range(len(blocks)):
            p = p_ref[b, h : h + 1, :]
            ds = p * (dp_s[b : b + 1, :] - delta) * scale
            dq = dq + ds * kv_ref[b, lo:hi, :].astype(F32)
            dkv_s[b, lo:hi, :] = (ds * q).astype(BF16)
            dkv_s[b, width + lo : width + hi, :] = (p * dmix).astype(BF16)
        dq_s[lo:hi, :] = dq.astype(BF16)
    dq = dq_s[...]
    dw_s[0:width, :] += nn(dq, n0[...])
    for b, (ref, out) in enumerate(zip(blocks, outs)):
        dkv = dkv_s[b]
        grad = tn(dkv, wt_ref[width : 3 * width])
        if b == 0:
            grad = grad + tn(dq, wt_ref[0:width])
        out[...] = grad.astype(out.dtype)
        dw_s[width : 3 * width, :] += nn(dkv, ref[...])

    @pl.when(step == pl.num_programs(0) - 1)
    def _():
        dw_ref[...] = dw_s[...].astype(dw_ref.dtype)


def last_kernel(
    first, start_ref, vis_ref, gain_ref, dh_ref, own_ref, far_ref, near_ref, prev_ref, out_ref
):
    tile, width = start_ref.shape
    shown = shown_column(vis_ref[...], first + pl.program_id(0) * tile, tile)
    dn = own_ref[...] + far_ref[...].astype(F32) + near_ref[...].astype(F32)
    grad = dh_ref[...] + norm_back(start_ref[...].astype(F32), gain_ref[0:1, :], dn)
    out_ref[...] = jnp.where(shown > 0.5, grad, 0.0)


def weights_kernel(
    factor, pieces, lat_ref, mine_ref, other_ref, wt_ref, gain_ref,
    qkv_ref, out_ref, gain_out_ref, rows_s,
):
    total, width = mine_ref.shape
    piece = total // pieces // 2
    lat = lat_ref[0]
    for ref, band in ((mine_ref, lat), (other_ref, 1 - lat)):
        for k in range(pieces):
            at = pl.multiple_of(band * (total // 2) + k * piece, 8)
            for layer in range(2):
                lo = (2 * k + layer) * piece
                rows_s[layer, pl.ds(at, piece), :] = ref[lo : lo + piece, :].astype(F32) * factor
    for layer in range(2):
        acc = jnp.zeros((1, width), F32)
        for i in range(3):
            lo, hi = i * width, (i + 1) * width
            grad = rows_s[layer, lo:hi, :]
            weight = wt_ref[layer, lo:hi, :].astype(F32)
            acc = acc + jnp.sum(weight * grad, axis=0, keepdims=True)
            qkv_ref[layer, :, lo:hi] = grad.T
        out_ref[layer] = rows_s[layer, 3 * width : 4 * width, :]
        gain_out_ref[layer : layer + 1, :] = acc / gain_ref[layer : layer + 1, :]


def call(
    kernel, out_shape, scratch=(), grid=None, in_specs=None, out_specs=None, us=1, aliases=None
):
    return pl.pallas_call(
        kernel,
        out_shape=out_shape,
        grid_spec=pltpu.PrefetchScalarGridSpec(
            num_scalar_prefetch=0,
            grid=grid or (),
            in_specs=in_specs,
            out_specs=out_specs,
            scratch_shapes=list(scratch),
        ),
        input_output_aliases=aliases or {},
        cost_estimate=pl.CostEstimate(
            flops=int(us * 1e6 * 800), bytes_accessed=int(us * 1e6), transcendentals=0
        ),
        compiler_params=pltpu.CompilerParams(vmem_limit_bytes=VMEM_BYTES),
    )


def whole():
    return pl.BlockSpec(memory_space=pltpu.VMEM)


def scalar():
    return pl.BlockSpec(memory_space=pltpu.SMEM)


def fixed(shape):
    return pl.BlockSpec(shape, lambda i: (0,) * len(shape))


def token_spec(tile, width, first=0):
    at = first // tile
    return pl.BlockSpec((tile, width), lambda i: (i + at, 0))


def layer_spec(layer, rows, width):
    return pl.BlockSpec((None, rows, width), lambda i: (layer, 0, 0))


CHUNKS = 2


def local(
    tokens, visible, mask_token, norm_gain_table, query_key_value_weight, output_weight, cotangent
):
    rows, cols, width = tokens.shape
    points = rows * cols
    size = points // CHUNKS
    firsts = [c * size for c in range(CHUNKS)]
    lat_count, lon_count = lax.axis_size("lat"), lax.axis_size("lon")
    lat = lax.axis_index("lat").astype(jnp.int32).reshape(1)
    wt = jnp.swapaxes(query_key_value_weight, 1, 2)
    struct = jax.ShapeDtypeStruct
    tokens = tokens.reshape(points, width)
    cot = cotangent.reshape(points, width)
    part = struct((size, width), BF16)
    gain_spec = fixed((2, width))
    wt_spec, wo_spec = layer_spec(0, 3 * width, width), layer_spec(0, width, width)

    small = 256
    starts, normals = [], []
    for first in firsts:
        start, normal = call(
            functools.partial(start_kernel, first),
            (part, part),
            grid=(size // small,),
            in_specs=[
                token_spec(small, width, first),
                fixed((rows, cols)),
                fixed((width,)),
                gain_spec,
            ],
            out_specs=(token_spec(small, width),) * 2,
            us=2,
        )(tokens, visible, mask_token, norm_gain_table)
        starts.append(start)
        normals.append(normal)

    swapped0 = lon_swap(normals[0])
    own1, swapped0 = chained(normals[1], swapped0)
    swapped1 = lon_swap(own1)
    beyond0, beyond1 = lon_forward(swapped0), lon_forward(swapped1)
    near0, near1 = lat_swap(normals[0]), lat_swap(own1)

    def blocks_of(own, near, swapped, beyond):
        return [own, near, swapped, beyond, lat_swap(swapped), lat_swap(beyond)]

    blocks = [blocks_of(normals[0], near0, swapped0, beyond0), None]

    tile = 256
    steps = size // tile
    tok_spec = token_spec(tile, width)
    feat_spec = pl.BlockSpec((width, tile), lambda i: (0, i))
    kv_spec = pl.BlockSpec((6, 2 * width, tile), lambda i: (0, 0, i))
    p_spec = pl.BlockSpec((6, 8, tile), lambda i: (0, 0, i))
    packs = []
    kept = []
    for c in range(CHUNKS):
        kernel = functools.partial(first_kernel, firsts[c])
        *keep, normal1, row, left, right = call(
            kernel if packs else functools.partial(without, kernel, 8, 3),
            (
                struct((width, size), BF16),
                struct((6, 2 * width, size), BF16),
                struct((6, 8, size), F32),
                struct((width, size), BF16),
                part,
                part,
                *[struct((32, width), BF16)] * 3,
            ),
            grid=(steps,),
            in_specs=[scalar()]
            + [tok_spec] * 7
            + [fixed((32, width))] * len(packs)
            + [wt_spec, wo_spec, gain_spec],
            out_specs=(
                feat_spec, kv_spec, p_spec, feat_spec, tok_spec, tok_spec,
                *[fixed((32, width))] * 3,
            ),
            scratch=[pltpu.VMEM((6, 8, tile), F32), pltpu.VMEM((96, width), F32)],
            us=8,
        )(lat, *blocks[c], starts[c], *packs, wt, output_weight, norm_gain_table)
        packs = [row, left, right]
        kept.append((keep, normal1))
        if c == 0:
            beyond1, row, left, right = lax.optimization_barrier((beyond1, *packs))
            packs = [row, left, right]
            blocks[1] = blocks_of(own1, near1, swapped1, beyond1)

    row, left, right = packs
    from_l, from_r = from_left(right), from_right(left)
    ext = points + 64
    halo_cols = HALO - 32
    every, halo_struct = pltpu.VMEM((points, width), BF16), pltpu.VMEM((HALO, width), BF16)
    dn1, dw1, brow, bleft, bright = call(
        second_kernel,
        (
            struct((points, width), F32),
            struct((4 * width, width), BF16),
            struct((32, width), BF16),
            struct((48, width), BF16),
            struct((48, width), BF16),
        ),
        in_specs=[scalar()] + [whole()] * 10,
        out_specs=(whole(),) * 5,
        scratch=[
            *[every] * 4,
            *[halo_struct] * 3,
            pltpu.VMEM((points, width), BF16),
            pltpu.VMEM((ext, width), BF16),
            pltpu.VMEM((ext, width), BF16),
            pltpu.VMEM((halo_cols, width), BF16),
            pltpu.VMEM((halo_cols, width), BF16),
            pltpu.VMEM((ext, width), F32),
            pltpu.VMEM((ext, width), F32),
            pltpu.VMEM((halo_cols, width), F32),
            pltpu.VMEM((halo_cols, width), F32),
            pltpu.VMEM((points, width), BF16),
            pltpu.VMEM((192, 256), F32),
            pltpu.VMEM((points, width), BF16),
        ],
        us=22,
    )(
        lat, kept[0][1], kept[1][1], lat_swap(row), from_l, from_r, lat_swap(from_l),
        lat_swap(from_r), query_key_value_weight, output_weight, cot,
    )

    from_l, from_r, brow = from_left(bright), from_right(bleft), lat_swap(brow)
    packs = jnp.concatenate(
        [brow, from_l, from_r, lat_swap(from_l), lat_swap(from_r)], 0
    )
    stages = lon_factors()
    sum1 = halves_summed(dw1)
    packs, sum1 = chained(packs, sum1)

    def plus(a, b):
        return (a.astype(F32) + b.astype(F32)).astype(BF16)

    weights = None
    backs = []
    for c in range(CHUNKS):
        q0, kv0, p0, mixed0, h1 = kept[c][0]
        final = c == CHUNKS - 1
        kernel = functools.partial(third_kernel, firsts[c])
        extra = [] if weights is None else [weights]
        if weights is None:
            kernel = functools.partial(without, kernel, 18, 1)
        dh1, d0, d1, d2, d3, d4, d5, weights = call(
            kernel,
            (
                struct((size, width), F32),
                struct((size, width), F32),
                *[part] * 5,
                struct((4 * width, width), BF16 if final else F32),
            ),
            grid=(steps,),
            in_specs=[scalar()]
            + [tok_spec] * 6
            + [feat_spec, kv_spec, p_spec, feat_spec, tok_spec]
            + [token_spec(tile, width, firsts[c])] * 2
            + [fixed((RETURNED, width)), wt_spec, wo_spec, gain_spec]
            + [fixed((4 * width, width))] * len(extra),
            out_specs=(*[tok_spec] * 7, fixed((4 * width, width))),
            scratch=[
                pltpu.VMEM((4 * width, width), F32),
                pltpu.VMEM((width, tile), F32),
                pltpu.VMEM((6, 2 * width, tile), BF16),
                pltpu.VMEM((width, tile), BF16),
                pltpu.VMEM((8, tile), F32),
            ],
            us=13,
        )(
            lat, *blocks[c], q0, kv0, p0, mixed0, h1, dn1, cot, packs, wt, output_weight,
            norm_gain_table, *extra,
        )
        d3 = plus(d3, lat_swap(d5))
        d2 = plus(d2, lat_swap(d4))
        d1 = lat_swap(d1)
        if c == 0:
            sum1 = stage_summed(sum1, stages[0])
            weights, sum1, d1, d2, d3 = lax.optimization_barrier((weights, sum1, d1, d2, d3))
            for stage in stages[1:]:
                sum1 = stage_summed(sum1, stage)
            d2 = plus(d2, lon_backward(d3))
        backs.append((dh1, d0, d1, d2, d3))

    d2_0, (d1_1, d2_1, d3_1) = backs[0][3], backs[1][2:]
    sum0 = halves_summed(weights)
    sum0, sum1, d2_0, d1_1, d2_1, d3_1 = lax.optimization_barrier(
        (sum0, sum1, d2_0, d1_1, d2_1, d3_1)
    )
    back_1 = lon_backward(d3_1)
    sum0 = stage_summed(sum0, stages[0])
    sum0, d2_0, back_1 = lax.optimization_barrier((sum0, d2_0, back_1))
    far_0 = lon_swap(d2_0)
    d2_1 = plus(d2_1, back_1)
    for stage in stages[1:]:
        sum0 = stage_summed(sum0, stage)
    sum0, d2_1, far_0 = lax.optimization_barrier((sum0, d2_1, far_0))
    far_1 = lon_swap(d2_1)
    sums = jnp.concatenate([sum0, sum1], 0)
    for stage in stages[:0:-1]:
        sums = spread(sums, *stage)
    sums, far_1 = chained(sums, far_1)
    sums = spread(sums, *stages[0])
    other = lat_swap(sums)
    ends = [(*backs[0][:3], far_0), (*backs[1][:2], d1_1, far_1)]

    grad_tokens = None
    for c in range(CHUNKS):
        dh1, d0, near, far = ends[c]
        extra = [] if grad_tokens is None else [grad_tokens]
        kernel = functools.partial(last_kernel, firsts[c])
        grad_tokens = call(
            kernel if extra else functools.partial(without, kernel, 7, 1),
            struct((points, width), F32),
            grid=(size // small,),
            in_specs=[token_spec(small, width), fixed((rows, cols)), gain_spec]
            + [token_spec(small, width)] * 4
            + [pl.BlockSpec(memory_space=pl.ANY)] * len(extra),
            out_specs=token_spec(small, width, firsts[c]),
            aliases={7: 0} if extra else {},
            us=4,
        )(starts[c], visible, norm_gain_table, dh1, d0, far, near, *extra)

    factor = (points * lat_count * lon_count) ** (-0.5)
    g_qkv, g_out, g_gain = call(
        functools.partial(weights_kernel, factor, lon_count),
        (
            struct((2, width, 3 * width), F32),
            struct((2, width, width), F32),
            struct((2, width), F32),
        ),
        in_specs=[scalar()] + [whole()] * 4,
        out_specs=(whole(),) * 3,
        scratch=[pltpu.VMEM((2, 4 * width, width), F32)],
        us=5,
    )(lat, sums, other, wt, norm_gain_table)
    return grad_tokens.reshape(rows, cols, width), g_qkv, g_out, g_gain


def without(kernel, at, count, *refs):
    kernel(*refs[:at], *[None] * count, *refs[at:])


def solution(mesh):
    return jax.shard_map(
        local,
        mesh=mesh,
        in_specs=(
            P(("group", "lat"), "lon", None),
            P(("group", "lat"), "lon"),
            P(),
            P(),
            P(),
            P(),
            P(("group", "lat"), "lon", None),
        ),
        out_specs=(
            P(("group", "lat"), "lon", None),
            P("group", None, None),
            P("group", None, None),
            P("group", None),
        ),
        check_vma=False,
    )
```

```python
import functools

import jax
import jax.numpy as jnp
from jax import lax
from jax.experimental import pallas as pl
from jax.experimental.pallas import tpu as pltpu
from jax.sharding import PartitionSpec as P

HEADS = 6
EPS = 1e-05
F32 = jnp.float32
BF16 = jnp.bfloat16
VMEM_BYTES = 26 * 1024 * 1024
HALO = 112
CORNER = 96
RETURNED = 224


def nn(a, b):
    return lax.dot_general(a, b, (((1,), (0,)), ((), ())), preferred_element_type=F32)


def nt(a, b):
    return lax.dot_general(a, b, (((1,), (1,)), ((), ())), preferred_element_type=F32)


def tn(a, b):
    return lax.dot_general(a, b, (((0,), (0,)), ((), ())), preferred_element_type=F32)


def iota(shape, dim):
    return lax.broadcasted_iota(jnp.int32, shape, dim)


def one_hot(condition):
    return jnp.where(condition, 1.0, 0.0).astype(BF16)


def permuted(value, axis, target):
    count = lax.axis_size(axis)
    return lax.ppermute(value, axis, [(i, target(i) % count) for i in range(count)])


def lat_swap(value):
    return permuted(value, "lat", lambda i: i ^ 1)


def lon_swap(value):
    return permuted(value, "lon", lambda i: i ^ 1)


def lon_forward(value):
    return permuted(value, "lon", lambda i: i + 2 if i % 2 == 0 else i - 2)


def lon_backward(value):
    return permuted(value, "lon", lambda i: i - 2 if i % 2 == 0 else i + 2)


def from_left(value):
    return permuted(value, "lon", lambda i: i + 1)


def from_right(value):
    return permuted(value, "lon", lambda i: i - 1)


def chained(value, after):
    return lax.optimization_barrier((value, after))


def exchanged(parts, axis_stride, factor):
    count = lax.axis_size("lon")
    digit = (lax.axis_index("lon") // axis_stride) % factor
    moved = []
    for d in range(1, factor):
        pairs = [(i, shifted(i, axis_stride, factor, d)) for i in range(count)]
        moved.append(lax.ppermute(parts(digit ^ d), "lon", pairs))
    total = parts(digit).astype(F32)
    for piece in moved:
        total = total + piece.astype(F32)
    return total.astype(BF16)


def shifted(i, stride, factor, d):
    digit = (i // stride) % factor
    return i + ((digit ^ d) - digit) * stride


def spread(value, axis_stride, factor):
    count = lax.axis_size("lon")
    digit = (lax.axis_index("lon") // axis_stride) % factor
    rows = value.shape[0]
    full = jnp.zeros((factor * rows,) + value.shape[1:], value.dtype)
    full = lax.dynamic_update_slice(full, value, (digit * rows, 0))
    for d in range(1, factor):
        pairs = [(i, shifted(i, axis_stride, factor, d)) for i in range(count)]
        got = lax.ppermute(value, "lon", pairs)
        at = (digit ^ d) * rows
        full = lax.dynamic_update_slice(full, got, (at, 0))
    return full


def lon_factors():
    left = lax.axis_size("lon")
    stride, out = 1, []
    for factor in [2] + [4] * 10:
        if left == 1:
            break
        factor = min(factor, left)
        out.append((stride, factor))
        stride, left = stride * factor, left // factor
    return out


def halves_summed(value):
    lat = lax.axis_index("lat")
    half = value.shape[0] // 2
    mine = lax.dynamic_slice_in_dim(value, lat * half, half, 0)
    other = lat_swap(lax.dynamic_slice_in_dim(value, (1 - lat) * half, half, 0))
    return (mine.astype(F32) + other.astype(F32)).astype(BF16)


def stage_summed(value, stage):
    stride, factor = stage
    size = value.shape[0] // factor
    return exchanged(
        lambda k: lax.dynamic_slice_in_dim(value, k * size, size, 0), stride, factor
    )


def norm_parts(x):
    mean = jnp.mean(x, axis=-1, keepdims=True)
    centred = x - mean
    spread = jnp.mean(centred * centred, axis=-1, keepdims=True)
    rstd = lax.rsqrt(spread + EPS)
    return centred * rstd, rstd


def norm_back(x, gain, grad_normal):
    xhat, rstd = norm_parts(x)
    g = grad_normal * gain
    return rstd * (
        g - jnp.mean(g, axis=-1, keepdims=True) - xhat * jnp.mean(g * xhat, axis=-1, keepdims=True)
    )


def shown_column(visible, base, tile):
    rows, cols = visible.shape
    token = base + iota((tile, rows), 0)
    of_row = nn(one_hot(token // cols == iota((tile, rows), 1)), visible.astype(F32).astype(BF16))
    token = base + iota((tile, cols), 0)
    mine = token % cols == iota((tile, cols), 1)
    return jnp.sum(jnp.where(mine, of_row, 0.0), axis=1, keepdims=True)


def start_kernel(first, tok_ref, vis_ref, mask_ref, gain_ref, start_ref, normal_ref):
    tile, width = tok_ref.shape
    base = first + pl.program_id(0) * tile
    shown = shown_column(vis_ref[...], base, tile)
    x = jnp.where(shown > 0.5, tok_ref[...].astype(F32), mask_ref[...].astype(F32).reshape(1, width))
    start_ref[...] = x.astype(BF16)
    xhat, _ = norm_parts(x)
    normal_ref[...] = (xhat * gain_ref[0:1, :]).astype(BF16)


def first_kernel(
    first, lat_ref, n0, n1, n2, n3, n4, n5, start_ref, row_in, left_in, right_in,
    wt_ref, wo_ref, gain_ref,
    q_ref, kv_ref, p_ref, mixed_ref, h_ref, normal_ref, row_ref, left_ref, right_ref,
    w_s, pack_s,
):
    width, tile = q_ref.shape
    head = width // HEADS
    blocks = (n0, n1, n2, n3, n4, n5)
    q_ref[...] = nt(wt_ref[0:width], n0[...]).astype(BF16)
    for b, ref in enumerate(blocks):
        kv_ref[b] = nt(wt_ref[width : 3 * width], ref[...]).astype(BF16)
    for h in range(HEADS):
        lo, hi = h * head, (h + 1) * head
        q = q_ref[lo:hi, :].astype(F32) * (head**-0.5)
        total = jnp.zeros((1, tile), F32)
        out = jnp.zeros((head, tile), F32)
        for b in range(len(blocks)):
            k = kv_ref[b, lo:hi, :].astype(F32)
            w = jnp.exp(jnp.sum(q * k, axis=0, keepdims=True))
            w_s[b, h : h + 1, :] = w
            total = total + w
            out = out + w * kv_ref[b, width + lo : width + hi, :].astype(F32)
        inverse = 1.0 / total
        for b in range(len(blocks)):
            p_ref[b, h : h + 1, :] = w_s[b, h : h + 1, :] * inverse
        mixed_ref[lo:hi, :] = (out * inverse).astype(BF16)
    h1 = start_ref[...].astype(F32) + tn(mixed_ref[...], wo_ref[...])
    h1 = h1.astype(BF16)
    h_ref[...] = h1
    xhat, _ = norm_parts(h1.astype(F32))
    normal = (xhat * gain_ref[1:2, :]).astype(BF16)
    normal_ref[...] = normal
    step = pl.program_id(0)
    brow = jnp.where(lat_ref[0] == 0, 31, 0)
    slot = iota((96, tile), 0)
    token = first + step * tile + iota((96, tile), 1)
    r, c = token // 32, token % 32
    pick = one_hot(
        ((slot < 32) & (r == brow) & (c == slot))
        | ((slot >= 32) & (slot < 64) & (c == 0) & (r == slot - 32))
        | ((slot >= 64) & (c == 31) & (r == slot - 64))
    )

    @pl.when(step == 0)
    def _():
        for i, ref in enumerate((row_in, left_in, right_in)):
            known = jnp.zeros((32, width), F32) if ref is None else ref[...].astype(F32)
            pack_s[i * 32 : i * 32 + 32, :] = known

    pack_s[...] += nn(pick, normal)

    @pl.when(step == pl.num_programs(0) - 1)
    def _():
        for i, ref in enumerate((row_ref, left_ref, right_ref)):
            ref[...] = pack_s[i * 32 : i * 32 + 32, :].astype(BF16)


def second_kernel(
    lat_ref, na_ref, nb_ref, row_ref, left_ref, right_ref, dleft_ref, dright_ref,
    w_all, wo_all, cot_ref,
    dn_ref, dw_ref, brow_ref, bleft_ref, bright_ref,
    dq_ref, dk_ref, dv_ref, mixed_s, dkh_ref, dvh_ref, halo_s,
    q_s, k_s, v_s, kc_s, vc_s, dk_s, dv_s, dkc_s, dvc_s, do_s, mask_s, normal_s,
):
    points, width = cot_ref.shape
    head = width // HEADS
    w_ref, wo_ref = w_all.at[1], wo_all.at[1]
    upper = lat_ref[0] == 0
    halo_s[0:32, :] = row_ref[...]
    halo_s[32:64, :] = left_ref[...]
    halo_s[64:96, :] = right_ref[...]
    a, b = iota((16, 32), 0), iota((16, 32), 1)
    sent = b == jnp.where(upper, 0, 31)
    corners = nn(one_hot(sent & (a == 0)), dleft_ref[...])
    corners += nn(one_hot(sent & (a == 1)), dright_ref[...])
    halo_s[CORNER:HALO, :] = corners.astype(BF16)
    halo = halo_s[...]
    normal_s[0 : points // 2, :] = na_ref[...]
    normal_s[points // 2 : points, :] = nb_ref[...]
    normal = normal_s[...]
    scale = head**-0.5
    q_s[...] = (nn(normal, w_ref[:, 0:width]).astype(BF16).astype(F32) * scale).astype(BF16)
    k_s[32 : 32 + points, :] = nn(normal, w_ref[:, width : 2 * width]).astype(BF16)
    v_s[32 : 32 + points, :] = nn(normal, w_ref[:, 2 * width : 3 * width]).astype(BF16)
    kh = nn(halo, w_ref[:, width : 2 * width]).astype(BF16)
    vh = nn(halo, w_ref[:, 2 * width : 3 * width]).astype(BF16)
    for at in (0, 32 + points):
        k_s[at : at + 32, :] = kh[0:32]
        v_s[at : at + 32, :] = vh[0:32]
    kc_s[...] = kh[32:HALO]
    vc_s[...] = vh[32:HALO]
    dk_s[...] = jnp.zeros_like(dk_s)
    dv_s[...] = jnp.zeros_like(dv_s)
    dkc_s[...] = jnp.zeros_like(dkc_s)
    dvc_s[...] = jnp.zeros_like(dvc_s)
    cot = cot_ref[...].astype(BF16)
    do_s[...] = nt(cot, wo_ref[...]).astype(BF16)

    key, query = iota((192, 256), 0), iota((192, 256), 1) % 128
    drow = key // 32 - 1 - query // 32
    dcol = key % 32 - query % 32
    mask_s[...] = jnp.where((jnp.abs(drow) <= 1) & (jnp.abs(dcol) <= 1), 1.0, 0.0)

    tiles = points // 128

    def tile_step(t, carry):
        base = pl.multiple_of(t * 128, 128)
        key = iota((192, 256), 0)
        first = jnp.where(upper & (t == 0), 32, 0)
        last = jnp.where(jnp.logical_not(upper) & (t == tiles - 1), 160, 192)
        mask1 = (mask_s[...] > 0.5) & (key >= first) & (key < last)
        e, query = iota((HALO - 32, 256), 0), iota((HALO - 32, 256), 1) % 128
        corner = e >= 64
        key_row = jnp.where(corner, jnp.where(upper, 32, -1), e % 32)
        is_left = (e < 32) | (e == 64)
        near = jnp.abs(key_row - (4 * t + query // 32)) <= 1
        side = query % 32 == jnp.where(is_left, 0, 31)
        mask2 = near & side & (e < 66)
        lane = iota((128, 128), 1)
        even = lane < 64
        for pair in range(HEADS // 2):
            lanes = slice(pair * 128, pair * 128 + 128)
            win = pl.ds(base, 192)
            here = pl.ds(base, 128)
            q = q_s[here, lanes]
            do = do_s[here, lanes]
            zero = jnp.zeros_like(q)
            qm = jnp.concatenate([jnp.where(even, q, zero), jnp.where(even, zero, q)], 0)
            dom = jnp.concatenate([jnp.where(even, do, zero), jnp.where(even, zero, do)], 0)
            k1, v1 = k_s[win, lanes], v_s[win, lanes]
            k2, v2 = kc_s[:, lanes], vc_s[:, lanes]
            w1 = jnp.where(mask1, jnp.exp(nt(k1, qm)), 0.0)
            w2 = jnp.where(mask2, jnp.exp(nt(k2, qm)), 0.0)
            total = jnp.sum(w1, axis=0, keepdims=True) + jnp.sum(w2, axis=0, keepdims=True)
            inverse = 1.0 / total
            p1, p2 = w1 * inverse, w2 * inverse
            dp1, dp2 = nt(v1, dom), nt(v2, dom)
            delta = jnp.sum(p1 * dp1, axis=0, keepdims=True) + jnp.sum(
                p2 * dp2, axis=0, keepdims=True
            )
            ds1, ds2 = (p1 * (dp1 - delta)).astype(BF16), (p2 * (dp2 - delta)).astype(BF16)
            p1, p2 = p1.astype(BF16), p2.astype(BF16)
            out = tn(p1, v1) + tn(p2, v2)
            mixed_s[here, lanes] = jnp.where(even, out[0:128], out[128:256]).astype(BF16)
            dq = (tn(ds1, k1) + tn(ds2, k2)) * scale
            dq_ref[here, lanes] = jnp.where(even, dq[0:128], dq[128:256]).astype(BF16)
            dk_s[win, lanes] += nn(ds1, qm)
            dv_s[win, lanes] += nn(p1, dom)
            dkc_s[:, lanes] += nn(ds2, qm)
            dvc_s[:, lanes] += nn(p2, dom)
        return carry

    lax.fori_loop(0, tiles, tile_step, 0)

    row_at = pl.multiple_of(jnp.where(upper, 32 + points, 0), 32)
    dkh = jnp.concatenate([dk_s[pl.ds(row_at, 32), :], dkc_s[...]], 0).astype(BF16)
    dvh = jnp.concatenate([dv_s[pl.ds(row_at, 32), :], dvc_s[...]], 0).astype(BF16)
    dkh_ref[...] = dkh
    dvh_ref[...] = dvh
    dk_ref[...] = dk_s[32 : 32 + points, :].astype(BF16)
    dv_ref[...] = dv_s[32 : 32 + points, :].astype(BF16)
    wk, wv = (w_ref[:, i * width : (i + 1) * width] for i in (1, 2))
    back = (nt(dkh, wk) + nt(dvh, wv)).astype(BF16)
    brow_ref[...] = back[0:32]
    for ref, at in ((bleft_ref, 32), (bright_ref, 64)):
        ref[0:32, :] = back[at : at + 32]
        ref[32:48, :] = back[CORNER:HALO]
    wq, wk, wv = (w_all[1, :, i * width : (i + 1) * width] for i in range(3))
    dw_ref[0:width, :] = tn(dq_ref[...], normal).astype(BF16)
    dw_ref[width : 2 * width, :] = (tn(dk_ref[...], normal) + tn(dkh_ref[...], halo)).astype(BF16)
    dw_ref[2 * width : 3 * width, :] = (
        tn(dv_ref[...], normal) + tn(dvh_ref[...], halo)
    ).astype(BF16)
    dw_ref[3 * width : 4 * width, :] = tn(mixed_s[...], cot).astype(BF16)
    dn_ref[...] = nt(dq_ref[...], wq) + nt(dk_ref[...], wk) + nt(dv_ref[...], wv)


def third_kernel(
    first, lat_ref, n0, n1, n2, n3, n4, n5, q_ref, kv_ref, p_ref, mixed_ref, h_ref, dn1_ref, cot_ref,
    packs_ref, wt_ref, wo_ref, gain_ref, dw_in,
    dh_ref, d0, d1, d2, d3, d4, d5, dw_ref,
    dw_s, dmix_s, dkv_s, dq_s, dp_s,
):
    width, tile = q_ref.shape
    head = width // HEADS
    scale = head**-0.5
    blocks = (n0, n1, n2, n3, n4, n5)
    outs = (d0, d1, d2, d3, d4, d5)
    step = pl.program_id(0)

    @pl.when(step == 0)
    def _():
        dw_s[...] = jnp.zeros_like(dw_s) if dw_in is None else dw_in[...]

    brow = jnp.where(lat_ref[0] == 0, 31, 0)
    shape = (tile, RETURNED)
    token = first + step * tile + iota(shape, 0)
    r, c, slot = token // 32, token % 32, iota(shape, 1)
    border = r == brow
    place = one_hot(
        (border & (slot < 32) & (slot == c))
        | ((c == 0) & (slot < 64) & (slot == 32 + r))
        | ((c == 31) & (slot < 112) & (slot == 80 + r))
        | (border & (c == 0) & (slot == 128 + 33))
        | (border & (c == 31) & (slot == 176 + 32))
    )
    dn = dn1_ref[...] + nn(place, packs_ref[...])
    dh = cot_ref[...] + norm_back(h_ref[...].astype(F32), gain_ref[1:2, :], dn)
    dh_ref[...] = dh
    dhb = dh.astype(BF16)
    dmix_s[...] = nt(wo_ref[...], dhb)
    dw_s[3 * width : 4 * width, :] += nn(mixed_ref[...], dhb)
    for h in range(HEADS):
        lo, hi = h * head, (h + 1) * head
        dmix = dmix_s[lo:hi, :]
        delta = jnp.zeros((1, tile), F32)
        for b in range(len(blocks)):
            dp = jnp.sum(
                dmix * kv_ref[b, width + lo : width + hi, :].astype(F32), axis=0, keepdims=True
            )
            dp_s[b : b + 1, :] = dp
            delta = delta + p_ref[b, h : h + 1, :] * dp
        q = q_ref[lo:hi, :].astype(F32)
        dq = jnp.zeros((head, tile), F32)
        for b in range(len(blocks)):
            p = p_ref[b, h : h + 1, :]
            ds = p * (dp_s[b : b + 1, :] - delta) * scale
            dq = dq + ds * kv_ref[b, lo:hi, :].astype(F32)
            dkv_s[b, lo:hi, :] = (ds * q).astype(BF16)
            dkv_s[b, width + lo : width + hi, :] = (p * dmix).astype(BF16)
        dq_s[lo:hi, :] = dq.astype(BF16)
    dq = dq_s[...]
    dw_s[0:width, :] += nn(dq, n0[...])
    for b, (ref, out) in enumerate(zip(blocks, outs)):
        dkv = dkv_s[b]
        grad = tn(dkv, wt_ref[width : 3 * width])
        if b == 0:
            grad = grad + tn(dq, wt_ref[0:width])
        out[...] = grad.astype(out.dtype)
        dw_s[width : 3 * width, :] += nn(dkv, ref[...])

    @pl.when(step == pl.num_programs(0) - 1)
    def _():
        dw_ref[...] = dw_s[...].astype(dw_ref.dtype)


def last_kernel(
    first, start_ref, vis_ref, gain_ref, dh_ref, own_ref, far_ref, near_ref, prev_ref, out_ref
):
    tile, width = start_ref.shape
    shown = shown_column(vis_ref[...], first + pl.program_id(0) * tile, tile)
    dn = own_ref[...] + far_ref[...].astype(F32) + near_ref[...].astype(F32)
    grad = dh_ref[...] + norm_back(start_ref[...].astype(F32), gain_ref[0:1, :], dn)
    out_ref[...] = jnp.where(shown > 0.5, grad, 0.0)


def weights_kernel(
    factor, pieces, lat_ref, mine_ref, other_ref, wt_ref, gain_ref,
    qkv_ref, out_ref, gain_out_ref, rows_s,
):
    total, width = mine_ref.shape
    piece = total // pieces // 2
    lat = lat_ref[0]
    for ref, band in ((mine_ref, lat), (other_ref, 1 - lat)):
        for k in range(pieces):
            at = pl.multiple_of(band * (total // 2) + k * piece, 8)
            for layer in range(2):
                lo = (2 * k + layer) * piece
                rows_s[layer, pl.ds(at, piece), :] = ref[lo : lo + piece, :].astype(F32) * factor
    for layer in range(2):
        acc = jnp.zeros((1, width), F32)
        for i in range(3):
            lo, hi = i * width, (i + 1) * width
            grad = rows_s[layer, lo:hi, :]
            weight = wt_ref[layer, lo:hi, :].astype(F32)
            acc = acc + jnp.sum(weight * grad, axis=0, keepdims=True)
            qkv_ref[layer, :, lo:hi] = grad.T
        out_ref[layer] = rows_s[layer, 3 * width : 4 * width, :]
        gain_out_ref[layer : layer + 1, :] = acc / gain_ref[layer : layer + 1, :]


def call(
    kernel, out_shape, scratch=(), grid=None, in_specs=None, out_specs=None, us=1, aliases=None
):
    return pl.pallas_call(
        kernel,
        out_shape=out_shape,
        grid_spec=pltpu.PrefetchScalarGridSpec(
            num_scalar_prefetch=0,
            grid=grid or (),
            in_specs=in_specs,
            out_specs=out_specs,
            scratch_shapes=list(scratch),
        ),
        input_output_aliases=aliases or {},
        cost_estimate=pl.CostEstimate(
            flops=int(us * 1e6 * 800), bytes_accessed=int(us * 1e6), transcendentals=0
        ),
        compiler_params=pltpu.CompilerParams(vmem_limit_bytes=VMEM_BYTES),
    )


def whole():
    return pl.BlockSpec(memory_space=pltpu.VMEM)


def scalar():
    return pl.BlockSpec(memory_space=pltpu.SMEM)


def fixed(shape):
    return pl.BlockSpec(shape, lambda i: (0,) * len(shape))


def token_spec(tile, width, first=0):
    at = first // tile
    return pl.BlockSpec((tile, width), lambda i: (i + at, 0))


def layer_spec(layer, rows, width):
    return pl.BlockSpec((None, rows, width), lambda i: (layer, 0, 0))


CHUNKS = 2
FORWARD_TILE = 256
BACKWARD_TILE = 256


def run_first(first, lat, blocks, start, packs, wt, output_weight, norm_gain_table):
    size, width = start.shape
    tile = min(FORWARD_TILE, size)
    struct = jax.ShapeDtypeStruct
    part = struct((size, width), BF16)
    tok_spec = token_spec(tile, width)
    feat_spec = pl.BlockSpec((width, tile), lambda i: (0, i))
    kernel = functools.partial(first_kernel, first)
    return call(
        kernel if packs else functools.partial(without, kernel, 8, 3),
        (
            struct((width, size), BF16),
            struct((6, 2 * width, size), BF16),
            struct((6, 8, size), F32),
            struct((width, size), BF16),
            part,
            part,
            *[struct((32, width), BF16)] * 3,
        ),
        grid=(size // tile,),
        in_specs=[scalar()]
        + [tok_spec] * 7
        + [fixed((32, width))] * len(packs)
        + [
            layer_spec(0, 3 * width, width),
            layer_spec(0, width, width),
            fixed((2, width)),
        ],
        out_specs=(
            feat_spec,
            pl.BlockSpec((6, 2 * width, tile), lambda i: (0, 0, i)),
            pl.BlockSpec((6, 8, tile), lambda i: (0, 0, i)),
            feat_spec,
            tok_spec,
            tok_spec,
            *[fixed((32, width))] * 3,
        ),
        scratch=[pltpu.VMEM((6, 8, tile), F32), pltpu.VMEM((96, width), F32)],
        us=8,
    )(lat, *blocks, start, *packs, wt, output_weight, norm_gain_table)


def run_second(lat, normals, halos, query_key_value_weight, output_weight, cot):
    points, width = cot.shape
    struct = jax.ShapeDtypeStruct
    ext, halo_cols = points + 64, HALO - 32
    every, halo = pltpu.VMEM((points, width), BF16), pltpu.VMEM((HALO, width), BF16)
    return call(
        second_kernel,
        (
            struct((points, width), F32),
            struct((4 * width, width), BF16),
            struct((32, width), BF16),
            struct((48, width), BF16),
            struct((48, width), BF16),
        ),
        in_specs=[scalar()] + [whole()] * 10,
        out_specs=(whole(),) * 5,
        scratch=[
            *[every] * 4,
            *[halo] * 3,
            every,
            pltpu.VMEM((ext, width), BF16),
            pltpu.VMEM((ext, width), BF16),
            pltpu.VMEM((halo_cols, width), BF16),
            pltpu.VMEM((halo_cols, width), BF16),
            pltpu.VMEM((ext, width), F32),
            pltpu.VMEM((ext, width), F32),
            pltpu.VMEM((halo_cols, width), F32),
            pltpu.VMEM((halo_cols, width), F32),
            every,
            pltpu.VMEM((192, 256), F32),
            every,
        ],
        us=22,
    )(lat, *normals, *halos, query_key_value_weight, output_weight, cot)


def run_third(
    first, lat, blocks, kept, dn1, cot, packs, wt, output_weight, norm_gain_table, weights, final
):
    q0, kv0, p0, mixed0, h1 = kept
    size, width = h1.shape
    tile = min(BACKWARD_TILE, size)
    struct = jax.ShapeDtypeStruct
    part = struct((size, width), BF16)
    tok_spec = token_spec(tile, width)
    feat_spec = pl.BlockSpec((width, tile), lambda i: (0, i))
    kernel = functools.partial(third_kernel, first)
    extra = [] if weights is None else [weights]
    return call(
        kernel if extra else functools.partial(without, kernel, 18, 1),
        (
            struct((size, width), F32),
            struct((size, width), F32),
            *[part] * 5,
            struct((4 * width, width), BF16 if final else F32),
        ),
        grid=(size // tile,),
        in_specs=[scalar()]
        + [tok_spec] * 6
        + [
            feat_spec,
            pl.BlockSpec((6, 2 * width, tile), lambda i: (0, 0, i)),
            pl.BlockSpec((6, 8, tile), lambda i: (0, 0, i)),
            feat_spec,
            tok_spec,
        ]
        + [token_spec(tile, width, first)] * 2
        + [
            fixed((RETURNED, width)),
            layer_spec(0, 3 * width, width),
            layer_spec(0, width, width),
            fixed((2, width)),
        ]
        + [fixed((4 * width, width))] * len(extra),
        out_specs=(*[tok_spec] * 7, fixed((4 * width, width))),
        scratch=[
            pltpu.VMEM((4 * width, width), F32),
            pltpu.VMEM((width, tile), F32),
            pltpu.VMEM((6, 2 * width, tile), BF16),
            pltpu.VMEM((width, tile), BF16),
            pltpu.VMEM((8, tile), F32),
        ],
        us=13,
    )(
        lat, *blocks, q0, kv0, p0, mixed0, h1, dn1, cot, packs, wt, output_weight,
        norm_gain_table, *extra,
    )


def local(
    tokens, visible, mask_token, norm_gain_table, query_key_value_weight, output_weight, cotangent
):
    rows, cols, width = tokens.shape
    points = rows * cols
    size = points // CHUNKS
    firsts = [c * size for c in range(CHUNKS)]
    lat_count, lon_count = lax.axis_size("lat"), lax.axis_size("lon")
    lat = lax.axis_index("lat").astype(jnp.int32).reshape(1)
    wt = jnp.swapaxes(query_key_value_weight, 1, 2)
    struct = jax.ShapeDtypeStruct
    tokens = tokens.reshape(points, width)
    cot = cotangent.reshape(points, width)
    part = struct((size, width), BF16)
    gain_spec = fixed((2, width))
    wt_spec, wo_spec = layer_spec(0, 3 * width, width), layer_spec(0, width, width)

    small = 256
    starts, normals = [], []
    for first in firsts:
        start, normal = call(
            functools.partial(start_kernel, first),
            (part, part),
            grid=(size // small,),
            in_specs=[
                token_spec(small, width, first),
                fixed((rows, cols)),
                fixed((width,)),
                gain_spec,
            ],
            out_specs=(token_spec(small, width),) * 2,
            us=2,
        )(tokens, visible, mask_token, norm_gain_table)
        starts.append(start)
        normals.append(normal)

    swapped0 = lon_swap(normals[0])
    own1, swapped0 = chained(normals[1], swapped0)
    swapped1 = lon_swap(own1)
    beyond0, beyond1 = lon_forward(swapped0), lon_forward(swapped1)
    near0, near1 = lat_swap(normals[0]), lat_swap(own1)

    def blocks_of(own, near, swapped, beyond):
        return [own, near, swapped, beyond, lat_swap(swapped), lat_swap(beyond)]

    blocks = [blocks_of(normals[0], near0, swapped0, beyond0), None]

    packs = []
    kept = []
    for c in range(CHUNKS):
        *keep, normal1, row, left, right = run_first(
            firsts[c], lat, blocks[c], starts[c], packs, wt, output_weight, norm_gain_table
        )
        packs = [row, left, right]
        kept.append((keep, normal1))
        if c == 0:
            beyond1, row, left, right = lax.optimization_barrier((beyond1, *packs))
            packs = [row, left, right]
            blocks[1] = blocks_of(own1, near1, swapped1, beyond1)

    row, left, right = packs
    from_l, from_r = from_left(right), from_right(left)
    halos = [lat_swap(row), from_l, from_r, lat_swap(from_l), lat_swap(from_r)]
    dn1, dw1, brow, bleft, bright = run_second(
        lat, [kept[0][1], kept[1][1]], halos, query_key_value_weight, output_weight, cot
    )

    from_l, from_r, brow = from_left(bright), from_right(bleft), lat_swap(brow)
    packs = jnp.concatenate(
        [brow, from_l, from_r, lat_swap(from_l), lat_swap(from_r)], 0
    )
    stages = lon_factors()
    sum1 = halves_summed(dw1)
    packs, sum1 = chained(packs, sum1)

    def plus(a, b):
        return (a.astype(F32) + b.astype(F32)).astype(BF16)

    weights = None
    backs = []
    for c in range(CHUNKS):
        dh1, d0, d1, d2, d3, d4, d5, weights = run_third(
            firsts[c], lat, blocks[c], kept[c][0], dn1, cot, packs, wt, output_weight,
            norm_gain_table, weights, c == CHUNKS - 1,
        )
        d3 = plus(d3, lat_swap(d5))
        d2 = plus(d2, lat_swap(d4))
        d1 = lat_swap(d1)
        if c == 0:
            sum1 = stage_summed(sum1, stages[0])
            weights, sum1, d1, d2, d3 = lax.optimization_barrier((weights, sum1, d1, d2, d3))
            for stage in stages[1:]:
                sum1 = stage_summed(sum1, stage)
            d2 = plus(d2, lon_backward(d3))
        backs.append((dh1, d0, d1, d2, d3))

    d2_0, (d1_1, d2_1, d3_1) = backs[0][3], backs[1][2:]
    sum0 = halves_summed(weights)
    sum0, sum1, d2_0, d1_1, d2_1, d3_1 = lax.optimization_barrier(
        (sum0, sum1, d2_0, d1_1, d2_1, d3_1)
    )
    back_1 = lon_backward(d3_1)
    sum0 = stage_summed(sum0, stages[0])
    sum0, d2_0, back_1 = lax.optimization_barrier((sum0, d2_0, back_1))
    far_0 = lon_swap(d2_0)
    d2_1 = plus(d2_1, back_1)
    for stage in stages[1:]:
        sum0 = stage_summed(sum0, stage)
    sum0, d2_1, far_0 = lax.optimization_barrier((sum0, d2_1, far_0))
    far_1 = lon_swap(d2_1)
    sums = jnp.concatenate([sum0, sum1], 0)
    for stage in stages[:0:-1]:
        sums = spread(sums, *stage)
    sums, far_1 = chained(sums, far_1)
    sums = spread(sums, *stages[0])
    ends = [(*backs[0][:3], far_0), (*backs[1][:2], d1_1, far_1)]

    grad_tokens = None
    for c in range(CHUNKS):
        dh1, d0, near, far = ends[c]
        extra = [] if grad_tokens is None else [grad_tokens]
        kernel = functools.partial(last_kernel, firsts[c])
        grad_tokens = call(
            kernel if extra else functools.partial(without, kernel, 7, 1),
            struct((points, width), F32),
            grid=(size // small,),
            in_specs=[token_spec(small, width), fixed((rows, cols)), gain_spec]
            + [token_spec(small, width)] * 4
            + [pl.BlockSpec(memory_space=pl.ANY)] * len(extra),
            out_specs=token_spec(small, width, firsts[c]),
            aliases={7: 0} if extra else {},
            us=4,
        )(starts[c], visible, norm_gain_table, dh1, d0, far, near, *extra)

    sums, grad_tokens = chained(sums, grad_tokens)
    other = lat_swap(sums)
    factor = (points * lat_count * lon_count) ** (-0.5)
    g_qkv, g_out, g_gain = call(
        functools.partial(weights_kernel, factor, lon_count),
        (
            struct((2, width, 3 * width), F32),
            struct((2, width, width), F32),
            struct((2, width), F32),
        ),
        in_specs=[scalar()] + [whole()] * 4,
        out_specs=(whole(),) * 3,
        scratch=[pltpu.VMEM((2, 4 * width, width), F32)],
        us=5,
    )(lat, sums, other, wt, norm_gain_table)
    return grad_tokens.reshape(rows, cols, width), g_qkv, g_out, g_gain


def without(kernel, at, count, *refs):
    kernel(*refs[:at], *[None] * count, *refs[at:])


def solution(mesh):
    return jax.shard_map(
        local,
        mesh=mesh,
        in_specs=(
            P(("group", "lat"), "lon", None),
            P(("group", "lat"), "lon"),
            P(),
            P(),
            P(),
            P(),
            P(("group", "lat"), "lon", None),
        ),
        out_specs=(
            P(("group", "lat"), "lon", None),
            P("group", None, None),
            P("group", None, None),
            P("group", None),
        ),
        check_vma=False,
    )
```

```python
import functools

import jax
import jax.numpy as jnp
from jax import lax
from jax.experimental import pallas as pl
from jax.experimental.pallas import tpu as pltpu
from jax.sharding import PartitionSpec as P

HEADS = 6
EPS = 1e-05
F32 = jnp.float32
BF16 = jnp.bfloat16
LARGE_MIB = 56
HALO = 112
CORNER = 96
KEYS = 208
RETURNED = 224


def nn(a, b):
    return lax.dot_general(a, b, (((1,), (0,)), ((), ())), preferred_element_type=F32)


def nt(a, b):
    return lax.dot_general(a, b, (((1,), (1,)), ((), ())), preferred_element_type=F32)


def tn(a, b):
    return lax.dot_general(a, b, (((0,), (0,)), ((), ())), preferred_element_type=F32)


def tt(a, b):
    return lax.dot_general(a, b, (((0,), (1,)), ((), ())), preferred_element_type=F32)


def iota(shape, dim):
    return lax.broadcasted_iota(jnp.int32, shape, dim)


def one_hot(condition):
    return jnp.where(condition, 1.0, 0.0).astype(BF16)


def permuted(value, axis, target):
    count = lax.axis_size(axis)
    return lax.ppermute(value, axis, [(i, target(i) % count) for i in range(count)])


def lat_swap(value):
    return permuted(value, "lat", lambda i: i ^ 1)


def lon_swap(value):
    return permuted(value, "lon", lambda i: i ^ 1)


def lon_forward(value):
    return permuted(value, "lon", lambda i: i + 2 if i % 2 == 0 else i - 2)


def lon_backward(value):
    return permuted(value, "lon", lambda i: i - 2 if i % 2 == 0 else i + 2)


def from_left(value):
    return permuted(value, "lon", lambda i: i + 1)


def from_right(value):
    return permuted(value, "lon", lambda i: i - 1)


def chained(value, after):
    return lax.optimization_barrier((value, after))


def exchanged(parts, axis_stride, factor):
    count = lax.axis_size("lon")
    digit = (lax.axis_index("lon") // axis_stride) % factor
    moved = []
    for d in range(1, factor):
        pairs = [(i, shifted(i, axis_stride, factor, d)) for i in range(count)]
        moved.append(lax.ppermute(parts(digit ^ d), "lon", pairs))
    total = parts(digit).astype(F32)
    for piece in moved:
        total = total + piece.astype(F32)
    return total.astype(BF16)


def shifted(i, stride, factor, d):
    digit = (i // stride) % factor
    return i + ((digit ^ d) - digit) * stride


def spread(value, axis_stride, factor):
    count = lax.axis_size("lon")
    digit = (lax.axis_index("lon") // axis_stride) % factor
    rows = value.shape[0]
    full = jnp.zeros((factor * rows,) + value.shape[1:], value.dtype)
    full = lax.dynamic_update_slice(full, value, (digit * rows, 0))
    for d in range(1, factor):
        pairs = [(i, shifted(i, axis_stride, factor, d)) for i in range(count)]
        got = lax.ppermute(value, "lon", pairs)
        at = (digit ^ d) * rows
        full = lax.dynamic_update_slice(full, got, (at, 0))
    return full


def lon_factors():
    left = lax.axis_size("lon")
    stride, out = 1, []
    for factor in [2] + [4] * 10:
        if left == 1:
            break
        factor = min(factor, left)
        out.append((stride, factor))
        stride, left = stride * factor, left // factor
    return out


def halves_summed(mine, other):
    return (mine.astype(F32) + lat_swap(other).astype(F32)).astype(BF16)


def stage_summed(value, stage):
    stride, factor = stage
    size = value.shape[0] // factor
    return exchanged(
        lambda k: lax.dynamic_slice_in_dim(value, k * size, size, 0), stride, factor
    )


def norm_parts(x):
    mean = jnp.mean(x, axis=-1, keepdims=True)
    centred = x - mean
    spread = jnp.mean(centred * centred, axis=-1, keepdims=True)
    rstd = lax.rsqrt(spread + EPS)
    return centred * rstd, rstd


def norm_back(x, gain, grad_normal):
    xhat, rstd = norm_parts(x)
    g = grad_normal * gain
    return rstd * (
        g - jnp.mean(g, axis=-1, keepdims=True) - xhat * jnp.mean(g * xhat, axis=-1, keepdims=True)
    )


def shown_column(visible, base, tile):
    rows, cols = visible.shape
    token = base + iota((tile, rows), 0)
    of_row = nn(one_hot(token // cols == iota((tile, rows), 1)), visible.astype(F32).astype(BF16))
    token = base + iota((tile, cols), 0)
    mine = token % cols == iota((tile, cols), 1)
    return jnp.sum(jnp.where(mine, of_row, 0.0), axis=1, keepdims=True)


def start_kernel(first, tok_ref, vis_ref, mask_ref, gain_ref, start_ref, normal_ref):
    tile, width = tok_ref.shape
    base = first + pl.program_id(0) * tile
    shown = shown_column(vis_ref[...], base, tile)
    x = jnp.where(shown > 0.5, tok_ref[...].astype(F32), mask_ref[...].astype(F32).reshape(1, width))
    start_ref[...] = x.astype(BF16)
    xhat, _ = norm_parts(x)
    normal_ref[...] = (xhat * gain_ref[0:1, :]).astype(BF16)


def first_kernel(
    first, lat_ref, n0, n1, n2, n3, n4, n5, start_ref, row_in, left_in, right_in,
    wt_ref, wo_ref, gain_ref,
    q_ref, kv_ref, p_ref, mixed_ref, h_ref, normal_ref, row_ref, left_ref, right_ref,
    w_s, pack_s,
):
    width, tile = q_ref.shape
    head = width // HEADS
    blocks = (n0, n1, n2, n3, n4, n5)
    q_ref[...] = nt(wt_ref[0:width], n0[...]).astype(BF16)
    for b, ref in enumerate(blocks):
        kv_ref[b] = nt(wt_ref[width : 3 * width], ref[...]).astype(BF16)
    for h in range(HEADS):
        lo, hi = h * head, (h + 1) * head
        q = q_ref[lo:hi, :].astype(F32) * (head**-0.5)
        total = jnp.zeros((1, tile), F32)
        out = jnp.zeros((head, tile), F32)
        for b in range(len(blocks)):
            k = kv_ref[b, lo:hi, :].astype(F32)
            w = jnp.exp(jnp.sum(q * k, axis=0, keepdims=True))
            w_s[b, h : h + 1, :] = w
            total = total + w
            out = out + w * kv_ref[b, width + lo : width + hi, :].astype(F32)
        inverse = 1.0 / total
        for b in range(len(blocks)):
            p_ref[b, h : h + 1, :] = w_s[b, h : h + 1, :] * inverse
        mixed_ref[lo:hi, :] = (out * inverse).astype(BF16)
    h1 = start_ref[...].astype(F32) + tn(mixed_ref[...], wo_ref[...])
    h1 = h1.astype(BF16)
    h_ref[...] = h1
    xhat, _ = norm_parts(h1.astype(F32))
    normal = (xhat * gain_ref[1:2, :]).astype(BF16)
    normal_ref[...] = normal
    step = pl.program_id(0)
    brow = jnp.where(lat_ref[0] == 0, 31, 0)
    slot = iota((96, tile), 0)
    token = first + step * tile + iota((96, tile), 1)
    r, c = token // 32, token % 32
    pick = one_hot(
        ((slot < 32) & (r == brow) & (c == slot))
        | ((slot >= 32) & (slot < 64) & (c == 0) & (r == slot - 32))
        | ((slot >= 64) & (c == 31) & (r == slot - 64))
    )

    @pl.when(step == 0)
    def _():
        for i, ref in enumerate((row_in, left_in, right_in)):
            known = jnp.zeros((32, width), F32) if ref is None else ref[...].astype(F32)
            pack_s[i * 32 : i * 32 + 32, :] = known

    pack_s[...] += nn(pick, normal)

    @pl.when(step == pl.num_programs(0) - 1)
    def _():
        for i, ref in enumerate((row_ref, left_ref, right_ref)):
            ref[...] = pack_s[i * 32 : i * 32 + 32, :].astype(BF16)


def write_halves(lat, total_ref, mine_ref, other_ref):
    half = mine_ref.shape[0]
    for band in range(2):

        @pl.when(lat == band)
        def _():
            mine_ref[...] = total_ref[band * half : (band + 1) * half, :].astype(BF16)
            other_ref[...] = total_ref[(1 - band) * half : (2 - band) * half, :].astype(BF16)


def second_kernel(
    lat_ref, na_ref, nb_ref, row_ref, left_ref, right_ref, dleft_ref, dright_ref,
    w_all, wo_all, cot_ref,
    dn_ref, dw_ref, brow_ref, bleft_ref, bright_ref,
    dq_ref, dk_ref, dv_ref, mixed_s, dkh_ref, dvh_ref, halo_s,
    q_s, k_s, v_s, kc_s, vc_s, dk_s, dv_s, dkc_s, dvc_s, do_s, mask_s, normal_s,
):
    points, width = cot_ref.shape
    head = width // HEADS
    w_ref, wo_ref = w_all.at[1], wo_all.at[1]
    upper = lat_ref[0] == 0
    halo_s[0:32, :] = row_ref[...]
    halo_s[32:64, :] = left_ref[...]
    halo_s[64:96, :] = right_ref[...]
    a, b = iota((16, 32), 0), iota((16, 32), 1)
    sent = b == jnp.where(upper, 0, 31)
    corners = nn(one_hot(sent & (a == 0)), dleft_ref[...])
    corners += nn(one_hot(sent & (a == 1)), dright_ref[...])
    halo_s[CORNER:HALO, :] = corners.astype(BF16)
    halo = halo_s[...]
    normal_s[0 : points // 2, :] = na_ref[...]
    normal_s[points // 2 : points, :] = nb_ref[...]
    normal = normal_s[...]
    scale = head**-0.5
    q_s[...] = (nn(normal, w_ref[:, 0:width]).astype(BF16).astype(F32) * scale).astype(BF16)
    k_s[32 : 32 + points, :] = nn(normal, w_ref[:, width : 2 * width]).astype(BF16)
    v_s[32 : 32 + points, :] = nn(normal, w_ref[:, 2 * width : 3 * width]).astype(BF16)
    kh = nn(halo, w_ref[:, width : 2 * width]).astype(BF16)
    vh = nn(halo, w_ref[:, 2 * width : 3 * width]).astype(BF16)
    for at in (0, 32 + points):
        k_s[at : at + 32, :] = kh[0:32]
        v_s[at : at + 32, :] = vh[0:32]
    tiles = points // 128
    slots = tiles * 16
    a, b = iota((slots, HALO - 32), 0), iota((slots, HALO - 32), 1)
    place, is_right = a % 16, jnp.where(a % 16 >= 6, 1, 0)
    ext_row = 4 * (a // 16) + place - 6 * is_right
    inner = (ext_row >= 1) & (ext_row <= 32)
    source = jnp.where(inner, 32 * is_right + ext_row - 1, 64 + is_right)
    spread_cols = one_hot((place < 12) & (b == source))
    kc_s[...] = nn(spread_cols, kh[32:HALO]).astype(BF16)
    vc_s[...] = nn(spread_cols, vh[32:HALO]).astype(BF16)
    dk_s[...] = jnp.zeros_like(dk_s)
    dv_s[...] = jnp.zeros_like(dv_s)
    cot = cot_ref[...].astype(BF16)
    do_s[...] = nt(cot, wo_ref[...]).astype(BF16)

    key, query = iota((KEYS, 256), 0), iota((KEYS, 256), 1) % 128
    place = key - 192
    right = place >= 6
    row = jnp.where(place < 0, key // 32, jnp.where(right, place - 6, place))
    col = jnp.where(place < 0, key % 32, jnp.where(right, 32, -1))
    near = (jnp.abs(row - 1 - query // 32) <= 1) & (jnp.abs(col - query % 32) <= 1)
    mask_s[...] = jnp.where(near & (place < 12), row, 9)

    def tile_step(t, carry):
        base = pl.multiple_of(t * 128, 128)
        first = jnp.where(upper & (t == 0), 1, 0)
        last = jnp.where(jnp.logical_not(upper) & (t == tiles - 1), 4, 5)
        mask = (mask_s[...] >= first) & (mask_s[...] <= last)
        even = iota((128, 128), 1) < 64
        top = iota((128, 128), 0) < 64
        win, here = pl.ds(base, 192), pl.ds(base, 128)
        side = pl.ds(pl.multiple_of(t * 16, 16), 16)
        for pair in range(HEADS // 2):
            lanes = slice(pair * 128, pair * 128 + 128)
            q = q_s[here, lanes]
            do = do_s[here, lanes]
            zero = jnp.zeros_like(q)
            qm = jnp.concatenate([jnp.where(even, q, zero), jnp.where(even, zero, q)], 0)
            dom = jnp.concatenate([jnp.where(even, do, zero), jnp.where(even, zero, do)], 0)
            k = jnp.concatenate([k_s[win, lanes], kc_s[side, lanes]], 0)
            v = jnp.concatenate([v_s[win, lanes], vc_s[side, lanes]], 0)
            w = jnp.where(mask, jnp.exp(nt(k, qm)), 0.0)
            p = w * (1.0 / jnp.sum(w, axis=0, keepdims=True))
            dp = nt(v, dom)
            delta = jnp.sum(p * dp, axis=0, keepdims=True)
            ds = (p * (dp - delta)).astype(BF16)
            p = p.astype(BF16)
            out = tn(v, p)
            mixed_s[lanes, here] = jnp.where(top, out[:, 0:128], out[:, 128:256]).astype(BF16)
            dq = tn(k, ds) * scale
            dq_ref[lanes, here] = jnp.where(top, dq[:, 0:128], dq[:, 128:256]).astype(BF16)
            dk, dv = nn(ds, qm), nn(p, dom)
            dk_s[win, lanes] += dk[0:192]
            dv_s[win, lanes] += dv[0:192]
            dkc_s[side, lanes] = dk[192:KEYS].astype(BF16)
            dvc_s[side, lanes] = dv[192:KEYS].astype(BF16)
        return carry

    lax.fori_loop(0, tiles, tile_step, 0)

    row_at = pl.multiple_of(jnp.where(upper, 32 + points, 0), 32)
    dkh = jnp.concatenate([dk_s[pl.ds(row_at, 32), :], tn(spread_cols, dkc_s[...])], 0).astype(BF16)
    dvh = jnp.concatenate([dv_s[pl.ds(row_at, 32), :], tn(spread_cols, dvc_s[...])], 0).astype(BF16)
    dkh_ref[...] = dkh
    dvh_ref[...] = dvh
    dk_ref[...] = dk_s[32 : 32 + points, :].astype(BF16)
    dv_ref[...] = dv_s[32 : 32 + points, :].astype(BF16)
    wk, wv = (w_ref[:, i * width : (i + 1) * width] for i in (1, 2))
    back = (nt(dkh, wk) + nt(dvh, wv)).astype(BF16)
    brow_ref[...] = back[0:32]
    for ref, at in ((bleft_ref, 32), (bright_ref, 64)):
        ref[0:32, :] = back[at : at + 32]
        ref[32:48, :] = back[CORNER:HALO]
    wq, wk, wv = (w_all[1, :, i * width : (i + 1) * width] for i in range(3))
    dw_ref[0:width, :] = nn(dq_ref[...], normal).astype(BF16)
    dw_ref[width : 2 * width, :] = (tn(dk_ref[...], normal) + tn(dkh_ref[...], halo)).astype(BF16)
    dw_ref[2 * width : 3 * width, :] = (
        tn(dv_ref[...], normal) + tn(dvh_ref[...], halo)
    ).astype(BF16)
    dw_ref[3 * width : 4 * width, :] = nn(mixed_s[...], cot).astype(BF16)
    dn_ref[...] = tt(dq_ref[...], wq) + nt(dk_ref[...], wk) + nt(dv_ref[...], wv)


def third_kernel(
    first, lat_ref, n0, n1, n2, n3, n4, n5, q_ref, kv_ref, p_ref, mixed_ref, h_ref, dn1_ref, cot_ref,
    packs_ref, wt_ref, wo_ref, gain_ref, dw_in,
    dh_ref, d0, d1, d2, d3, d4, d5, dw_ref, other_ref,
    dw_s, dmix_s, dkv_s, dq_s, dp_s, n_s,
):
    width, tile = q_ref.shape
    head = width // HEADS
    scale = head**-0.5
    blocks = (n0, n1, n2, n3, n4, n5)
    outs = (d0, d1, d2, d3, d4, d5)
    step = pl.program_id(0)

    @pl.when(step == 0)
    def _():
        dw_s[...] = jnp.zeros_like(dw_s) if dw_in is None else dw_in[...]

    brow = jnp.where(lat_ref[0] == 0, 31, 0)
    shape = (tile, RETURNED)
    token = first + step * tile + iota(shape, 0)
    r, c, slot = token // 32, token % 32, iota(shape, 1)
    border = r == brow
    place = one_hot(
        (border & (slot < 32) & (slot == c))
        | ((c == 0) & (slot < 64) & (slot == 32 + r))
        | ((c == 31) & (slot < 112) & (slot == 80 + r))
        | (border & (c == 0) & (slot == 128 + 33))
        | (border & (c == 31) & (slot == 176 + 32))
    )
    dn = dn1_ref[...] + nn(place, packs_ref[...])
    dh = cot_ref[...] + norm_back(h_ref[...].astype(F32), gain_ref[1:2, :], dn)
    dh_ref[...] = dh
    dhb = dh.astype(BF16)
    dmix_s[...] = nt(wo_ref[...], dhb)
    dw_s[3 * width : 4 * width, :] += nn(mixed_ref[...], dhb)
    for h in range(HEADS):
        lo, hi = h * head, (h + 1) * head
        dmix = dmix_s[lo:hi, :]
        delta = jnp.zeros((1, tile), F32)
        for b in range(len(blocks)):
            dp = jnp.sum(
                dmix * kv_ref[b, width + lo : width + hi, :].astype(F32), axis=0, keepdims=True
            )
            dp_s[b : b + 1, :] = dp
            delta = delta + p_ref[b, h : h + 1, :] * dp
        q = q_ref[lo:hi, :].astype(F32)
        dq = jnp.zeros((head, tile), F32)
        for b in range(len(blocks)):
            p = p_ref[b, h : h + 1, :]
            ds = p * (dp_s[b : b + 1, :] - delta) * scale
            dq = dq + ds * kv_ref[b, lo:hi, :].astype(F32)
            here = slice(b * tile, (b + 1) * tile)
            dkv_s[lo:hi, here] = (ds * q).astype(BF16)
            dkv_s[width + lo : width + hi, here] = (p * dmix).astype(BF16)
        dq_s[lo:hi, :] = dq.astype(BF16)
    dq = dq_s[...]
    dw_s[0:width, :] += nn(dq, n0[...])
    for b, ref in enumerate(blocks):
        n_s[b * tile : (b + 1) * tile, :] = ref[...]
    dw_s[width : 3 * width, :] += nn(dkv_s[...], n_s[...])
    grads = tn(dkv_s[...], wt_ref[width : 3 * width])
    outs[0][...] = grads[0:tile] + tn(dq, wt_ref[0:width])
    for b in range(1, len(blocks)):
        outs[b][...] = grads[b * tile : (b + 1) * tile].astype(BF16)

    @pl.when(step == pl.num_programs(0) - 1)
    def _():
        if other_ref is None:
            dw_ref[...] = dw_s[...]
        else:
            write_halves(lat_ref[0], dw_s, dw_ref, other_ref)


def last_kernel(
    first, start_ref, vis_ref, gain_ref, dh_ref, own_ref, far_ref, near_ref, prev_ref, out_ref
):
    tile, width = start_ref.shape
    shown = shown_column(vis_ref[...], first + pl.program_id(0) * tile, tile)
    dn = own_ref[...] + far_ref[...].astype(F32) + near_ref[...].astype(F32)
    grad = dh_ref[...] + norm_back(start_ref[...].astype(F32), gain_ref[0:1, :], dn)
    out_ref[...] = jnp.where(shown > 0.5, grad, 0.0)


def weights_kernel(
    factor, pieces, lat_ref, mine_ref, other_ref, wt_ref, gain_ref,
    qkv_ref, out_ref, gain_out_ref, rows_s,
):
    total, width = mine_ref.shape
    piece = total // pieces // 2
    lat = lat_ref[0]
    for ref, band in ((mine_ref, lat), (other_ref, 1 - lat)):
        for k in range(pieces):
            at = pl.multiple_of(band * (total // 2) + k * piece, 8)
            for layer in range(2):
                lo = (2 * k + layer) * piece
                rows_s[layer, pl.ds(at, piece), :] = ref[lo : lo + piece, :].astype(F32) * factor
    for layer in range(2):
        acc = jnp.zeros((1, width), F32)
        for i in range(3):
            lo, hi = i * width, (i + 1) * width
            grad = rows_s[layer, lo:hi, :]
            weight = wt_ref[layer, lo:hi, :].astype(F32)
            acc = acc + jnp.sum(weight * grad, axis=0, keepdims=True)
            qkv_ref[layer, :, lo:hi] = grad.T
        out_ref[layer] = rows_s[layer, 3 * width : 4 * width, :]
        gain_out_ref[layer : layer + 1, :] = acc / gain_ref[layer : layer + 1, :]


def call(
    kernel, out_shape, scratch=(), grid=None, in_specs=None, out_specs=None, us=1, aliases=None, mib=12
):
    return pl.pallas_call(
        kernel,
        out_shape=out_shape,
        grid_spec=pltpu.PrefetchScalarGridSpec(
            num_scalar_prefetch=0,
            grid=grid or (),
            in_specs=in_specs,
            out_specs=out_specs,
            scratch_shapes=list(scratch),
        ),
        input_output_aliases=aliases or {},
        cost_estimate=pl.CostEstimate(
            flops=int(us * 1e6 * 800), bytes_accessed=int(us * 1e6), transcendentals=0
        ),
        compiler_params=pltpu.CompilerParams(vmem_limit_bytes=mib * 1024 * 1024),
    )


def whole():
    return pl.BlockSpec(memory_space=pltpu.VMEM)


def scalar():
    return pl.BlockSpec(memory_space=pltpu.SMEM)


def fixed(shape):
    return pl.BlockSpec(shape, lambda i: (0,) * len(shape))


def token_spec(tile, width, first=0):
    at = first // tile
    return pl.BlockSpec((tile, width), lambda i: (i + at, 0))


def layer_spec(layer, rows, width):
    return pl.BlockSpec((None, rows, width), lambda i: (layer, 0, 0))


CHUNKS = 2
FORWARD_TILE = 256
BACKWARD_TILE = 256


def run_first(first, lat, blocks, start, packs, wt, output_weight, norm_gain_table):
    size, width = start.shape
    tile = min(FORWARD_TILE, size)
    struct = jax.ShapeDtypeStruct
    part = struct((size, width), BF16)
    tok_spec = token_spec(tile, width)
    feat_spec = pl.BlockSpec((width, tile), lambda i: (0, i))
    kernel = functools.partial(first_kernel, first)
    return call(
        kernel if packs else functools.partial(without, kernel, 8, 3),
        (
            struct((width, size), BF16),
            struct((6, 2 * width, size), BF16),
            struct((6, 8, size), F32),
            struct((width, size), BF16),
            part,
            part,
            *[struct((32, width), BF16)] * 3,
        ),
        grid=(size // tile,),
        in_specs=[scalar()]
        + [tok_spec] * 7
        + [fixed((32, width))] * len(packs)
        + [
            layer_spec(0, 3 * width, width),
            layer_spec(0, width, width),
            fixed((2, width)),
        ],
        out_specs=(
            feat_spec,
            pl.BlockSpec((6, 2 * width, tile), lambda i: (0, 0, i)),
            pl.BlockSpec((6, 8, tile), lambda i: (0, 0, i)),
            feat_spec,
            tok_spec,
            tok_spec,
            *[fixed((32, width))] * 3,
        ),
        scratch=[pltpu.VMEM((6, 8, tile), F32), pltpu.VMEM((96, width), F32)],
        mib=LARGE_MIB,
        us=8,
    )(lat, *blocks, start, *packs, wt, output_weight, norm_gain_table)


def run_second(lat, normals, halos, query_key_value_weight, output_weight, cot):
    points, width = cot.shape
    struct = jax.ShapeDtypeStruct
    ext, slots = points + 64, points // 8
    across = pltpu.VMEM((width, points), BF16)
    every, halo = pltpu.VMEM((points, width), BF16), pltpu.VMEM((HALO, width), BF16)
    return call(
        second_kernel,
        (
            struct((points, width), F32),
            struct((4 * width, width), BF16),
            struct((32, width), BF16),
            struct((48, width), BF16),
            struct((48, width), BF16),
        ),
        in_specs=[scalar()] + [whole()] * 10,
        out_specs=(whole(),) * 5,
        scratch=[
            across, every, every, across,
            *[halo] * 3,
            every,
            pltpu.VMEM((ext, width), BF16),
            pltpu.VMEM((ext, width), BF16),
            *[pltpu.VMEM((slots, width), BF16)] * 2,
            pltpu.VMEM((ext, width), F32),
            pltpu.VMEM((ext, width), F32),
            *[pltpu.VMEM((slots, width), BF16)] * 2,
            every,
            pltpu.VMEM((KEYS, 256), jnp.int32),
            every,
        ],
        mib=LARGE_MIB,
        us=22,
    )(lat, *normals, *halos, query_key_value_weight, output_weight, cot)


def run_third(
    first, size, at, lat, blocks, kept, dn1, cot, packs, wt, output_weight, norm_gain_table, weights, final
):
    q0, kv0, p0, mixed0, h1 = kept
    width = h1.shape[1]
    tile = min(BACKWARD_TILE, size)
    struct = jax.ShapeDtypeStruct
    part = struct((size, width), BF16)
    tok_spec, from_spec = token_spec(tile, width), token_spec(tile, width, at)
    skip = at // tile
    feat_spec = pl.BlockSpec((width, tile), lambda i: (0, i + skip))
    kernel = functools.partial(third_kernel, first)
    extra = [] if weights is None else [weights]
    if not extra:
        kernel = functools.partial(without, kernel, 18, 1)
    if not final:
        kernel = functools.partial(without, kernel, 26 + len(extra) , 1)
    return call(
        kernel,
        (
            struct((size, width), F32),
            struct((size, width), F32),
            *[part] * 5,
            *([struct((2 * width, width), BF16)] * 2 if final else [struct((4 * width, width), F32)]),
        ),
        grid=(size // tile,),
        in_specs=[scalar()]
        + [from_spec] * 6
        + [
            feat_spec,
            pl.BlockSpec((6, 2 * width, tile), lambda i: (0, 0, i + skip)),
            pl.BlockSpec((6, 8, tile), lambda i: (0, 0, i + skip)),
            feat_spec,
            from_spec,
        ]
        + [token_spec(tile, width, first)] * 2
        + [
            fixed((RETURNED, width)),
            layer_spec(0, 3 * width, width),
            layer_spec(0, width, width),
            fixed((2, width)),
        ]
        + [fixed((4 * width, width))] * len(extra),
        out_specs=(
            *[tok_spec] * 7,
            *([fixed((2 * width, width))] * 2 if final else [fixed((4 * width, width))]),
        ),
        scratch=[
            pltpu.VMEM((4 * width, width), F32),
            pltpu.VMEM((width, tile), F32),
            pltpu.VMEM((2 * width, 6 * tile), BF16),
            pltpu.VMEM((width, tile), BF16),
            pltpu.VMEM((8, tile), F32),
            pltpu.VMEM((6 * tile, width), BF16),
        ],
        mib=LARGE_MIB,
        us=13,
    )(
        lat, *blocks, q0, kv0, p0, mixed0, h1, dn1, cot, packs, wt, output_weight,
        norm_gain_table, *extra,
    )


def local(
    tokens, visible, mask_token, norm_gain_table, query_key_value_weight, output_weight, cotangent
):
    rows, cols, width = tokens.shape
    points = rows * cols
    size = points // CHUNKS
    firsts = [c * size for c in range(CHUNKS)]
    lat_count, lon_count = lax.axis_size("lat"), lax.axis_size("lon")
    lat = lax.axis_index("lat").astype(jnp.int32).reshape(1)
    wt = jnp.swapaxes(query_key_value_weight, 1, 2)
    struct = jax.ShapeDtypeStruct
    tokens = tokens.reshape(points, width)
    cot = cotangent.reshape(points, width)
    part = struct((size, width), BF16)
    gain_spec = fixed((2, width))
    wt_spec, wo_spec = layer_spec(0, 3 * width, width), layer_spec(0, width, width)

    small = 256
    starts, normals = [], []
    for first in firsts:
        start, normal = call(
            functools.partial(start_kernel, first),
            (part, part),
            grid=(size // small,),
            in_specs=[
                token_spec(small, width, first),
                fixed((rows, cols)),
                fixed((width,)),
                gain_spec,
            ],
            out_specs=(token_spec(small, width),) * 2,
            mib=LARGE_MIB,
            us=2,
        )(tokens, visible, mask_token, norm_gain_table)
        starts.append(start)
        normals.append(normal)

    swapped0 = lon_swap(normals[0])
    own1, swapped0 = chained(normals[1], swapped0)
    swapped1 = lon_swap(own1)
    beyond0, beyond1 = lon_forward(swapped0), lon_forward(swapped1)
    near0, near1 = lat_swap(normals[0]), lat_swap(own1)

    def blocks_of(own, near, swapped, beyond):
        return [own, near, swapped, beyond, lat_swap(swapped), lat_swap(beyond)]

    blocks = [blocks_of(normals[0], near0, swapped0, beyond0), None]

    packs = []
    kept = []
    for c in range(CHUNKS):
        *keep, normal1, row, left, right = run_first(
            firsts[c], lat, blocks[c], starts[c], packs, wt, output_weight, norm_gain_table
        )
        packs = [row, left, right]
        kept.append((keep, normal1))
        if c == 0:
            beyond1, row, left, right = lax.optimization_barrier((beyond1, *packs))
            packs = [row, left, right]
            blocks[1] = blocks_of(own1, near1, swapped1, beyond1)

    row, left, right = packs
    from_l, from_r = from_left(right), from_right(left)
    halos = [lat_swap(row), from_l, from_r, lat_swap(from_l), lat_swap(from_r)]
    dn1, dw1, brow, bleft, bright = run_second(
        lat, [kept[0][1], kept[1][1]], halos, query_key_value_weight, output_weight, cot
    )

    from_l, from_r, brow = from_left(bright), from_right(bleft), lat_swap(brow)
    packs = jnp.concatenate(
        [brow, from_l, from_r, lat_swap(from_l), lat_swap(from_r)], 0
    )
    stages = lon_factors()
    sum1 = halves_summed(
        lax.dynamic_slice_in_dim(dw1, lat[0] * 2 * width, 2 * width, 0),
        lax.dynamic_slice_in_dim(dw1, (1 - lat[0]) * 2 * width, 2 * width, 0),
    )
    packs, sum1 = chained(packs, sum1)

    def plus(a, b):
        return (a.astype(F32) + b.astype(F32)).astype(BF16)

    pieces = [(first, size) for first in firsts]
    weights = None
    sum_stages = list(stages)
    ends = []
    coming = returned = None
    for n, (first, count) in enumerate(pieces):
        c = first // size
        dh1, d0, d1, d2, d3, d4, d5, *weights = run_third(
            first, count, first - c * size, lat, blocks[c], kept[c][0], dn1, cot, packs, wt,
            output_weight, norm_gain_table, weights, n == len(pieces) - 1,
        )
        if sum_stages:
            sum1 = stage_summed(sum1, sum_stages.pop(0))
        weights, sum1, d1, d2, d3, d4, d5, coming, returned = lax.optimization_barrier(
            (weights, sum1, d1, d2, d3, d4, d5, coming, returned)
        )
        d3 = plus(d3, lat_swap(d5))
        d2 = plus(d2, lat_swap(d4))
        d1 = lat_swap(d1)
        if n == len(pieces) - 1:
            weights = [halves_summed(*weights)]
        weights, d1, d2, d3 = lax.optimization_barrier((weights, d1, d2, d3))
        if returned is not None:
            ends[-2][-1] = returned
        returned = None
        if coming is not None:
            returned = lon_swap(coming)
        coming = plus(d2, lon_backward(d3))
        weights = weights[0]
        ends.append([first, count, dh1, d0, d1, None])

    sum0 = stage_summed(weights, stages[0])
    for stage in sum_stages:
        sum1 = stage_summed(sum1, stage)
    sum0, sum1, coming, returned = lax.optimization_barrier((sum0, sum1, coming, returned))
    ends[-2][-1] = returned
    returned = lon_swap(coming)
    sum0 = stage_summed(sum0, stages[1])
    sum0, returned = lax.optimization_barrier((sum0, returned))
    ends[-1][-1] = returned
    for stage in stages[2:]:
        sum0 = stage_summed(sum0, stage)
    sums = jnp.concatenate([sum0, sum1], 0)
    for stage in stages[::-1]:
        sums = spread(sums, *stage)

    grad_tokens = None
    for first, count, dh1, d0, near, far in ends:
        c = first // size
        extra = [] if grad_tokens is None else [grad_tokens]
        kernel = functools.partial(last_kernel, first)
        grad_tokens = call(
            kernel if extra else functools.partial(without, kernel, 7, 1),
            struct((points, width), F32),
            grid=(count // small,),
            in_specs=[token_spec(small, width, first - c * size), fixed((rows, cols)), gain_spec]
            + [token_spec(small, width)] * 4
            + [pl.BlockSpec(memory_space=pl.ANY)] * len(extra),
            out_specs=token_spec(small, width, first),
            aliases={7: 0} if extra else {},
            us=4,
        )(starts[c], visible, norm_gain_table, dh1, d0, far, near, *extra)

    sums, grad_tokens = chained(sums, grad_tokens)
    other = lat_swap(sums)
    factor = (points * lat_count * lon_count) ** (-0.5)
    g_qkv, g_out, g_gain = call(
        functools.partial(weights_kernel, factor, lon_count),
        (
            struct((2, width, 3 * width), F32),
            struct((2, width, width), F32),
            struct((2, width), F32),
        ),
        in_specs=[scalar()] + [whole()] * 4,
        out_specs=(whole(),) * 3,
        scratch=[pltpu.VMEM((2, 4 * width, width), F32)],
        mib=20,
        us=5,
    )(lat, sums, other, wt, norm_gain_table)
    return grad_tokens.reshape(rows, cols, width), g_qkv, g_out, g_gain


def without(kernel, at, count, *refs):
    kernel(*refs[:at], *[None] * count, *refs[at:])


def solution(mesh):
    return jax.shard_map(
        local,
        mesh=mesh,
        in_specs=(
            P(("group", "lat"), "lon", None),
            P(("group", "lat"), "lon"),
            P(),
            P(),
            P(),
            P(),
            P(("group", "lat"), "lon", None),
        ),
        out_specs=(
            P(("group", "lat"), "lon", None),
            P("group", None, None),
            P("group", None, None),
            P("group", None),
        ),
        check_vma=False,
    )
```

```python
import functools

import jax
import jax.numpy as jnp
import numpy as np
from jax import lax
from jax.experimental import pallas as pl
from jax.experimental.pallas import tpu as pltpu
from jax.sharding import PartitionSpec as P

HEADS = 6
EPS = 1e-05
F32 = jnp.float32
BF16 = jnp.bfloat16
LARGE_MIB = 56
HALO = 112
CORNER = 96
KEYS = 208
RETURNED = 224


def nn(a, b):
    return lax.dot_general(a, b, (((1,), (0,)), ((), ())), preferred_element_type=F32)


def nt(a, b):
    return lax.dot_general(a, b, (((1,), (1,)), ((), ())), preferred_element_type=F32)


def tn(a, b):
    return lax.dot_general(a, b, (((0,), (0,)), ((), ())), preferred_element_type=F32)


def tt(a, b):
    return lax.dot_general(a, b, (((0,), (1,)), ((), ())), preferred_element_type=F32)


def iota(shape, dim):
    return lax.broadcasted_iota(jnp.int32, shape, dim)


def one_hot(condition):
    return jnp.where(condition, 1.0, 0.0).astype(BF16)


def permuted(value, axis, target):
    count = lax.axis_size(axis)
    return lax.ppermute(value, axis, [(i, target(i) % count) for i in range(count)])


def lat_swap(value):
    return permuted(value, "lat", lambda i: i ^ 1)


def lon_swap(value):
    return permuted(value, "lon", lambda i: i ^ 1)


def lon_forward(value):
    return permuted(value, "lon", lambda i: i + 2 if i % 2 == 0 else i - 2)


def lon_backward(value):
    return permuted(value, "lon", lambda i: i - 2 if i % 2 == 0 else i + 2)


def from_left(value):
    return permuted(value, "lon", lambda i: i + 1)


def from_right(value):
    return permuted(value, "lon", lambda i: i - 1)


def chained(value, after):
    return lax.optimization_barrier((value, after))


def exchanged(parts, axis_stride, factor):
    count = lax.axis_size("lon")
    digit = (lax.axis_index("lon") // axis_stride) % factor
    moved = []
    for d in range(1, factor):
        pairs = [(i, shifted(i, axis_stride, factor, d)) for i in range(count)]
        moved.append(lax.ppermute(parts(digit ^ d), "lon", pairs))
    total = parts(digit).astype(F32)
    for piece in moved:
        total = total + piece.astype(F32)
    return total.astype(BF16)


def shifted(i, stride, factor, d):
    digit = (i // stride) % factor
    return i + ((digit ^ d) - digit) * stride


def spread(value, axis_stride, factor):
    count = lax.axis_size("lon")
    digit = (lax.axis_index("lon") // axis_stride) % factor
    rows = value.shape[0]
    full = jnp.zeros((factor * rows,) + value.shape[1:], value.dtype)
    full = lax.dynamic_update_slice(full, value, (digit * rows, 0))
    for d in range(1, factor):
        pairs = [(i, shifted(i, axis_stride, factor, d)) for i in range(count)]
        got = lax.ppermute(value, "lon", pairs)
        at = (digit ^ d) * rows
        full = lax.dynamic_update_slice(full, got, (at, 0))
    return full


def lon_factors():
    left = lax.axis_size("lon")
    stride, out = 1, []
    for factor in [2] + [4] * 10:
        if left == 1:
            break
        factor = min(factor, left)
        out.append((stride, factor))
        stride, left = stride * factor, left // factor
    return out


def halves_summed(mine, other):
    return (mine.astype(F32) + lat_swap(other).astype(F32)).astype(BF16)


def stage_summed(value, stage):
    stride, factor = stage
    size = value.shape[0] // factor
    return exchanged(
        lambda k: lax.dynamic_slice_in_dim(value, k * size, size, 0), stride, factor
    )


def norm_parts(x):
    mean = jnp.mean(x, axis=-1, keepdims=True)
    centred = x - mean
    spread = jnp.mean(centred * centred, axis=-1, keepdims=True)
    rstd = lax.rsqrt(spread + EPS)
    return centred * rstd, rstd


def norm_back(x, gain, grad_normal):
    xhat, rstd = norm_parts(x)
    g = grad_normal * gain
    return rstd * (
        g - jnp.mean(g, axis=-1, keepdims=True) - xhat * jnp.mean(g * xhat, axis=-1, keepdims=True)
    )


def shown_column(visible, token):
    rows, cols = visible.shape
    tile = token.shape[0]
    of_row = nn(one_hot(token // cols == iota((tile, rows), 1)), visible.astype(F32).astype(BF16))
    mine = token % cols == iota((tile, cols), 1)
    return jnp.sum(jnp.where(mine, of_row, 0.0), axis=1, keepdims=True)


def token_order(rows, cols):
    row, col = np.divmod(np.arange(rows * cols), cols)
    border = (row == 0) | (row == rows - 1) | (col == 0) | (col == cols - 1)
    order = np.argsort(~border, kind="stable").astype(np.int32)
    return order, np.argsort(order, kind="stable").astype(np.int32)


def picked(places, values):
    count = values.shape[0]
    return nn(one_hot(places == iota((places.shape[0], count), 1)), values)


def start_kernel(order_ref, tok_ref, vis_ref, mask_ref, gain_ref, start_ref, normal_ref):
    width = tok_ref.shape[1]
    token = order_ref[...]
    shown = shown_column(vis_ref[...], token)
    x = jnp.where(
        shown > 0.5, picked(token, tok_ref[...]), mask_ref[...].astype(F32).reshape(1, width)
    )
    start_ref[...] = x.astype(BF16)
    xhat, _ = norm_parts(x)
    normal_ref[...] = (xhat * gain_ref[0:1, :]).astype(BF16)


def first_kernel(
    lat_ref, order_ref, n0, n1, n2, n3, n4, n5, start_ref,
    wt_ref, wo_ref, gain_ref,
    q_ref, kv_ref, p_ref, mixed_ref, h_ref, normal_ref, row_ref, left_ref, right_ref,
    w_s, pack_s,
):
    width, tile = q_ref.shape
    head = width // HEADS
    blocks = (n0, n1, n2, n3, n4, n5)
    q_ref[...] = nt(wt_ref[0:width], n0[...]).astype(BF16)
    for b, ref in enumerate(blocks):
        kv_ref[b] = nt(wt_ref[width : 3 * width], ref[...]).astype(BF16)
    for h in range(HEADS):
        lo, hi = h * head, (h + 1) * head
        q = q_ref[lo:hi, :].astype(F32) * (head**-0.5)
        total = jnp.zeros((1, tile), F32)
        out = jnp.zeros((head, tile), F32)
        for b in range(len(blocks)):
            k = kv_ref[b, lo:hi, :].astype(F32)
            w = jnp.exp(jnp.sum(q * k, axis=0, keepdims=True))
            w_s[b, h : h + 1, :] = w
            total = total + w
            out = out + w * kv_ref[b, width + lo : width + hi, :].astype(F32)
        inverse = 1.0 / total
        for b in range(len(blocks)):
            p_ref[b, h : h + 1, :] = w_s[b, h : h + 1, :] * inverse
        mixed_ref[lo:hi, :] = (out * inverse).astype(BF16)
    h1 = start_ref[...].astype(F32) + tn(mixed_ref[...], wo_ref[...])
    h1 = h1.astype(BF16)
    h_ref[...] = h1
    xhat, _ = norm_parts(h1.astype(F32))
    normal = (xhat * gain_ref[1:2, :]).astype(BF16)
    normal_ref[...] = normal
    step = pl.program_id(0)
    brow = jnp.where(lat_ref[0] == 0, 31, 0)
    slot = iota((96, tile), 0)
    r, c = order_ref[...] // 32, order_ref[...] % 32
    pick = one_hot(
        ((slot < 32) & (r == brow) & (c == slot))
        | ((slot >= 32) & (slot < 64) & (c == 0) & (r == slot - 32))
        | ((slot >= 64) & (c == 31) & (r == slot - 64))
    )

    @pl.when(step == 0)
    def _():
        pack_s[...] = jnp.zeros_like(pack_s)

    pack_s[...] += nn(pick, normal)

    @pl.when(step == pl.num_programs(0) - 1)
    def _():
        for i, ref in enumerate((row_ref, left_ref, right_ref)):
            ref[...] = pack_s[i * 32 : i * 32 + 32, :].astype(BF16)


def write_halves(lat, total_ref, mine_ref, other_ref):
    half = mine_ref.shape[0]
    for band in range(2):

        @pl.when(lat == band)
        def _():
            mine_ref[...] = total_ref[band * half : (band + 1) * half, :].astype(BF16)
            other_ref[...] = total_ref[(1 - band) * half : (2 - band) * half, :].astype(BF16)


def second_kernel(
    lat_ref, place_ref, na_ref, nb_ref, row_ref, left_ref, right_ref, dleft_ref, dright_ref,
    w_all, wo_all, cot_ref,
    both_ref, dw_ref, brow_ref, bleft_ref, bright_ref,
    dq_ref, dk_ref, dv_ref, mixed_s, dkh_ref, dvh_ref, halo_s,
    q_s, k_s, v_s, kc_s, vc_s, dk_s, dv_s, dkc_s, dvc_s, do_s, mask_s, normal_s,
):
    points, width = cot_ref.shape
    head = width // HEADS
    w_ref, wo_ref = w_all.at[1], wo_all.at[1]
    upper = lat_ref[0] == 0
    halo_s[0:32, :] = row_ref[...]
    halo_s[32:64, :] = left_ref[...]
    halo_s[64:96, :] = right_ref[...]
    a, b = iota((16, 32), 0), iota((16, 32), 1)
    sent = b == jnp.where(upper, 0, 31)
    corners = nn(one_hot(sent & (a == 0)), dleft_ref[...])
    corners += nn(one_hot(sent & (a == 1)), dright_ref[...])
    halo_s[CORNER:HALO, :] = corners.astype(BF16)
    halo = halo_s[...]
    ordered = jnp.concatenate([na_ref[...], nb_ref[...]], 0)
    for at in range(0, points, 256):
        rows = slice(at, at + 256)
        normal_s[rows, :] = picked(place_ref[rows, :], ordered).astype(BF16)
    normal = normal_s[...]
    scale = head**-0.5
    q_s[...] = (nn(normal, w_ref[:, 0:width]).astype(BF16).astype(F32) * scale).astype(BF16)
    k_s[32 : 32 + points, :] = nn(normal, w_ref[:, width : 2 * width]).astype(BF16)
    v_s[32 : 32 + points, :] = nn(normal, w_ref[:, 2 * width : 3 * width]).astype(BF16)
    kh = nn(halo, w_ref[:, width : 2 * width]).astype(BF16)
    vh = nn(halo, w_ref[:, 2 * width : 3 * width]).astype(BF16)
    for at in (0, 32 + points):
        k_s[at : at + 32, :] = kh[0:32]
        v_s[at : at + 32, :] = vh[0:32]
    tiles = points // 128
    slots = tiles * 16
    a, b = iota((slots, HALO - 32), 0), iota((slots, HALO - 32), 1)
    place, is_right = a % 16, jnp.where(a % 16 >= 6, 1, 0)
    ext_row = 4 * (a // 16) + place - 6 * is_right
    inner = (ext_row >= 1) & (ext_row <= 32)
    source = jnp.where(inner, 32 * is_right + ext_row - 1, 64 + is_right)
    spread_cols = one_hot((place < 12) & (b == source))
    kc_s[...] = nn(spread_cols, kh[32:HALO]).astype(BF16)
    vc_s[...] = nn(spread_cols, vh[32:HALO]).astype(BF16)
    dk_s[...] = jnp.zeros_like(dk_s)
    dv_s[...] = jnp.zeros_like(dv_s)
    cot = cot_ref[...].astype(BF16)
    both_ref[:, width : 2 * width] = cot
    do_s[...] = nt(cot, wo_ref[...]).astype(BF16)

    key, query = iota((KEYS, 256), 0), iota((KEYS, 256), 1) % 128
    place = key - 192
    right = place >= 6
    row = jnp.where(place < 0, key // 32, jnp.where(right, place - 6, place))
    col = jnp.where(place < 0, key % 32, jnp.where(right, 32, -1))
    near = (jnp.abs(row - 1 - query // 32) <= 1) & (jnp.abs(col - query % 32) <= 1)
    mask_s[...] = jnp.where(near & (place < 12), row, 9)

    def tile_step(t, carry):
        base = pl.multiple_of(t * 128, 128)
        first = jnp.where(upper & (t == 0), 1, 0)
        last = jnp.where(jnp.logical_not(upper) & (t == tiles - 1), 4, 5)
        mask = (mask_s[...] >= first) & (mask_s[...] <= last)
        even = iota((128, 128), 1) < 64
        top = iota((128, 128), 0) < 64
        win, here = pl.ds(base, 192), pl.ds(base, 128)
        side = pl.ds(pl.multiple_of(t * 16, 16), 16)
        for pair in range(HEADS // 2):
            lanes = slice(pair * 128, pair * 128 + 128)
            q = q_s[here, lanes]
            do = do_s[here, lanes]
            zero = jnp.zeros_like(q)
            qm = jnp.concatenate([jnp.where(even, q, zero), jnp.where(even, zero, q)], 0)
            dom = jnp.concatenate([jnp.where(even, do, zero), jnp.where(even, zero, do)], 0)
            k = jnp.concatenate([k_s[win, lanes], kc_s[side, lanes]], 0)
            v = jnp.concatenate([v_s[win, lanes], vc_s[side, lanes]], 0)
            w = jnp.where(mask, jnp.exp(nt(k, qm)), 0.0)
            p = w * (1.0 / jnp.sum(w, axis=0, keepdims=True))
            dp = nt(v, dom)
            delta = jnp.sum(p * dp, axis=0, keepdims=True)
            ds = (p * (dp - delta)).astype(BF16)
            p = p.astype(BF16)
            out = tn(v, p)
            mixed_s[lanes, here] = jnp.where(top, out[:, 0:128], out[:, 128:256]).astype(BF16)
            dq = tn(k, ds) * scale
            dq_ref[lanes, here] = jnp.where(top, dq[:, 0:128], dq[:, 128:256]).astype(BF16)
            dk, dv = nn(ds, qm), nn(p, dom)
            dk_s[win, lanes] += dk[0:192]
            dv_s[win, lanes] += dv[0:192]
            dkc_s[side, lanes] = dk[192:KEYS].astype(BF16)
            dvc_s[side, lanes] = dv[192:KEYS].astype(BF16)
        return carry

    lax.fori_loop(0, tiles, tile_step, 0)

    row_at = pl.multiple_of(jnp.where(upper, 32 + points, 0), 32)
    dkh = jnp.concatenate([dk_s[pl.ds(row_at, 32), :], tn(spread_cols, dkc_s[...])], 0).astype(BF16)
    dvh = jnp.concatenate([dv_s[pl.ds(row_at, 32), :], tn(spread_cols, dvc_s[...])], 0).astype(BF16)
    dkh_ref[...] = dkh
    dvh_ref[...] = dvh
    dk_ref[...] = dk_s[32 : 32 + points, :].astype(BF16)
    dv_ref[...] = dv_s[32 : 32 + points, :].astype(BF16)
    wk, wv = (w_ref[:, i * width : (i + 1) * width] for i in (1, 2))
    back = (nt(dkh, wk) + nt(dvh, wv)).astype(BF16)
    brow_ref[...] = back[0:32]
    for ref, at in ((bleft_ref, 32), (bright_ref, 64)):
        ref[0:32, :] = back[at : at + 32]
        ref[32:48, :] = back[CORNER:HALO]
    wq, wk, wv = (w_all[1, :, i * width : (i + 1) * width] for i in range(3))
    dw_ref[0:width, :] = nn(dq_ref[...], normal).astype(BF16)
    dw_ref[width : 2 * width, :] = (tn(dk_ref[...], normal) + tn(dkh_ref[...], halo)).astype(BF16)
    dw_ref[2 * width : 3 * width, :] = (
        tn(dv_ref[...], normal) + tn(dvh_ref[...], halo)
    ).astype(BF16)
    dw_ref[3 * width : 4 * width, :] = nn(mixed_s[...], cot).astype(BF16)
    both_ref[:, 0:width] = (tt(dq_ref[...], wq) + nt(dk_ref[...], wk) + nt(dv_ref[...], wv)).astype(BF16)


def third_kernel(
    lat_ref, order_ref, n0, n1, n2, n3, n4, n5, q_ref, kv_ref, p_ref, mixed_ref, h_ref, both_ref,
    packs_ref, wt_ref, wo_ref, gain_ref, dw_in,
    dh_ref, d0, d1, d2, d3, d4, d5, dw_ref, other_ref,
    dw_s, dmix_s, dkv_s, dq_s, dp_s, n_s,
):
    width, tile = q_ref.shape
    head = width // HEADS
    scale = head**-0.5
    blocks = (n0, n1, n2, n3, n4, n5)
    outs = (d0, d1, d2, d3, d4, d5)
    step = pl.program_id(0)

    @pl.when(step == 0)
    def _():
        dw_s[...] = jnp.zeros_like(dw_s) if dw_in is None else dw_in[...]

    token = order_ref[...]
    both = picked(token, both_ref[...])
    dn = both[:, 0:width]
    if packs_ref is not None:
        brow = jnp.where(lat_ref[0] == 0, 31, 0)
        r, c, slot = token // 32, token % 32, iota((tile, RETURNED), 1)
        border = r == brow
        place = one_hot(
            (border & (slot < 32) & (slot == c))
            | ((c == 0) & (slot < 64) & (slot == 32 + r))
            | ((c == 31) & (slot < 112) & (slot == 80 + r))
            | (border & (c == 0) & (slot == 128 + 33))
            | (border & (c == 31) & (slot == 176 + 32))
        )
        dn = dn + nn(place, packs_ref[...])
    dh = norm_back(h_ref[...].astype(F32), gain_ref[1:2, :], dn)
    dh_ref[...] = dh
    dh = dh + both[:, width : 2 * width]
    dhb = dh.astype(BF16)
    dmix_s[...] = nt(wo_ref[...], dhb)
    dw_s[3 * width : 4 * width, :] += nn(mixed_ref[...], dhb)
    for h in range(HEADS):
        lo, hi = h * head, (h + 1) * head
        dmix = dmix_s[lo:hi, :]
        delta = jnp.zeros((1, tile), F32)
        for b in range(len(blocks)):
            dp = jnp.sum(
                dmix * kv_ref[b, width + lo : width + hi, :].astype(F32), axis=0, keepdims=True
            )
            dp_s[b : b + 1, :] = dp
            delta = delta + p_ref[b, h : h + 1, :] * dp
        q = q_ref[lo:hi, :].astype(F32)
        dq = jnp.zeros((head, tile), F32)
        for b in range(len(blocks)):
            p = p_ref[b, h : h + 1, :]
            ds = p * (dp_s[b : b + 1, :] - delta) * scale
            dq = dq + ds * kv_ref[b, lo:hi, :].astype(F32)
            here = slice(b * tile, (b + 1) * tile)
            dkv_s[lo:hi, here] = (ds * q).astype(BF16)
            dkv_s[width + lo : width + hi, here] = (p * dmix).astype(BF16)
        dq_s[lo:hi, :] = dq.astype(BF16)
    dq = dq_s[...]
    dw_s[0:width, :] += nn(dq, n0[...])
    for b, ref in enumerate(blocks):
        n_s[b * tile : (b + 1) * tile, :] = ref[...]
    dw_s[width : 3 * width, :] += nn(dkv_s[...], n_s[...])
    grads = tn(dkv_s[...], wt_ref[width : 3 * width])
    outs[0][...] = grads[0:tile] + tn(dq, wt_ref[0:width])
    for b in range(1, len(blocks)):
        outs[b][...] = grads[b * tile : (b + 1) * tile].astype(BF16)

    @pl.when(step == pl.num_programs(0) - 1)
    def _():
        if other_ref is None:
            dw_ref[...] = dw_s[...]
        else:
            write_halves(lat_ref[0], dw_s, dw_ref, other_ref)


def last_kernel(place_ref, vis_ref, gain_ref, cot_ref, *refs):
    inputs, out_ref, high_s, low_s = refs[:-3], refs[-3], refs[-2], refs[-1]
    points, width = cot_ref.shape
    tile = 256
    at = 0
    while inputs:
        start_ref, dh_ref, own_ref, far_ref, near_ref = inputs[:5]
        for lo in range(0, start_ref.shape[0], tile):
            rows = slice(lo, lo + tile)
            dn = own_ref[rows] + far_ref[rows].astype(F32) + near_ref[rows].astype(F32)
            back = norm_back(start_ref[rows].astype(F32), gain_ref[0:1, :], dn)
            grad = dh_ref[rows] + back
            high = grad.astype(BF16)
            high_s[at : at + tile, :] = high
            low_s[at : at + tile, :] = (grad - high.astype(F32)).astype(BF16)
            at += tile
        inputs = inputs[5:]
    for lo in range(0, points, tile):
        rows = slice(lo, lo + tile)
        place = place_ref[rows, :]
        shown = shown_column(vis_ref[...], lo + iota((tile, 1), 0))
        grad = picked(place, high_s[...]) + picked(place, low_s[...]) + cot_ref[rows]
        out_ref[rows] = jnp.where(shown > 0.5, grad, 0.0)


def weights_kernel(
    factor, pieces, lat_ref, mine_ref, other_ref, wt_ref, gain_ref,
    qkv_ref, out_ref, gain_out_ref, rows_s,
):
    total, width = mine_ref.shape
    piece = total // pieces // 2
    lat = lat_ref[0]
    for ref, band in ((mine_ref, lat), (other_ref, 1 - lat)):
        for k in range(pieces):
            at = pl.multiple_of(band * (total // 2) + k * piece, 8)
            for layer in range(2):
                lo = (2 * k + layer) * piece
                rows_s[layer, pl.ds(at, piece), :] = ref[lo : lo + piece, :].astype(F32) * factor
    for layer in range(2):
        acc = jnp.zeros((1, width), F32)
        for i in range(3):
            lo, hi = i * width, (i + 1) * width
            grad = rows_s[layer, lo:hi, :]
            weight = wt_ref[layer, lo:hi, :].astype(F32)
            acc = acc + jnp.sum(weight * grad, axis=0, keepdims=True)
            qkv_ref[layer, :, lo:hi] = grad.T
        out_ref[layer] = rows_s[layer, 3 * width : 4 * width, :]
        gain_out_ref[layer : layer + 1, :] = acc / gain_ref[layer : layer + 1, :]


def call(
    kernel, out_shape, scratch=(), grid=None, in_specs=None, out_specs=None, us=1, aliases=None, mib=12
):
    return pl.pallas_call(
        kernel,
        out_shape=out_shape,
        grid_spec=pltpu.PrefetchScalarGridSpec(
            num_scalar_prefetch=0,
            grid=grid or (),
            in_specs=in_specs,
            out_specs=out_specs,
            scratch_shapes=list(scratch),
        ),
        input_output_aliases=aliases or {},
        cost_estimate=pl.CostEstimate(
            flops=int(us * 1e6 * 800), bytes_accessed=int(us * 1e6), transcendentals=0
        ),
        compiler_params=pltpu.CompilerParams(vmem_limit_bytes=mib * 1024 * 1024),
    )


def whole():
    return pl.BlockSpec(memory_space=pltpu.VMEM)


def scalar():
    return pl.BlockSpec(memory_space=pltpu.SMEM)


def fixed(shape):
    return pl.BlockSpec(shape, lambda i: (0,) * len(shape))


def token_spec(tile, width, first=0):
    at = first // tile
    return pl.BlockSpec((tile, width), lambda i: (i + at, 0))


def layer_spec(layer, rows, width):
    return pl.BlockSpec((None, rows, width), lambda i: (layer, 0, 0))


CHUNKS = 2
FORWARD_TILE = 256
BACKWARD_TILE = 256


def run_first(first, lat, order, blocks, start, wt, output_weight, norm_gain_table):
    size, width = start.shape
    tile = min(FORWARD_TILE, size)
    struct = jax.ShapeDtypeStruct
    part = struct((size, width), BF16)
    tok_spec = token_spec(tile, width)
    feat_spec = pl.BlockSpec((width, tile), lambda i: (0, i))
    at = first // tile
    return call(
        first_kernel,
        (
            struct((width, size), BF16),
            struct((6, 2 * width, size), BF16),
            struct((6, 8, size), F32),
            struct((width, size), BF16),
            part,
            part,
            *[struct((32, width), BF16)] * 3,
        ),
        grid=(size // tile,),
        in_specs=[scalar(), pl.BlockSpec((1, tile), lambda i: (0, i + at))]
        + [tok_spec] * 7
        + [
            layer_spec(0, 3 * width, width),
            layer_spec(0, width, width),
            fixed((2, width)),
        ],
        out_specs=(
            feat_spec,
            pl.BlockSpec((6, 2 * width, tile), lambda i: (0, 0, i)),
            pl.BlockSpec((6, 8, tile), lambda i: (0, 0, i)),
            feat_spec,
            tok_spec,
            tok_spec,
            *[fixed((32, width))] * 3,
        ),
        scratch=[pltpu.VMEM((6, 8, tile), F32), pltpu.VMEM((96, width), F32)],
        mib=LARGE_MIB,
        us=8,
    )(lat, order, *blocks, start, wt, output_weight, norm_gain_table)


def run_second(lat, places, normals, halos, query_key_value_weight, output_weight, cot):
    points, width = cot.shape
    struct = jax.ShapeDtypeStruct
    ext, slots = points + 64, points // 8
    across = pltpu.VMEM((width, points), BF16)
    every, halo = pltpu.VMEM((points, width), BF16), pltpu.VMEM((HALO, width), BF16)
    return call(
        second_kernel,
        (
            struct((points, 2 * width), BF16),
            struct((4 * width, width), BF16),
            struct((32, width), BF16),
            struct((48, width), BF16),
            struct((48, width), BF16),
        ),
        in_specs=[scalar()] + [whole()] * 11,
        out_specs=(whole(),) * 5,
        scratch=[
            across, every, every, across,
            *[halo] * 3,
            every,
            pltpu.VMEM((ext, width), BF16),
            pltpu.VMEM((ext, width), BF16),
            *[pltpu.VMEM((slots, width), BF16)] * 2,
            pltpu.VMEM((ext, width), F32),
            pltpu.VMEM((ext, width), F32),
            *[pltpu.VMEM((slots, width), BF16)] * 2,
            every,
            pltpu.VMEM((KEYS, 256), jnp.int32),
            every,
        ],
        mib=LARGE_MIB,
        us=22,
    )(lat, places, *normals, *halos, query_key_value_weight, output_weight, cot)


def inner_third_kernel(*refs):
    third_kernel(*refs[:14], None, *refs[14:17], None, *refs[17:25], None, *refs[25:])


def run_third(
    first, lat, order, blocks, kept, both, packs, wt, output_weight, norm_gain_table, weights
):
    q0, kv0, p0, mixed0, h1 = kept
    size, width = h1.shape
    points = both.shape[0]
    tile = min(BACKWARD_TILE, size)
    struct = jax.ShapeDtypeStruct
    part = struct((size, width), BF16)
    tok_spec = token_spec(tile, width)
    feat_spec = pl.BlockSpec((width, tile), lambda i: (0, i))
    final = packs is not None
    whole_dw, half_dw = (4 * width, width), (2 * width, width)
    return call(
        third_kernel if final else inner_third_kernel,
        (
            struct((size, width), F32),
            struct((size, width), F32),
            *[part] * 5,
            *([struct(half_dw, BF16)] * 2 if final else [struct(whole_dw, F32)]),
        ),
        grid=(size // tile,),
        in_specs=[scalar(), token_spec(tile, 1, first)]
        + [tok_spec] * 6
        + [
            feat_spec,
            pl.BlockSpec((6, 2 * width, tile), lambda i: (0, 0, i)),
            pl.BlockSpec((6, 8, tile), lambda i: (0, 0, i)),
            feat_spec,
            tok_spec,
        ]
        + [fixed((points, 2 * width))]
        + [fixed((RETURNED, width))] * final
        + [
            layer_spec(0, 3 * width, width),
            layer_spec(0, width, width),
            fixed((2, width)),
        ]
        + [fixed(whole_dw)] * final,
        out_specs=(*[tok_spec] * 7, *([fixed(half_dw)] * 2 if final else [fixed(whole_dw)])),
        scratch=[
            pltpu.VMEM(whole_dw, F32),
            pltpu.VMEM((width, tile), F32),
            pltpu.VMEM((2 * width, 6 * tile), BF16),
            pltpu.VMEM((width, tile), BF16),
            pltpu.VMEM((8, tile), F32),
            pltpu.VMEM((6 * tile, width), BF16),
        ],
        mib=LARGE_MIB,
        us=13,
    )(
        lat, order, *blocks, q0, kv0, p0, mixed0, h1, both, *([packs] if final else []), wt,
        output_weight, norm_gain_table, *([weights] if final else []),
    )


def local(
    tokens, visible, mask_token, norm_gain_table, query_key_value_weight, output_weight, cotangent
):
    rows, cols, width = tokens.shape
    points = rows * cols
    size = points // CHUNKS
    firsts = [c * size for c in range(CHUNKS)]
    lat_count, lon_count = lax.axis_size("lat"), lax.axis_size("lon")
    lat = lax.axis_index("lat").astype(jnp.int32).reshape(1)
    wt = jnp.swapaxes(query_key_value_weight, 1, 2)
    struct = jax.ShapeDtypeStruct
    tokens = tokens.reshape(points, width)
    cot = cotangent.reshape(points, width)
    part = struct((size, width), BF16)
    gain_spec = fixed((2, width))
    wt_spec, wo_spec = layer_spec(0, 3 * width, width), layer_spec(0, width, width)

    order, places = token_order(rows, cols)
    order_row = jnp.asarray(order.reshape(1, points))
    order, places = jnp.asarray(order.reshape(points, 1)), jnp.asarray(places.reshape(points, 1))

    small = 256
    starts, normals = [], []
    for first in firsts:
        start, normal = call(
            start_kernel,
            (part, part),
            grid=(size // small,),
            in_specs=[
                token_spec(small, 1, first),
                fixed((points, width)),
                fixed((rows, cols)),
                fixed((width,)),
                gain_spec,
            ],
            out_specs=(token_spec(small, width),) * 2,
            mib=LARGE_MIB,
            us=2,
        )(order, tokens, visible, mask_token, norm_gain_table)
        starts.append(start)
        normals.append(normal)

    swapped0 = lon_swap(normals[0])
    own1, swapped0 = chained(normals[1], swapped0)
    swapped1 = lon_swap(own1)
    beyond0, beyond1 = lon_forward(swapped0), lon_forward(swapped1)
    near0, near1 = lat_swap(normals[0]), lat_swap(own1)

    def blocks_of(own, near, swapped, beyond):
        return [own, near, swapped, beyond, lat_swap(swapped), lat_swap(beyond)]

    blocks = [blocks_of(normals[0], near0, swapped0, beyond0), None]

    kept = []
    for c in range(CHUNKS):
        *keep, normal1, row, left, right = run_first(
            firsts[c], lat, order_row, blocks[c], starts[c], wt, output_weight, norm_gain_table
        )
        if c == 1:
            keep, normal1, halos = lax.optimization_barrier((keep, normal1, halos))
            halos = [*halos, lat_swap(halos[1]), lat_swap(halos[2])]
        kept.append((keep, normal1))
        if c == 0:
            beyond1, row, left, right = lax.optimization_barrier((beyond1, row, left, right))
            halos = [lat_swap(row), from_left(right), from_right(left)]
            blocks[1] = blocks_of(own1, near1, swapped1, beyond1)

    both1, dw1, brow, bleft, bright = run_second(
        lat, places, [kept[0][1], kept[1][1]], halos, query_key_value_weight, output_weight, cot
    )

    from_l, from_r, brow = from_left(bright), from_right(bleft), lat_swap(brow)
    stages = lon_factors()
    sum1 = halves_summed(
        lax.dynamic_slice_in_dim(dw1, lat[0] * 2 * width, 2 * width, 0),
        lax.dynamic_slice_in_dim(dw1, (1 - lat[0]) * 2 * width, 2 * width, 0),
    )
    both1, sum1 = chained(both1, sum1)
    border = (brow, from_l, from_r)

    def plus(a, b):
        return (a.astype(F32) + b.astype(F32)).astype(BF16)

    weights = packs = None
    sum_stages = list(stages)
    ends = []
    coming = returned = None
    for n, c in enumerate(range(CHUNKS)[::-1]):
        dh1, d0, d1, d2, d3, d4, d5, *weights = run_third(
            firsts[c], lat, order, blocks[c], kept[c][0], both1, packs, wt,
            output_weight, norm_gain_table, weights,
        )
        if n == 0:
            sum1 = stage_summed(sum1, sum_stages.pop(0))
        border, weights, sum1, d1, d2, d3, d4, d5, coming, returned = lax.optimization_barrier(
            (border, weights, sum1, d1, d2, d3, d4, d5, coming, returned)
        )
        if n == 0:
            brow, from_l, from_r = border
            packs = jnp.concatenate([brow, from_l, from_r, lat_swap(from_l), lat_swap(from_r)], 0)
        d3 = plus(d3, lat_swap(d5))
        d2 = plus(d2, lat_swap(d4))
        d1 = lat_swap(d1)
        if n == CHUNKS - 1:
            weights = [halves_summed(*weights)]
        weights, d1, d2, d3 = lax.optimization_barrier((weights, d1, d2, d3))
        if returned is not None:
            ends[-2][-1] = returned
        returned = None
        if coming is not None:
            returned = lon_swap(coming)
        coming = plus(d2, lon_backward(d3))
        weights = weights[0]
        ends.append([c, dh1, d0, d1, None])

    sum0 = stage_summed(weights, stages[0])
    for stage in sum_stages:
        sum1 = stage_summed(sum1, stage)
    sum0, sum1, coming, returned = lax.optimization_barrier((sum0, sum1, coming, returned))
    ends[-2][-1] = returned
    returned = lon_swap(coming)
    sum0 = stage_summed(sum0, stages[1])
    sum0, returned = lax.optimization_barrier((sum0, returned))
    ends[-1][-1] = returned
    for stage in stages[2:]:
        sum0 = stage_summed(sum0, stage)
    sums = jnp.concatenate([sum0, sum1], 0)
    for stage in stages[::-1]:
        sums = spread(sums, *stage)

    pieces = []
    for c, dh1, d0, near, far in ends:
        pieces.append((c, [starts[c], dh1, d0, far, near]))
    pieces = [array for _, arrays in sorted(pieces, key=lambda p: p[0]) for array in arrays]
    grad_tokens = call(
        last_kernel,
        struct((points, width), F32),
        in_specs=[whole()] * (4 + len(pieces)),
        out_specs=whole(),
        scratch=[pltpu.VMEM((points, width), BF16)] * 2,
        mib=LARGE_MIB,
        us=6,
    )(places, visible, norm_gain_table, cot, *pieces)
    sums, grad_tokens = chained(sums, grad_tokens)
    other = lat_swap(sums)
    factor = (points * lat_count * lon_count) ** (-0.5)
    g_qkv, g_out, g_gain = call(
        functools.partial(weights_kernel, factor, lon_count),
        (
            struct((2, width, 3 * width), F32),
            struct((2, width, width), F32),
            struct((2, width), F32),
        ),
        in_specs=[scalar()] + [whole()] * 4,
        out_specs=(whole(),) * 3,
        scratch=[pltpu.VMEM((2, 4 * width, width), F32)],
        mib=20,
        us=5,
    )(lat, sums, other, wt, norm_gain_table)
    return grad_tokens.reshape(rows, cols, width), g_qkv, g_out, g_gain


def without(kernel, at, count, *refs):
    kernel(*refs[:at], *[None] * count, *refs[at:])


def solution(mesh):
    return jax.shard_map(
        local,
        mesh=mesh,
        in_specs=(
            P(("group", "lat"), "lon", None),
            P(("group", "lat"), "lon"),
            P(),
            P(),
            P(),
            P(),
            P(("group", "lat"), "lon", None),
        ),
        out_specs=(
            P(("group", "lat"), "lon", None),
            P("group", None, None),
            P("group", None, None),
            P("group", None),
        ),
        check_vma=False,
    )
```

```python
import functools

import jax
import jax.numpy as jnp
import numpy as np
from jax import lax
from jax.experimental import pallas as pl
from jax.experimental.pallas import tpu as pltpu
from jax.sharding import PartitionSpec as P

HEADS = 6
EPS = 1e-05
F32 = jnp.float32
BF16 = jnp.bfloat16
LARGE_MIB = 56
HALO = 112
CORNER = 96
KEYS = 208
RETURNED = 224


def nn(a, b):
    return lax.dot_general(a, b, (((1,), (0,)), ((), ())), preferred_element_type=F32)


def nt(a, b):
    return lax.dot_general(a, b, (((1,), (1,)), ((), ())), preferred_element_type=F32)


def tn(a, b):
    return lax.dot_general(a, b, (((0,), (0,)), ((), ())), preferred_element_type=F32)


def tt(a, b):
    return lax.dot_general(a, b, (((0,), (1,)), ((), ())), preferred_element_type=F32)


def iota(shape, dim):
    return lax.broadcasted_iota(jnp.int32, shape, dim)


def one_hot(condition):
    return jnp.where(condition, 1.0, 0.0).astype(BF16)


def permuted(value, axis, target):
    count = lax.axis_size(axis)
    return lax.ppermute(value, axis, [(i, target(i) % count) for i in range(count)])


def lat_swap(value):
    return permuted(value, "lat", lambda i: i ^ 1)


def lon_swap(value):
    return permuted(value, "lon", lambda i: i ^ 1)


def lon_forward(value):
    return permuted(value, "lon", lambda i: i + 2 if i % 2 == 0 else i - 2)


def lon_backward(value):
    return permuted(value, "lon", lambda i: i - 2 if i % 2 == 0 else i + 2)


def from_left(value):
    return permuted(value, "lon", lambda i: i + 1)


def from_right(value):
    return permuted(value, "lon", lambda i: i - 1)


def chained(value, after):
    return lax.optimization_barrier((value, after))


def exchanged(parts, axis_stride, factor):
    count = lax.axis_size("lon")
    digit = (lax.axis_index("lon") // axis_stride) % factor
    moved = []
    for d in range(1, factor):
        pairs = [(i, shifted(i, axis_stride, factor, d)) for i in range(count)]
        moved.append(lax.ppermute(parts(digit ^ d), "lon", pairs))
    total = parts(digit).astype(F32)
    for piece in moved:
        total = total + piece.astype(F32)
    return total.astype(BF16)


def shifted(i, stride, factor, d):
    digit = (i // stride) % factor
    return i + ((digit ^ d) - digit) * stride


def spread(value, axis_stride, factor):
    count = lax.axis_size("lon")
    digit = (lax.axis_index("lon") // axis_stride) % factor
    rows = value.shape[0]
    full = jnp.zeros((factor * rows,) + value.shape[1:], value.dtype)
    full = lax.dynamic_update_slice(full, value, (digit * rows, 0))
    for d in range(1, factor):
        pairs = [(i, shifted(i, axis_stride, factor, d)) for i in range(count)]
        got = lax.ppermute(value, "lon", pairs)
        at = (digit ^ d) * rows
        full = lax.dynamic_update_slice(full, got, (at, 0))
    return full


def lon_factors():
    left = lax.axis_size("lon")
    stride, out = 1, []
    for factor in [2] + [4] * 10:
        if left == 1:
            break
        factor = min(factor, left)
        out.append((stride, factor))
        stride, left = stride * factor, left // factor
    return out


def halves_summed(mine, other):
    return (mine.astype(F32) + lat_swap(other).astype(F32)).astype(BF16)


def stage_summed(value, stage):
    stride, factor = stage
    size = value.shape[0] // factor
    return exchanged(
        lambda k: lax.dynamic_slice_in_dim(value, k * size, size, 0), stride, factor
    )


def norm_parts(x):
    mean = jnp.mean(x, axis=-1, keepdims=True)
    centred = x - mean
    spread = jnp.mean(centred * centred, axis=-1, keepdims=True)
    rstd = lax.rsqrt(spread + EPS)
    return centred * rstd, rstd


def norm_back(x, gain, grad_normal):
    xhat, rstd = norm_parts(x)
    g = grad_normal * gain
    return rstd * (
        g - jnp.mean(g, axis=-1, keepdims=True) - xhat * jnp.mean(g * xhat, axis=-1, keepdims=True)
    )


def shown_column(visible, token):
    rows, cols = visible.shape
    tile = token.shape[0]
    of_row = nn(one_hot(token // cols == iota((tile, rows), 1)), visible.astype(F32).astype(BF16))
    mine = token % cols == iota((tile, cols), 1)
    return jnp.sum(jnp.where(mine, of_row, 0.0), axis=1, keepdims=True)


def token_order(rows, cols):
    row, col = np.divmod(np.arange(rows * cols), cols)
    border = (row == 0) | (row == rows - 1) | (col == 0) | (col == cols - 1)
    order = np.argsort(~border, kind="stable").astype(np.int32)
    return order, np.argsort(order, kind="stable").astype(np.int32)


def picked(places, values):
    count = values.shape[0]
    return nn(one_hot(places == iota((places.shape[0], count), 1)), values)


def start_kernel(order_ref, tok_ref, vis_ref, mask_ref, gain_ref, start_ref, normal_ref):
    width = tok_ref.shape[1]
    token = order_ref[...]
    shown = shown_column(vis_ref[...], token)
    x = jnp.where(
        shown > 0.5, picked(token, tok_ref[...]), mask_ref[...].astype(F32).reshape(1, width)
    )
    start_ref[...] = x.astype(BF16)
    xhat, _ = norm_parts(x)
    normal_ref[...] = (xhat * gain_ref[0:1, :]).astype(BF16)


def first_kernel(
    lat_ref, order_ref, n0, n1, n2, n3, n4, n5, start_ref,
    wt_ref, wo_ref, gain_ref,
    q_ref, kv_ref, p_ref, mixed_ref, h_ref, normal_ref, row_ref, left_ref, right_ref,
    w_s, pack_s,
):
    width, tile = q_ref.shape
    head = width // HEADS
    blocks = (n0, n1, n2, n3, n4, n5)
    q_ref[...] = nt(wt_ref[0:width], n0[...]).astype(BF16)
    for b, ref in enumerate(blocks):
        kv_ref[b] = nt(wt_ref[width : 3 * width], ref[...]).astype(BF16)
    for h in range(HEADS):
        lo, hi = h * head, (h + 1) * head
        q = q_ref[lo:hi, :].astype(F32) * (head**-0.5)
        total = jnp.zeros((1, tile), F32)
        out = jnp.zeros((head, tile), F32)
        for b in range(len(blocks)):
            k = kv_ref[b, lo:hi, :].astype(F32)
            w = jnp.exp(jnp.sum(q * k, axis=0, keepdims=True))
            w_s[b, h : h + 1, :] = w
            total = total + w
            out = out + w * kv_ref[b, width + lo : width + hi, :].astype(F32)
        inverse = 1.0 / total
        for b in range(len(blocks)):
            p_ref[b, h : h + 1, :] = w_s[b, h : h + 1, :] * inverse
        mixed_ref[lo:hi, :] = (out * inverse).astype(BF16)
    h1 = start_ref[...].astype(F32) + tn(mixed_ref[...], wo_ref[...])
    h1 = h1.astype(BF16)
    h_ref[...] = h1
    xhat, _ = norm_parts(h1.astype(F32))
    normal = (xhat * gain_ref[1:2, :]).astype(BF16)
    normal_ref[...] = normal
    step = pl.program_id(0)
    brow = jnp.where(lat_ref[0] == 0, 31, 0)
    slot = iota((96, tile), 0)
    r, c = order_ref[...] // 32, order_ref[...] % 32
    pick = one_hot(
        ((slot < 32) & (r == brow) & (c == slot))
        | ((slot >= 32) & (slot < 64) & (c == 0) & (r == slot - 32))
        | ((slot >= 64) & (c == 31) & (r == slot - 64))
    )

    @pl.when(step == 0)
    def _():
        pack_s[...] = jnp.zeros_like(pack_s)

    pack_s[...] += nn(pick, normal)

    @pl.when(step == pl.num_programs(0) - 1)
    def _():
        for i, ref in enumerate((row_ref, left_ref, right_ref)):
            ref[...] = pack_s[i * 32 : i * 32 + 32, :].astype(BF16)


def write_halves(lat, total_ref, mine_ref, other_ref):
    half = mine_ref.shape[0]
    for band in range(2):

        @pl.when(lat == band)
        def _():
            mine_ref[...] = total_ref[band * half : (band + 1) * half, :].astype(BF16)
            other_ref[...] = total_ref[(1 - band) * half : (2 - band) * half, :].astype(BF16)


def second_kernel(
    lat_ref, place_ref, na_ref, nb_ref, row_ref, left_ref, right_ref, dleft_ref, dright_ref,
    w_all, wo_all, cot_ref,
    both_ref, dw_ref, brow_ref, bleft_ref, bright_ref,
    dq_ref, dk_ref, dv_ref, mixed_s, dkh_ref, dvh_ref, halo_s,
    q_s, k_s, v_s, kc_s, vc_s, dk_s, dv_s, dkc_s, dvc_s, do_s, mask_s, normal_s,
):
    points, width = cot_ref.shape
    head = width // HEADS
    w_ref, wo_ref = w_all.at[1], wo_all.at[1]
    upper = lat_ref[0] == 0
    halo_s[0:32, :] = row_ref[...]
    halo_s[32:64, :] = left_ref[...]
    halo_s[64:96, :] = right_ref[...]
    a, b = iota((16, 32), 0), iota((16, 32), 1)
    sent = b == jnp.where(upper, 0, 31)
    corners = nn(one_hot(sent & (a == 0)), dleft_ref[...])
    corners += nn(one_hot(sent & (a == 1)), dright_ref[...])
    halo_s[CORNER:HALO, :] = corners.astype(BF16)
    halo = halo_s[...]
    ordered = jnp.concatenate([na_ref[...], nb_ref[...]], 0)
    for at in range(0, points, 256):
        rows = slice(at, at + 256)
        normal_s[rows, :] = picked(place_ref[rows, :], ordered).astype(BF16)
    normal = normal_s[...]
    scale = head**-0.5
    q_s[...] = (nn(normal, w_ref[:, 0:width]).astype(BF16).astype(F32) * scale).astype(BF16)
    k_s[32 : 32 + points, :] = nn(normal, w_ref[:, width : 2 * width]).astype(BF16)
    v_s[32 : 32 + points, :] = nn(normal, w_ref[:, 2 * width : 3 * width]).astype(BF16)
    kh = nn(halo, w_ref[:, width : 2 * width]).astype(BF16)
    vh = nn(halo, w_ref[:, 2 * width : 3 * width]).astype(BF16)
    for at in (0, 32 + points):
        k_s[at : at + 32, :] = kh[0:32]
        v_s[at : at + 32, :] = vh[0:32]
    tiles = points // 128
    slots = tiles * 16
    a, b = iota((slots, HALO - 32), 0), iota((slots, HALO - 32), 1)
    place, is_right = a % 16, jnp.where(a % 16 >= 6, 1, 0)
    ext_row = 4 * (a // 16) + place - 6 * is_right
    inner = (ext_row >= 1) & (ext_row <= 32)
    source = jnp.where(inner, 32 * is_right + ext_row - 1, 64 + is_right)
    spread_cols = one_hot((place < 12) & (b == source))
    kc_s[...] = nn(spread_cols, kh[32:HALO]).astype(BF16)
    vc_s[...] = nn(spread_cols, vh[32:HALO]).astype(BF16)
    dk_s[...] = jnp.zeros_like(dk_s)
    dv_s[...] = jnp.zeros_like(dv_s)
    cot = cot_ref[...].astype(BF16)
    both_ref[:, width : 2 * width] = cot
    do_s[...] = nt(cot, wo_ref[...]).astype(BF16)

    key, query = iota((KEYS, 256), 0), iota((KEYS, 256), 1) % 128
    place = key - 192
    right = place >= 6
    row = jnp.where(place < 0, key // 32, jnp.where(right, place - 6, place))
    col = jnp.where(place < 0, key % 32, jnp.where(right, 32, -1))
    near = (jnp.abs(row - 1 - query // 32) <= 1) & (jnp.abs(col - query % 32) <= 1)
    mask_s[...] = jnp.where(near & (place < 12), row, 9)

    def tile_step(t, carry):
        base = pl.multiple_of(t * 128, 128)
        first = jnp.where(upper & (t == 0), 1, 0)
        last = jnp.where(jnp.logical_not(upper) & (t == tiles - 1), 4, 5)
        mask = (mask_s[...] >= first) & (mask_s[...] <= last)
        even = iota((128, 128), 1) < 64
        top = iota((128, 128), 0) < 64
        win, here = pl.ds(base, 192), pl.ds(base, 128)
        side = pl.ds(pl.multiple_of(t * 16, 16), 16)
        for pair in range(HEADS // 2):
            lanes = slice(pair * 128, pair * 128 + 128)
            q = q_s[here, lanes]
            do = do_s[here, lanes]
            zero = jnp.zeros_like(q)
            qm = jnp.concatenate([jnp.where(even, q, zero), jnp.where(even, zero, q)], 0)
            dom = jnp.concatenate([jnp.where(even, do, zero), jnp.where(even, zero, do)], 0)
            k = jnp.concatenate([k_s[win, lanes], kc_s[side, lanes]], 0)
            v = jnp.concatenate([v_s[win, lanes], vc_s[side, lanes]], 0)
            w = jnp.where(mask, jnp.exp(nt(k, qm)), 0.0)
            p = w * (1.0 / jnp.sum(w, axis=0, keepdims=True))
            dp = nt(v, dom)
            delta = jnp.sum(p * dp, axis=0, keepdims=True)
            ds = (p * (dp - delta)).astype(BF16)
            p = p.astype(BF16)
            out = tn(v, p)
            mixed_s[lanes, here] = jnp.where(top, out[:, 0:128], out[:, 128:256]).astype(BF16)
            dq = tn(k, ds) * scale
            dq_ref[lanes, here] = jnp.where(top, dq[:, 0:128], dq[:, 128:256]).astype(BF16)
            dk, dv = nn(ds, qm), nn(p, dom)
            dk_s[win, lanes] += dk[0:192]
            dv_s[win, lanes] += dv[0:192]
            dkc_s[side, lanes] = dk[192:KEYS].astype(BF16)
            dvc_s[side, lanes] = dv[192:KEYS].astype(BF16)
        return carry

    lax.fori_loop(0, tiles, tile_step, 0)

    row_at = pl.multiple_of(jnp.where(upper, 32 + points, 0), 32)
    dkh = jnp.concatenate([dk_s[pl.ds(row_at, 32), :], tn(spread_cols, dkc_s[...])], 0).astype(BF16)
    dvh = jnp.concatenate([dv_s[pl.ds(row_at, 32), :], tn(spread_cols, dvc_s[...])], 0).astype(BF16)
    dkh_ref[...] = dkh
    dvh_ref[...] = dvh
    dk_ref[...] = dk_s[32 : 32 + points, :].astype(BF16)
    dv_ref[...] = dv_s[32 : 32 + points, :].astype(BF16)
    wk, wv = (w_ref[:, i * width : (i + 1) * width] for i in (1, 2))
    back = (nt(dkh, wk) + nt(dvh, wv)).astype(BF16)
    brow_ref[...] = back[0:32]
    for ref, at in ((bleft_ref, 32), (bright_ref, 64)):
        ref[0:32, :] = back[at : at + 32]
        ref[32:48, :] = back[CORNER:HALO]
    wq, wk, wv = (w_all[1, :, i * width : (i + 1) * width] for i in range(3))
    dw_ref[0:width, :] = nn(dq_ref[...], normal).astype(BF16)
    dw_ref[width : 2 * width, :] = (tn(dk_ref[...], normal) + tn(dkh_ref[...], halo)).astype(BF16)
    dw_ref[2 * width : 3 * width, :] = (
        tn(dv_ref[...], normal) + tn(dvh_ref[...], halo)
    ).astype(BF16)
    dw_ref[3 * width : 4 * width, :] = nn(mixed_s[...], cot).astype(BF16)
    both_ref[:, 0:width] = (tt(dq_ref[...], wq) + nt(dk_ref[...], wk) + nt(dv_ref[...], wv)).astype(BF16)


def third_kernel(
    lat_ref, order_ref, n0, n1, n2, n3, n4, n5, q_ref, kv_ref, p_ref, mixed_ref, h_ref, both_ref,
    packs_ref, wt_ref, wo_ref, gain_ref, dw_in,
    dh_ref, d0, d1, d2, d3, d4, d5, dw_ref, other_ref,
    dw_s, dmix_s, dkv_s, dq_s, dp_s, n_s,
):
    width, tile = q_ref.shape
    head = width // HEADS
    scale = head**-0.5
    blocks = (n0, n1, n2, n3, n4, n5)
    outs = (d0, d1, d2, d3, d4, d5)
    step = pl.program_id(0)

    @pl.when(step == 0)
    def _():
        dw_s[...] = jnp.zeros_like(dw_s) if dw_in is None else dw_in[...]

    token = order_ref[...]
    both = picked(token, both_ref[...])
    dn = both[:, 0:width]
    if packs_ref is not None:
        brow = jnp.where(lat_ref[0] == 0, 31, 0)
        r, c, slot = token // 32, token % 32, iota((tile, RETURNED), 1)
        border = r == brow
        place = one_hot(
            (border & (slot < 32) & (slot == c))
            | ((c == 0) & (slot < 64) & (slot == 32 + r))
            | ((c == 31) & (slot < 112) & (slot == 80 + r))
            | (border & (c == 0) & (slot == 128 + 33))
            | (border & (c == 31) & (slot == 176 + 32))
        )
        dn = dn + nn(place, packs_ref[...])
    dh = norm_back(h_ref[...].astype(F32), gain_ref[1:2, :], dn)
    dh_ref[...] = dh
    dh = dh + both[:, width : 2 * width]
    dhb = dh.astype(BF16)
    dmix_s[...] = nt(wo_ref[...], dhb)
    dw_s[3 * width : 4 * width, :] += nn(mixed_ref[...], dhb)
    for h in range(HEADS):
        lo, hi = h * head, (h + 1) * head
        dmix = dmix_s[lo:hi, :]
        delta = jnp.zeros((1, tile), F32)
        for b in range(len(blocks)):
            dp = jnp.sum(
                dmix * kv_ref[b, width + lo : width + hi, :].astype(F32), axis=0, keepdims=True
            )
            dp_s[b : b + 1, :] = dp
            delta = delta + p_ref[b, h : h + 1, :] * dp
        q = q_ref[lo:hi, :].astype(F32)
        dq = jnp.zeros((head, tile), F32)
        for b in range(len(blocks)):
            p = p_ref[b, h : h + 1, :]
            ds = p * (dp_s[b : b + 1, :] - delta) * scale
            dq = dq + ds * kv_ref[b, lo:hi, :].astype(F32)
            here = slice(b * tile, (b + 1) * tile)
            dkv_s[lo:hi, here] = (ds * q).astype(BF16)
            dkv_s[width + lo : width + hi, here] = (p * dmix).astype(BF16)
        dq_s[lo:hi, :] = dq.astype(BF16)
    dq = dq_s[...]
    dw_s[0:width, :] += nn(dq, n0[...])
    for b, ref in enumerate(blocks):
        n_s[b * tile : (b + 1) * tile, :] = ref[...]
    dw_s[width : 3 * width, :] += nn(dkv_s[...], n_s[...])
    grads = tn(dkv_s[...], wt_ref[width : 3 * width])
    outs[0][...] = grads[0:tile] + tn(dq, wt_ref[0:width])
    for b in range(1, len(blocks)):
        outs[b][...] = grads[b * tile : (b + 1) * tile].astype(BF16)

    @pl.when(step == pl.num_programs(0) - 1)
    def _():
        if other_ref is None:
            dw_ref[...] = dw_s[...]
        else:
            write_halves(lat_ref[0], dw_s, dw_ref, other_ref)


def last_kernel(place_ref, vis_ref, gain_ref, cot_ref, *refs):
    inputs, out_ref, high_s, low_s = refs[:-3], refs[-3], refs[-2], refs[-1]
    points, width = cot_ref.shape
    tile = 256
    at = 0
    while inputs:
        start_ref, dh_ref, own_ref, far_ref, near_ref = inputs[:5]
        for lo in range(0, start_ref.shape[0], tile):
            rows = slice(lo, lo + tile)
            dn = own_ref[rows] + far_ref[rows].astype(F32) + near_ref[rows].astype(F32)
            back = norm_back(start_ref[rows].astype(F32), gain_ref[0:1, :], dn)
            grad = dh_ref[rows] + back
            high = grad.astype(BF16)
            high_s[at : at + tile, :] = high
            low_s[at : at + tile, :] = (grad - high.astype(F32)).astype(BF16)
            at += tile
        inputs = inputs[5:]
    for lo in range(0, points, tile):
        rows = slice(lo, lo + tile)
        place = place_ref[rows, :]
        shown = shown_column(vis_ref[...], lo + iota((tile, 1), 0))
        grad = picked(place, high_s[...]) + picked(place, low_s[...]) + cot_ref[rows]
        out_ref[rows] = jnp.where(shown > 0.5, grad, 0.0)


def weights_kernel(
    factor, pieces, lat_ref, mine_ref, other_ref, wt_ref, gain_ref,
    qkv_ref, out_ref, gain_out_ref, rows_s,
):
    total, width = mine_ref.shape
    piece = total // pieces // 2
    lat = lat_ref[0]
    for ref, band in ((mine_ref, lat), (other_ref, 1 - lat)):
        for k in range(pieces):
            at = pl.multiple_of(band * (total // 2) + k * piece, 8)
            for layer in range(2):
                lo = (2 * k + layer) * piece
                rows_s[layer, pl.ds(at, piece), :] = ref[lo : lo + piece, :].astype(F32) * factor
    for layer in range(2):
        acc = jnp.zeros((1, width), F32)
        for i in range(3):
            lo, hi = i * width, (i + 1) * width
            grad = rows_s[layer, lo:hi, :]
            weight = wt_ref[layer, lo:hi, :].astype(F32)
            acc = acc + jnp.sum(weight * grad, axis=0, keepdims=True)
            qkv_ref[layer, :, lo:hi] = grad.T
        out_ref[layer] = rows_s[layer, 3 * width : 4 * width, :]
        gain_out_ref[layer : layer + 1, :] = acc / gain_ref[layer : layer + 1, :]


def call(
    kernel, out_shape, scratch=(), grid=None, in_specs=None, out_specs=None, us=1, aliases=None, mib=12
):
    return pl.pallas_call(
        kernel,
        out_shape=out_shape,
        grid_spec=pltpu.PrefetchScalarGridSpec(
            num_scalar_prefetch=0,
            grid=grid or (),
            in_specs=in_specs,
            out_specs=out_specs,
            scratch_shapes=list(scratch),
        ),
        input_output_aliases=aliases or {},
        cost_estimate=pl.CostEstimate(
            flops=int(us * 1e6 * 800), bytes_accessed=int(us * 1e6), transcendentals=0
        ),
        compiler_params=pltpu.CompilerParams(vmem_limit_bytes=mib * 1024 * 1024),
    )


def whole():
    return pl.BlockSpec(memory_space=pltpu.VMEM)


def scalar():
    return pl.BlockSpec(memory_space=pltpu.SMEM)


def fixed(shape):
    return pl.BlockSpec(shape, lambda i: (0,) * len(shape))


def token_spec(tile, width, first=0):
    at = first // tile
    return pl.BlockSpec((tile, width), lambda i: (i + at, 0))


def layer_spec(layer, rows, width):
    return pl.BlockSpec((None, rows, width), lambda i: (layer, 0, 0))


CHUNKS = 2
FORWARD_TILE = 512
BACKWARD_TILE = 512


def run_first(first, lat, order, blocks, start, wt, output_weight, norm_gain_table):
    size, width = start.shape
    tile = min(FORWARD_TILE, size)
    struct = jax.ShapeDtypeStruct
    part = struct((size, width), BF16)
    tok_spec = token_spec(tile, width)
    feat_spec = pl.BlockSpec((width, tile), lambda i: (0, i))
    at = first // tile
    return call(
        first_kernel,
        (
            struct((width, size), BF16),
            struct((6, 2 * width, size), BF16),
            struct((6, 8, size), F32),
            struct((width, size), BF16),
            part,
            part,
            *[struct((32, width), BF16)] * 3,
        ),
        grid=(size // tile,),
        in_specs=[scalar(), pl.BlockSpec((1, tile), lambda i: (0, i + at))]
        + [tok_spec] * 7
        + [
            layer_spec(0, 3 * width, width),
            layer_spec(0, width, width),
            fixed((2, width)),
        ],
        out_specs=(
            feat_spec,
            pl.BlockSpec((6, 2 * width, tile), lambda i: (0, 0, i)),
            pl.BlockSpec((6, 8, tile), lambda i: (0, 0, i)),
            feat_spec,
            tok_spec,
            tok_spec,
            *[fixed((32, width))] * 3,
        ),
        scratch=[pltpu.VMEM((6, 8, tile), F32), pltpu.VMEM((96, width), F32)],
        mib=LARGE_MIB,
        us=8,
    )(lat, order, *blocks, start, wt, output_weight, norm_gain_table)


def run_second(lat, places, normals, halos, query_key_value_weight, output_weight, cot):
    points, width = cot.shape
    struct = jax.ShapeDtypeStruct
    ext, slots = points + 64, points // 8
    across = pltpu.VMEM((width, points), BF16)
    every, halo = pltpu.VMEM((points, width), BF16), pltpu.VMEM((HALO, width), BF16)
    return call(
        second_kernel,
        (
            struct((points, 2 * width), BF16),
            struct((4 * width, width), BF16),
            struct((32, width), BF16),
            struct((48, width), BF16),
            struct((48, width), BF16),
        ),
        in_specs=[scalar()] + [whole()] * 11,
        out_specs=(whole(),) * 5,
        scratch=[
            across, every, every, across,
            *[halo] * 3,
            every,
            pltpu.VMEM((ext, width), BF16),
            pltpu.VMEM((ext, width), BF16),
            *[pltpu.VMEM((slots, width), BF16)] * 2,
            pltpu.VMEM((ext, width), F32),
            pltpu.VMEM((ext, width), F32),
            *[pltpu.VMEM((slots, width), BF16)] * 2,
            every,
            pltpu.VMEM((KEYS, 256), jnp.int32),
            every,
        ],
        mib=LARGE_MIB,
        us=22,
    )(lat, places, *normals, *halos, query_key_value_weight, output_weight, cot)


def inner_third_kernel(*refs):
    third_kernel(*refs[:14], None, *refs[14:17], None, *refs[17:25], None, *refs[25:])


def run_third(
    first, lat, order, blocks, kept, both, packs, wt, output_weight, norm_gain_table, weights
):
    q0, kv0, p0, mixed0, h1 = kept
    size, width = h1.shape
    points = both.shape[0]
    tile = min(BACKWARD_TILE, size)
    struct = jax.ShapeDtypeStruct
    part = struct((size, width), BF16)
    tok_spec = token_spec(tile, width)
    feat_spec = pl.BlockSpec((width, tile), lambda i: (0, i))
    final = packs is not None
    whole_dw, half_dw = (4 * width, width), (2 * width, width)
    return call(
        third_kernel if final else inner_third_kernel,
        (
            struct((size, width), F32),
            struct((size, width), F32),
            *[part] * 5,
            *([struct(half_dw, BF16)] * 2 if final else [struct(whole_dw, F32)]),
        ),
        grid=(size // tile,),
        in_specs=[scalar(), token_spec(tile, 1, first)]
        + [tok_spec] * 6
        + [
            feat_spec,
            pl.BlockSpec((6, 2 * width, tile), lambda i: (0, 0, i)),
            pl.BlockSpec((6, 8, tile), lambda i: (0, 0, i)),
            feat_spec,
            tok_spec,
        ]
        + [fixed((points, 2 * width))]
        + [fixed((RETURNED, width))] * final
        + [
            layer_spec(0, 3 * width, width),
            layer_spec(0, width, width),
            fixed((2, width)),
        ]
        + [fixed(whole_dw)] * final,
        out_specs=(*[tok_spec] * 7, *([fixed(half_dw)] * 2 if final else [fixed(whole_dw)])),
        scratch=[
            pltpu.VMEM(whole_dw, F32),
            pltpu.VMEM((width, tile), F32),
            pltpu.VMEM((2 * width, 6 * tile), BF16),
            pltpu.VMEM((width, tile), BF16),
            pltpu.VMEM((8, tile), F32),
            pltpu.VMEM((6 * tile, width), BF16),
        ],
        mib=LARGE_MIB,
        us=13,
    )(
        lat, order, *blocks, q0, kv0, p0, mixed0, h1, both, *([packs] if final else []), wt,
        output_weight, norm_gain_table, *([weights] if final else []),
    )


def local(
    tokens, visible, mask_token, norm_gain_table, query_key_value_weight, output_weight, cotangent
):
    rows, cols, width = tokens.shape
    points = rows * cols
    size = points // CHUNKS
    firsts = [c * size for c in range(CHUNKS)]
    lat_count, lon_count = lax.axis_size("lat"), lax.axis_size("lon")
    lat = lax.axis_index("lat").astype(jnp.int32).reshape(1)
    wt = jnp.swapaxes(query_key_value_weight, 1, 2)
    struct = jax.ShapeDtypeStruct
    tokens = tokens.reshape(points, width)
    cot = cotangent.reshape(points, width)
    part = struct((size, width), BF16)
    gain_spec = fixed((2, width))
    wt_spec, wo_spec = layer_spec(0, 3 * width, width), layer_spec(0, width, width)

    order, places = token_order(rows, cols)
    order_row = jnp.asarray(order.reshape(1, points))
    order, places = jnp.asarray(order.reshape(points, 1)), jnp.asarray(places.reshape(points, 1))

    small = 512
    starts, normals = [], []
    for first in firsts:
        start, normal = call(
            start_kernel,
            (part, part),
            grid=(size // small,),
            in_specs=[
                token_spec(small, 1, first),
                fixed((points, width)),
                fixed((rows, cols)),
                fixed((width,)),
                gain_spec,
            ],
            out_specs=(token_spec(small, width),) * 2,
            mib=LARGE_MIB,
            us=2,
        )(order, tokens, visible, mask_token, norm_gain_table)
        starts.append(start)
        normals.append(normal)

    swapped0 = lon_swap(normals[0])
    own1, swapped0, wt = lax.optimization_barrier((normals[1], swapped0, wt))
    swapped1 = lon_swap(own1)
    beyond0, beyond1 = lon_forward(swapped0), lon_forward(swapped1)
    near0, near1 = lat_swap(normals[0]), lat_swap(own1)

    def blocks_of(own, near, swapped, beyond):
        return [own, near, swapped, beyond, lat_swap(swapped), lat_swap(beyond)]

    blocks = [blocks_of(normals[0], near0, swapped0, beyond0), None]

    kept = []
    for c in range(CHUNKS):
        *keep, normal1, row, left, right = run_first(
            firsts[c], lat, order_row, blocks[c], starts[c], wt, output_weight, norm_gain_table
        )
        if c == 1:
            keep, normal1, halos = lax.optimization_barrier((keep, normal1, halos))
            halos = [*halos, lat_swap(halos[1]), lat_swap(halos[2])]
        kept.append((keep, normal1))
        if c == 0:
            beyond1, row, left, right = lax.optimization_barrier((beyond1, row, left, right))
            halos = [lat_swap(row), from_left(right), from_right(left)]
            blocks[1] = blocks_of(own1, near1, swapped1, beyond1)

    both1, dw1, brow, bleft, bright = run_second(
        lat, places, [kept[0][1], kept[1][1]], halos, query_key_value_weight, output_weight, cot
    )

    from_l, from_r, brow = from_left(bright), from_right(bleft), lat_swap(brow)
    stages = lon_factors()
    sum1 = halves_summed(
        lax.dynamic_slice_in_dim(dw1, lat[0] * 2 * width, 2 * width, 0),
        lax.dynamic_slice_in_dim(dw1, (1 - lat[0]) * 2 * width, 2 * width, 0),
    )
    both1, sum1 = chained(both1, sum1)
    border = (brow, from_l, from_r)

    def plus(a, b):
        return (a.astype(F32) + b.astype(F32)).astype(BF16)

    weights = packs = None
    sum_stages = list(stages)
    ends = []
    coming = returned = None
    for n, c in enumerate(range(CHUNKS)[::-1]):
        dh1, d0, d1, d2, d3, d4, d5, *weights = run_third(
            firsts[c], lat, order, blocks[c], kept[c][0], both1, packs, wt,
            output_weight, norm_gain_table, weights,
        )
        if n == 0:
            sum1 = stage_summed(sum1, sum_stages.pop(0))
        border, weights, sum1, d1, d2, d3, d4, d5, coming, returned = lax.optimization_barrier(
            (border, weights, sum1, d1, d2, d3, d4, d5, coming, returned)
        )
        if n == 0:
            brow, from_l, from_r = border
            packs = jnp.concatenate([brow, from_l, from_r, lat_swap(from_l), lat_swap(from_r)], 0)
        d3 = plus(d3, lat_swap(d5))
        d2 = plus(d2, lat_swap(d4))
        d1 = lat_swap(d1)
        if n == CHUNKS - 1:
            weights = [halves_summed(*weights)]
        weights, d1, d2, d3 = lax.optimization_barrier((weights, d1, d2, d3))
        if returned is not None:
            ends[-2][-1] = returned
        returned = None
        if coming is not None:
            returned = lon_swap(coming)
        coming = plus(d2, lon_backward(d3))
        weights = weights[0]
        ends.append([c, dh1, d0, d1, None])

    sum0 = stage_summed(weights, stages[0])
    for stage in sum_stages:
        sum1 = stage_summed(sum1, stage)
    sum0, sum1, coming, returned = lax.optimization_barrier((sum0, sum1, coming, returned))
    ends[-2][-1] = returned
    returned = lon_swap(coming)
    sum0 = stage_summed(sum0, stages[1])
    sum0, returned = lax.optimization_barrier((sum0, returned))
    ends[-1][-1] = returned
    for stage in stages[2:]:
        sum0 = stage_summed(sum0, stage)
    sums = jnp.concatenate([sum0, sum1], 0)
    for stage in stages[::-1]:
        sums = spread(sums, *stage)

    pieces = []
    for c, dh1, d0, near, far in ends:
        pieces.append((c, [starts[c], dh1, d0, far, near]))
    pieces = [array for _, arrays in sorted(pieces, key=lambda p: p[0]) for array in arrays]
    grad_tokens = call(
        last_kernel,
        struct((points, width), F32),
        in_specs=[whole()] * (4 + len(pieces)),
        out_specs=whole(),
        scratch=[pltpu.VMEM((points, width), BF16)] * 2,
        mib=LARGE_MIB,
        us=6,
    )(places, visible, norm_gain_table, cot, *pieces)
    sums, grad_tokens = chained(sums, grad_tokens)
    other = lat_swap(sums)
    factor = (points * lat_count * lon_count) ** (-0.5)
    g_qkv, g_out, g_gain = call(
        functools.partial(weights_kernel, factor, lon_count),
        (
            struct((2, width, 3 * width), F32),
            struct((2, width, width), F32),
            struct((2, width), F32),
        ),
        in_specs=[scalar()] + [whole()] * 4,
        out_specs=(whole(),) * 3,
        scratch=[pltpu.VMEM((2, 4 * width, width), F32)],
        mib=20,
        us=5,
    )(lat, sums, other, wt, norm_gain_table)
    return grad_tokens.reshape(rows, cols, width), g_qkv, g_out, g_gain


def without(kernel, at, count, *refs):
    kernel(*refs[:at], *[None] * count, *refs[at:])


def solution(mesh):
    return jax.shard_map(
        local,
        mesh=mesh,
        in_specs=(
            P(("group", "lat"), "lon", None),
            P(("group", "lat"), "lon"),
            P(),
            P(),
            P(),
            P(),
            P(("group", "lat"), "lon", None),
        ),
        out_specs=(
            P(("group", "lat"), "lon", None),
            P("group", None, None),
            P("group", None, None),
            P("group", None),
        ),
        check_vma=False,
    )
```

```python
import functools

import jax
import jax.numpy as jnp
import numpy as np
from jax import lax
from jax.experimental import pallas as pl
from jax.experimental.pallas import tpu as pltpu
from jax.sharding import PartitionSpec as P

HEADS = 6
EPS = 1e-05
F32 = jnp.float32
BF16 = jnp.bfloat16
LARGE_MIB = 56
HALO = 112
CORNER = 96
KEYS = 208
RETURNED = 224


def nn(a, b):
    return lax.dot_general(a, b, (((1,), (0,)), ((), ())), preferred_element_type=F32)


def nt(a, b):
    return lax.dot_general(a, b, (((1,), (1,)), ((), ())), preferred_element_type=F32)


def tn(a, b):
    return lax.dot_general(a, b, (((0,), (0,)), ((), ())), preferred_element_type=F32)


def tt(a, b):
    return lax.dot_general(a, b, (((0,), (1,)), ((), ())), preferred_element_type=F32)


def iota(shape, dim):
    return lax.broadcasted_iota(jnp.int32, shape, dim)


def one_hot(condition):
    return jnp.where(condition, 1.0, 0.0).astype(BF16)


def permuted(value, axis, target):
    count = lax.axis_size(axis)
    return lax.ppermute(value, axis, [(i, target(i) % count) for i in range(count)])


def lat_swap(value):
    return permuted(value, "lat", lambda i: i ^ 1)


def lon_swap(value):
    return permuted(value, "lon", lambda i: i ^ 1)


def lon_forward(value):
    return permuted(value, "lon", lambda i: i + 2 if i % 2 == 0 else i - 2)


def lon_backward(value):
    return permuted(value, "lon", lambda i: i - 2 if i % 2 == 0 else i + 2)


def from_left(value):
    return permuted(value, "lon", lambda i: i + 1)


def from_right(value):
    return permuted(value, "lon", lambda i: i - 1)


def chained(value, after):
    return lax.optimization_barrier((value, after))


def exchanged(parts, axis_stride, factor):
    count = lax.axis_size("lon")
    digit = (lax.axis_index("lon") // axis_stride) % factor
    moved = []
    for d in range(1, factor):
        pairs = [(i, shifted(i, axis_stride, factor, d)) for i in range(count)]
        moved.append(lax.ppermute(parts(digit ^ d), "lon", pairs))
    total = parts(digit).astype(F32)
    for piece in moved:
        total = total + piece.astype(F32)
    return total.astype(BF16)


def shifted(i, stride, factor, d):
    digit = (i // stride) % factor
    return i + ((digit ^ d) - digit) * stride


def spread(value, axis_stride, factor):
    count = lax.axis_size("lon")
    digit = (lax.axis_index("lon") // axis_stride) % factor
    rows = value.shape[0]
    full = jnp.zeros((factor * rows,) + value.shape[1:], value.dtype)
    full = lax.dynamic_update_slice(full, value, (digit * rows, 0))
    for d in range(1, factor):
        pairs = [(i, shifted(i, axis_stride, factor, d)) for i in range(count)]
        got = lax.ppermute(value, "lon", pairs)
        at = (digit ^ d) * rows
        full = lax.dynamic_update_slice(full, got, (at, 0))
    return full


def lon_factors():
    left = lax.axis_size("lon")
    stride, out = 1, []
    for factor in [2] + [4] * 10:
        if left == 1:
            break
        factor = min(factor, left)
        out.append((stride, factor))
        stride, left = stride * factor, left // factor
    return out


def halves_summed(mine, other):
    return (mine.astype(F32) + lat_swap(other).astype(F32)).astype(BF16)


def stage_summed(value, stage):
    stride, factor = stage
    size = value.shape[0] // factor
    return exchanged(
        lambda k: lax.dynamic_slice_in_dim(value, k * size, size, 0), stride, factor
    )


def norm_parts(x):
    mean = jnp.mean(x, axis=-1, keepdims=True)
    centred = x - mean
    spread = jnp.mean(centred * centred, axis=-1, keepdims=True)
    rstd = lax.rsqrt(spread + EPS)
    return centred * rstd, rstd


def norm_back(x, gain, grad_normal):
    xhat, rstd = norm_parts(x)
    g = grad_normal * gain
    return rstd * (
        g - jnp.mean(g, axis=-1, keepdims=True) - xhat * jnp.mean(g * xhat, axis=-1, keepdims=True)
    )


def shown_column(visible, token):
    rows, cols = visible.shape
    tile = token.shape[0]
    of_row = nn(one_hot(token // cols == iota((tile, rows), 1)), visible.astype(F32).astype(BF16))
    mine = token % cols == iota((tile, cols), 1)
    return jnp.sum(jnp.where(mine, of_row, 0.0), axis=1, keepdims=True)


def token_order(rows, cols):
    row, col = np.divmod(np.arange(rows * cols), cols)
    border = (row == 0) | (row == rows - 1) | (col == 0) | (col == cols - 1)
    order = np.argsort(~border, kind="stable").astype(np.int32)
    return order, np.argsort(order, kind="stable").astype(np.int32)


def picked(places, values):
    count = values.shape[0]
    return nn(one_hot(places == iota((places.shape[0], count), 1)), values)


def start_kernel(order_ref, tok_ref, vis_ref, mask_ref, gain_ref, start_ref, normal_ref):
    width = tok_ref.shape[1]
    token = order_ref[...]
    shown = shown_column(vis_ref[...], token)
    x = jnp.where(
        shown > 0.5, picked(token, tok_ref[...]), mask_ref[...].astype(F32).reshape(1, width)
    )
    start_ref[...] = x.astype(BF16)
    xhat, _ = norm_parts(x)
    normal_ref[...] = (xhat * gain_ref[0:1, :]).astype(BF16)


def first_kernel(
    lat_ref, order_ref, n0, n1, n2, n3, n4, n5, start_ref,
    wt_ref, wo_ref, gain_ref,
    q_ref, kv_ref, p_ref, mixed_ref, h_ref, normal_ref, row_ref, left_ref, right_ref,
    w_s, pack_s,
):
    width, tile = q_ref.shape
    head = width // HEADS
    blocks = (n0, n1, n2, n3, n4, n5)
    q_ref[...] = nt(wt_ref[0:width], n0[...]).astype(BF16)
    for b, ref in enumerate(blocks):
        kv_ref[b] = nt(wt_ref[width : 3 * width], ref[...]).astype(BF16)
    for h in range(HEADS):
        lo, hi = h * head, (h + 1) * head
        q = q_ref[lo:hi, :].astype(F32) * (head**-0.5)
        total = jnp.zeros((1, tile), F32)
        out = jnp.zeros((head, tile), F32)
        for b in range(len(blocks)):
            k = kv_ref[b, lo:hi, :].astype(F32)
            w = jnp.exp(jnp.sum(q * k, axis=0, keepdims=True))
            w_s[b, h : h + 1, :] = w
            total = total + w
            out = out + w * kv_ref[b, width + lo : width + hi, :].astype(F32)
        inverse = 1.0 / total
        for b in range(len(blocks)):
            p_ref[b, h : h + 1, :] = w_s[b, h : h + 1, :] * inverse
        mixed_ref[lo:hi, :] = (out * inverse).astype(BF16)
    h1 = start_ref[...].astype(F32) + tn(mixed_ref[...], wo_ref[...])
    h1 = h1.astype(BF16)
    h_ref[...] = h1
    xhat, _ = norm_parts(h1.astype(F32))
    normal = (xhat * gain_ref[1:2, :]).astype(BF16)
    normal_ref[...] = normal
    step = pl.program_id(0)
    brow = jnp.where(lat_ref[0] == 0, 31, 0)
    slot = iota((96, tile), 0)
    r, c = order_ref[...] // 32, order_ref[...] % 32
    pick = one_hot(
        ((slot < 32) & (r == brow) & (c == slot))
        | ((slot >= 32) & (slot < 64) & (c == 0) & (r == slot - 32))
        | ((slot >= 64) & (c == 31) & (r == slot - 64))
    )

    @pl.when(step == 0)
    def _():
        pack_s[...] = jnp.zeros_like(pack_s)

    pack_s[...] += nn(pick, normal)

    @pl.when(step == pl.num_programs(0) - 1)
    def _():
        for i, ref in enumerate((row_ref, left_ref, right_ref)):
            ref[...] = pack_s[i * 32 : i * 32 + 32, :].astype(BF16)


def write_halves(lat, total_ref, mine_ref, other_ref):
    half = mine_ref.shape[0]
    for band in range(2):

        @pl.when(lat == band)
        def _():
            mine_ref[...] = total_ref[band * half : (band + 1) * half, :].astype(BF16)
            other_ref[...] = total_ref[(1 - band) * half : (2 - band) * half, :].astype(BF16)


def second_kernel(
    lat_ref, place_ref, na_ref, nb_ref, row_ref, left_ref, right_ref, dleft_ref, dright_ref,
    w_all, wo_all, cot_ref,
    both_ref, dw_ref, brow_ref, bleft_ref, bright_ref,
    dq_ref, dk_ref, dv_ref, mixed_s, dkh_ref, dvh_ref, halo_s,
    q_s, k_s, v_s, kc_s, vc_s, dk_s, dv_s, dkc_s, dvc_s, do_s, mask_s, normal_s,
):
    points, width = cot_ref.shape
    head = width // HEADS
    w_ref, wo_ref = w_all.at[1], wo_all.at[1]
    upper = lat_ref[0] == 0
    halo_s[0:32, :] = row_ref[...]
    halo_s[32:64, :] = left_ref[...]
    halo_s[64:96, :] = right_ref[...]
    a, b = iota((16, 32), 0), iota((16, 32), 1)
    sent = b == jnp.where(upper, 0, 31)
    corners = nn(one_hot(sent & (a == 0)), dleft_ref[...])
    corners += nn(one_hot(sent & (a == 1)), dright_ref[...])
    halo_s[CORNER:HALO, :] = corners.astype(BF16)
    halo = halo_s[...]
    ordered = jnp.concatenate([na_ref[...], nb_ref[...]], 0)
    @pl.loop(0, points // 256)
    def _(step):
        rows = pl.ds(pl.multiple_of(step * 256, 256), 256)
        normal_s[rows, :] = picked(place_ref[rows, :], ordered).astype(BF16)
    normal = normal_s[...]
    scale = head**-0.5
    q_s[...] = (nn(normal, w_ref[:, 0:width]).astype(BF16).astype(F32) * scale).astype(BF16)
    k_s[32 : 32 + points, :] = nn(normal, w_ref[:, width : 2 * width]).astype(BF16)
    v_s[32 : 32 + points, :] = nn(normal, w_ref[:, 2 * width : 3 * width]).astype(BF16)
    kh = nn(halo, w_ref[:, width : 2 * width]).astype(BF16)
    vh = nn(halo, w_ref[:, 2 * width : 3 * width]).astype(BF16)
    for at in (0, 32 + points):
        k_s[at : at + 32, :] = kh[0:32]
        v_s[at : at + 32, :] = vh[0:32]
    tiles = points // 128
    slots = tiles * 16
    a, b = iota((slots, HALO - 32), 0), iota((slots, HALO - 32), 1)
    place, is_right = a % 16, jnp.where(a % 16 >= 6, 1, 0)
    ext_row = 4 * (a // 16) + place - 6 * is_right
    inner = (ext_row >= 1) & (ext_row <= 32)
    source = jnp.where(inner, 32 * is_right + ext_row - 1, 64 + is_right)
    spread_cols = one_hot((place < 12) & (b == source))
    kc_s[...] = nn(spread_cols, kh[32:HALO]).astype(BF16)
    vc_s[...] = nn(spread_cols, vh[32:HALO]).astype(BF16)
    dk_s[...] = jnp.zeros_like(dk_s)
    dv_s[...] = jnp.zeros_like(dv_s)
    cot = cot_ref[...].astype(BF16)
    both_ref[:, width : 2 * width] = cot
    do_s[...] = nt(cot, wo_ref[...]).astype(BF16)

    key, query = iota((KEYS, 256), 0), iota((KEYS, 256), 1) % 128
    place = key - 192
    right = place >= 6
    row = jnp.where(place < 0, key // 32, jnp.where(right, place - 6, place))
    col = jnp.where(place < 0, key % 32, jnp.where(right, 32, -1))
    near = (jnp.abs(row - 1 - query // 32) <= 1) & (jnp.abs(col - query % 32) <= 1)
    mask_s[...] = jnp.where(near & (place < 12), row, 9)

    def tile_step(t, carry):
        base = pl.multiple_of(t * 128, 128)
        first = jnp.where(upper & (t == 0), 1, 0)
        last = jnp.where(jnp.logical_not(upper) & (t == tiles - 1), 4, 5)
        mask = (mask_s[...] >= first) & (mask_s[...] <= last)
        even = iota((128, 128), 1) < 64
        top = iota((128, 128), 0) < 64
        win, here = pl.ds(base, 192), pl.ds(base, 128)
        side = pl.ds(pl.multiple_of(t * 16, 16), 16)
        for pair in range(HEADS // 2):
            lanes = slice(pair * 128, pair * 128 + 128)
            q = q_s[here, lanes]
            do = do_s[here, lanes]
            zero = jnp.zeros_like(q)
            qm = jnp.concatenate([jnp.where(even, q, zero), jnp.where(even, zero, q)], 0)
            dom = jnp.concatenate([jnp.where(even, do, zero), jnp.where(even, zero, do)], 0)
            k = jnp.concatenate([k_s[win, lanes], kc_s[side, lanes]], 0)
            v = jnp.concatenate([v_s[win, lanes], vc_s[side, lanes]], 0)
            w = jnp.where(mask, jnp.exp(nt(k, qm)), 0.0)
            p = w * (1.0 / jnp.sum(w, axis=0, keepdims=True))
            dp = nt(v, dom)
            delta = jnp.sum(p * dp, axis=0, keepdims=True)
            ds = (p * (dp - delta)).astype(BF16)
            p = p.astype(BF16)
            out = tn(v, p)
            mixed_s[lanes, here] = jnp.where(top, out[:, 0:128], out[:, 128:256]).astype(BF16)
            dq = tn(k, ds) * scale
            dq_ref[lanes, here] = jnp.where(top, dq[:, 0:128], dq[:, 128:256]).astype(BF16)
            dk, dv = nn(ds, qm), nn(p, dom)
            dk_s[win, lanes] += dk[0:192]
            dv_s[win, lanes] += dv[0:192]
            dkc_s[side, lanes] = dk[192:KEYS].astype(BF16)
            dvc_s[side, lanes] = dv[192:KEYS].astype(BF16)
        return carry

    lax.fori_loop(0, tiles, tile_step, 0)

    row_at = pl.multiple_of(jnp.where(upper, 32 + points, 0), 32)
    dkh = jnp.concatenate([dk_s[pl.ds(row_at, 32), :], tn(spread_cols, dkc_s[...])], 0).astype(BF16)
    dvh = jnp.concatenate([dv_s[pl.ds(row_at, 32), :], tn(spread_cols, dvc_s[...])], 0).astype(BF16)
    dkh_ref[...] = dkh
    dvh_ref[...] = dvh
    dk_ref[...] = dk_s[32 : 32 + points, :].astype(BF16)
    dv_ref[...] = dv_s[32 : 32 + points, :].astype(BF16)
    wk, wv = (w_ref[:, i * width : (i + 1) * width] for i in (1, 2))
    back = (nt(dkh, wk) + nt(dvh, wv)).astype(BF16)
    brow_ref[...] = back[0:32]
    for ref, at in ((bleft_ref, 32), (bright_ref, 64)):
        ref[0:32, :] = back[at : at + 32]
        ref[32:48, :] = back[CORNER:HALO]
    wq, wk, wv = (w_all[1, :, i * width : (i + 1) * width] for i in range(3))
    dw_ref[0:width, :] = nn(dq_ref[...], normal).astype(BF16)
    dw_ref[width : 2 * width, :] = (tn(dk_ref[...], normal) + tn(dkh_ref[...], halo)).astype(BF16)
    dw_ref[2 * width : 3 * width, :] = (
        tn(dv_ref[...], normal) + tn(dvh_ref[...], halo)
    ).astype(BF16)
    dw_ref[3 * width : 4 * width, :] = nn(mixed_s[...], cot).astype(BF16)
    both_ref[:, 0:width] = (tt(dq_ref[...], wq) + nt(dk_ref[...], wk) + nt(dv_ref[...], wv)).astype(BF16)


def third_kernel(
    lat_ref, order_ref, n0, n1, n2, n3, n4, n5, q_ref, kv_ref, p_ref, mixed_ref, h_ref, both_ref,
    packs_ref, wt_ref, wo_ref, gain_ref, dw_in,
    dh_ref, d0, d1, d2, d3, d4, d5, dw_ref, other_ref,
    dw_s, dmix_s, dkv_s, dq_s, dp_s, n_s,
):
    width, tile = q_ref.shape
    head = width // HEADS
    scale = head**-0.5
    blocks = (n0, n1, n2, n3, n4, n5)
    outs = (d0, d1, d2, d3, d4, d5)
    step = pl.program_id(0)

    @pl.when(step == 0)
    def _():
        dw_s[...] = jnp.zeros_like(dw_s) if dw_in is None else dw_in[...]

    token = order_ref[...]
    both = picked(token, both_ref[...])
    dn = both[:, 0:width]
    if packs_ref is not None:
        brow = jnp.where(lat_ref[0] == 0, 31, 0)
        r, c, slot = token // 32, token % 32, iota((tile, RETURNED), 1)
        border = r == brow
        place = one_hot(
            (border & (slot < 32) & (slot == c))
            | ((c == 0) & (slot < 64) & (slot == 32 + r))
            | ((c == 31) & (slot < 112) & (slot == 80 + r))
            | (border & (c == 0) & (slot == 128 + 33))
            | (border & (c == 31) & (slot == 176 + 32))
        )
        dn = dn + nn(place, packs_ref[...])
    dh = norm_back(h_ref[...].astype(F32), gain_ref[1:2, :], dn)
    dh_ref[...] = dh
    dh = dh + both[:, width : 2 * width]
    dhb = dh.astype(BF16)
    dmix_s[...] = nt(wo_ref[...], dhb)
    dw_s[3 * width : 4 * width, :] += nn(mixed_ref[...], dhb)
    for h in range(HEADS):
        lo, hi = h * head, (h + 1) * head
        dmix = dmix_s[lo:hi, :]
        delta = jnp.zeros((1, tile), F32)
        for b in range(len(blocks)):
            dp = jnp.sum(
                dmix * kv_ref[b, width + lo : width + hi, :].astype(F32), axis=0, keepdims=True
            )
            dp_s[b : b + 1, :] = dp
            delta = delta + p_ref[b, h : h + 1, :] * dp
        q = q_ref[lo:hi, :].astype(F32)
        dq = jnp.zeros((head, tile), F32)
        for b in range(len(blocks)):
            p = p_ref[b, h : h + 1, :]
            ds = p * (dp_s[b : b + 1, :] - delta) * scale
            dq = dq + ds * kv_ref[b, lo:hi, :].astype(F32)
            here = slice(b * tile, (b + 1) * tile)
            dkv_s[lo:hi, here] = (ds * q).astype(BF16)
            dkv_s[width + lo : width + hi, here] = (p * dmix).astype(BF16)
        dq_s[lo:hi, :] = dq.astype(BF16)
    dq = dq_s[...]
    dw_s[0:width, :] += nn(dq, n0[...])
    for b, ref in enumerate(blocks):
        n_s[b * tile : (b + 1) * tile, :] = ref[...]
    dw_s[width : 3 * width, :] += nn(dkv_s[...], n_s[...])
    grads = tn(dkv_s[...], wt_ref[width : 3 * width])
    outs[0][...] = grads[0:tile] + tn(dq, wt_ref[0:width])
    for b in range(1, len(blocks)):
        outs[b][...] = grads[b * tile : (b + 1) * tile].astype(BF16)

    @pl.when(step == pl.num_programs(0) - 1)
    def _():
        if other_ref is None:
            dw_ref[...] = dw_s[...]
        else:
            write_halves(lat_ref[0], dw_s, dw_ref, other_ref)


def last_kernel(place_ref, vis_ref, gain_ref, cot_ref, *refs):
    inputs, out_ref, high_s, low_s = refs[:-3], refs[-3], refs[-2], refs[-1]
    points, width = cot_ref.shape
    tile = 256
    at = 0
    while inputs:
        start_ref, dh_ref, own_ref, far_ref, near_ref = inputs[:5]
        for lo in range(0, start_ref.shape[0], tile):
            rows = slice(lo, lo + tile)
            dn = own_ref[rows] + far_ref[rows].astype(F32) + near_ref[rows].astype(F32)
            back = norm_back(start_ref[rows].astype(F32), gain_ref[0:1, :], dn)
            grad = dh_ref[rows] + back
            high = grad.astype(BF16)
            high_s[at : at + tile, :] = high
            low_s[at : at + tile, :] = (grad - high.astype(F32)).astype(BF16)
            at += tile
        inputs = inputs[5:]
    for lo in range(0, points, tile):
        rows = slice(lo, lo + tile)
        place = place_ref[rows, :]
        shown = shown_column(vis_ref[...], lo + iota((tile, 1), 0))
        grad = picked(place, high_s[...]) + picked(place, low_s[...]) + cot_ref[rows]
        out_ref[rows] = jnp.where(shown > 0.5, grad, 0.0)


def weights_kernel(
    factor, pieces, lat_ref, mine_ref, other_ref, wt_ref, gain_ref,
    qkv_ref, out_ref, gain_out_ref, rows_s,
):
    total, width = mine_ref.shape
    piece = total // pieces // 2
    lat = lat_ref[0]
    for ref, band in ((mine_ref, lat), (other_ref, 1 - lat)):
        for k in range(pieces):
            at = pl.multiple_of(band * (total // 2) + k * piece, 8)
            for layer in range(2):
                lo = (2 * k + layer) * piece
                rows_s[layer, pl.ds(at, piece), :] = ref[lo : lo + piece, :].astype(F32) * factor
    for layer in range(2):
        acc = jnp.zeros((1, width), F32)
        for i in range(3):
            lo, hi = i * width, (i + 1) * width
            grad = rows_s[layer, lo:hi, :]
            weight = wt_ref[layer, lo:hi, :].astype(F32)
            acc = acc + jnp.sum(weight * grad, axis=0, keepdims=True)
            qkv_ref[layer, :, lo:hi] = grad.T
        out_ref[layer] = rows_s[layer, 3 * width : 4 * width, :]
        gain_out_ref[layer : layer + 1, :] = acc / gain_ref[layer : layer + 1, :]


def call(
    kernel, out_shape, scratch=(), grid=None, in_specs=None, out_specs=None, us=1, aliases=None, mib=12
):
    return pl.pallas_call(
        kernel,
        out_shape=out_shape,
        grid_spec=pltpu.PrefetchScalarGridSpec(
            num_scalar_prefetch=0,
            grid=grid or (),
            in_specs=in_specs,
            out_specs=out_specs,
            scratch_shapes=list(scratch),
        ),
        input_output_aliases=aliases or {},
        cost_estimate=pl.CostEstimate(
            flops=int(us * 1e6 * 800), bytes_accessed=int(us * 1e6), transcendentals=0
        ),
        compiler_params=pltpu.CompilerParams(vmem_limit_bytes=mib * 1024 * 1024),
    )


def whole():
    return pl.BlockSpec(memory_space=pltpu.VMEM)


def scalar():
    return pl.BlockSpec(memory_space=pltpu.SMEM)


def fixed(shape):
    return pl.BlockSpec(shape, lambda i: (0,) * len(shape))


def token_spec(tile, width, first=0):
    at = first // tile
    return pl.BlockSpec((tile, width), lambda i: (i + at, 0))


def layer_spec(layer, rows, width):
    return pl.BlockSpec((None, rows, width), lambda i: (layer, 0, 0))


CHUNKS = 2
FORWARD_TILE = 256
BACKWARD_TILE = 256


def run_first(first, lat, order, blocks, start, wt, output_weight, norm_gain_table):
    size, width = start.shape
    tile = min(FORWARD_TILE, size)
    struct = jax.ShapeDtypeStruct
    part = struct((size, width), BF16)
    tok_spec = token_spec(tile, width)
    feat_spec = pl.BlockSpec((width, tile), lambda i: (0, i))
    at = first // tile
    return call(
        first_kernel,
        (
            struct((width, size), BF16),
            struct((6, 2 * width, size), BF16),
            struct((6, 8, size), F32),
            struct((width, size), BF16),
            part,
            part,
            *[struct((32, width), BF16)] * 3,
        ),
        grid=(size // tile,),
        in_specs=[scalar(), pl.BlockSpec((1, tile), lambda i: (0, i + at))]
        + [tok_spec] * 7
        + [
            layer_spec(0, 3 * width, width),
            layer_spec(0, width, width),
            fixed((2, width)),
        ],
        out_specs=(
            feat_spec,
            pl.BlockSpec((6, 2 * width, tile), lambda i: (0, 0, i)),
            pl.BlockSpec((6, 8, tile), lambda i: (0, 0, i)),
            feat_spec,
            tok_spec,
            tok_spec,
            *[fixed((32, width))] * 3,
        ),
        scratch=[pltpu.VMEM((6, 8, tile), F32), pltpu.VMEM((96, width), F32)],
        mib=LARGE_MIB,
        us=8,
    )(lat, order, *blocks, start, wt, output_weight, norm_gain_table)


def run_second(lat, places, normals, halos, query_key_value_weight, output_weight, cot):
    points, width = cot.shape
    struct = jax.ShapeDtypeStruct
    ext, slots = points + 64, points // 8
    across = pltpu.VMEM((width, points), BF16)
    every, halo = pltpu.VMEM((points, width), BF16), pltpu.VMEM((HALO, width), BF16)
    return call(
        second_kernel,
        (
            struct((points, 2 * width), BF16),
            struct((4 * width, width), BF16),
            struct((32, width), BF16),
            struct((48, width), BF16),
            struct((48, width), BF16),
        ),
        in_specs=[scalar()] + [whole()] * 11,
        out_specs=(whole(),) * 5,
        scratch=[
            across, every, every, across,
            *[halo] * 3,
            every,
            pltpu.VMEM((ext, width), BF16),
            pltpu.VMEM((ext, width), BF16),
            *[pltpu.VMEM((slots, width), BF16)] * 2,
            pltpu.VMEM((ext, width), F32),
            pltpu.VMEM((ext, width), F32),
            *[pltpu.VMEM((slots, width), BF16)] * 2,
            every,
            pltpu.VMEM((KEYS, 256), jnp.int32),
            every,
        ],
        mib=LARGE_MIB,
        us=22,
    )(lat, places, *normals, *halos, query_key_value_weight, output_weight, cot)


def inner_third_kernel(*refs):
    third_kernel(*refs[:14], None, *refs[14:17], None, *refs[17:25], None, *refs[25:])


def run_third(
    first, lat, order, blocks, kept, both, packs, wt, output_weight, norm_gain_table, weights
):
    q0, kv0, p0, mixed0, h1 = kept
    size, width = h1.shape
    points = both.shape[0]
    tile = min(BACKWARD_TILE, size)
    struct = jax.ShapeDtypeStruct
    part = struct((size, width), BF16)
    tok_spec = token_spec(tile, width)
    feat_spec = pl.BlockSpec((width, tile), lambda i: (0, i))
    final = packs is not None
    whole_dw, half_dw = (4 * width, width), (2 * width, width)
    return call(
        third_kernel if final else inner_third_kernel,
        (
            struct((size, width), F32),
            struct((size, width), F32),
            *[part] * 5,
            *([struct(half_dw, BF16)] * 2 if final else [struct(whole_dw, F32)]),
        ),
        grid=(size // tile,),
        in_specs=[scalar(), token_spec(tile, 1, first)]
        + [tok_spec] * 6
        + [
            feat_spec,
            pl.BlockSpec((6, 2 * width, tile), lambda i: (0, 0, i)),
            pl.BlockSpec((6, 8, tile), lambda i: (0, 0, i)),
            feat_spec,
            tok_spec,
        ]
        + [fixed((points, 2 * width))]
        + [fixed((RETURNED, width))] * final
        + [
            layer_spec(0, 3 * width, width),
            layer_spec(0, width, width),
            fixed((2, width)),
        ]
        + [fixed(whole_dw)] * final,
        out_specs=(*[tok_spec] * 7, *([fixed(half_dw)] * 2 if final else [fixed(whole_dw)])),
        scratch=[
            pltpu.VMEM(whole_dw, F32),
            pltpu.VMEM((width, tile), F32),
            pltpu.VMEM((2 * width, 6 * tile), BF16),
            pltpu.VMEM((width, tile), BF16),
            pltpu.VMEM((8, tile), F32),
            pltpu.VMEM((6 * tile, width), BF16),
        ],
        mib=LARGE_MIB,
        us=13,
    )(
        lat, order, *blocks, q0, kv0, p0, mixed0, h1, both, *([packs] if final else []), wt,
        output_weight, norm_gain_table, *([weights] if final else []),
    )


def local(
    tokens, visible, mask_token, norm_gain_table, query_key_value_weight, output_weight, cotangent
):
    rows, cols, width = tokens.shape
    points = rows * cols
    size = points // CHUNKS
    firsts = [c * size for c in range(CHUNKS)]
    lat_count, lon_count = lax.axis_size("lat"), lax.axis_size("lon")
    lat = lax.axis_index("lat").astype(jnp.int32).reshape(1)
    wt = jnp.swapaxes(query_key_value_weight, 1, 2)
    struct = jax.ShapeDtypeStruct
    tokens = tokens.reshape(points, width)
    cot = cotangent.reshape(points, width)
    part = struct((size, width), BF16)
    gain_spec = fixed((2, width))
    wt_spec, wo_spec = layer_spec(0, 3 * width, width), layer_spec(0, width, width)

    order, places = token_order(rows, cols)
    order_row = jnp.asarray(order.reshape(1, points))
    order, places = jnp.asarray(order.reshape(points, 1)), jnp.asarray(places.reshape(points, 1))

    small = 512
    starts, normals = [], []
    for first in firsts:
        start, normal = call(
            start_kernel,
            (part, part),
            grid=(size // small,),
            in_specs=[
                token_spec(small, 1, first),
                fixed((points, width)),
                fixed((rows, cols)),
                fixed((width,)),
                gain_spec,
            ],
            out_specs=(token_spec(small, width),) * 2,
            mib=LARGE_MIB,
            us=2,
        )(order, tokens, visible, mask_token, norm_gain_table)
        starts.append(start)
        normals.append(normal)

    swapped0 = lon_swap(normals[0])
    own1, swapped0, wt = lax.optimization_barrier((normals[1], swapped0, wt))
    swapped1 = lon_swap(own1)
    beyond0, beyond1 = lon_forward(swapped0), lon_forward(swapped1)
    near0, near1 = lat_swap(normals[0]), lat_swap(own1)

    def blocks_of(own, near, swapped, beyond):
        return [own, near, swapped, beyond, lat_swap(swapped), lat_swap(beyond)]

    blocks = [blocks_of(normals[0], near0, swapped0, beyond0), None]

    kept = []
    for c in range(CHUNKS):
        *keep, normal1, row, left, right = run_first(
            firsts[c], lat, order_row, blocks[c], starts[c], wt, output_weight, norm_gain_table
        )
        if c == 1:
            keep, normal1, halos = lax.optimization_barrier((keep, normal1, halos))
            halos = [*halos, lat_swap(halos[1]), lat_swap(halos[2])]
        kept.append((keep, normal1))
        if c == 0:
            beyond1, row, left, right = lax.optimization_barrier((beyond1, row, left, right))
            halos = [lat_swap(row), from_left(right), from_right(left)]
            blocks[1] = blocks_of(own1, near1, swapped1, beyond1)

    both1, dw1, brow, bleft, bright = run_second(
        lat, places, [kept[0][1], kept[1][1]], halos, query_key_value_weight, output_weight, cot
    )

    from_l, from_r, brow = from_left(bright), from_right(bleft), lat_swap(brow)
    stages = lon_factors()
    sum1 = halves_summed(
        lax.dynamic_slice_in_dim(dw1, lat[0] * 2 * width, 2 * width, 0),
        lax.dynamic_slice_in_dim(dw1, (1 - lat[0]) * 2 * width, 2 * width, 0),
    )
    both1, sum1 = chained(both1, sum1)
    border = (brow, from_l, from_r)

    def plus(a, b):
        return (a.astype(F32) + b.astype(F32)).astype(BF16)

    weights = packs = None
    sum_stages = list(stages)
    ends = []
    coming = returned = None
    for n, c in enumerate(range(CHUNKS)[::-1]):
        dh1, d0, d1, d2, d3, d4, d5, *weights = run_third(
            firsts[c], lat, order, blocks[c], kept[c][0], both1, packs, wt,
            output_weight, norm_gain_table, weights,
        )
        if n == 0:
            sum1 = stage_summed(sum1, sum_stages.pop(0))
        border, weights, sum1, d1, d2, d3, d4, d5, coming, returned = lax.optimization_barrier(
            (border, weights, sum1, d1, d2, d3, d4, d5, coming, returned)
        )
        if n == 0:
            brow, from_l, from_r = border
            packs = jnp.concatenate([brow, from_l, from_r, lat_swap(from_l), lat_swap(from_r)], 0)
        d3 = plus(d3, lat_swap(d5))
        d2 = plus(d2, lat_swap(d4))
        d1 = lat_swap(d1)
        if n == CHUNKS - 1:
            weights = [halves_summed(*weights)]
        weights, d1, d2, d3 = lax.optimization_barrier((weights, d1, d2, d3))
        if returned is not None:
            ends[-2][-1] = returned
        returned = None
        if coming is not None:
            returned = lon_swap(coming)
        coming = plus(d2, lon_backward(d3))
        weights = weights[0]
        ends.append([c, dh1, d0, d1, None])

    sum0 = stage_summed(weights, stages[0])
    for stage in sum_stages:
        sum1 = stage_summed(sum1, stage)
    sum0, sum1, coming, returned = lax.optimization_barrier((sum0, sum1, coming, returned))
    ends[-2][-1] = returned
    returned = lon_swap(coming)
    sum0 = stage_summed(sum0, stages[1])
    sum0, returned = lax.optimization_barrier((sum0, returned))
    ends[-1][-1] = returned
    for stage in stages[2:]:
        sum0 = stage_summed(sum0, stage)
    sums = jnp.concatenate([sum0, sum1], 0)
    for stage in stages[::-1]:
        sums = spread(sums, *stage)

    pieces = []
    for c, dh1, d0, near, far in ends:
        pieces.append((c, [starts[c], dh1, d0, far, near]))
    pieces = [array for _, arrays in sorted(pieces, key=lambda p: p[0]) for array in arrays]
    grad_tokens = call(
        last_kernel,
        struct((points, width), F32),
        in_specs=[whole()] * (4 + len(pieces)),
        out_specs=whole(),
        scratch=[pltpu.VMEM((points, width), BF16)] * 2,
        mib=LARGE_MIB,
        us=6,
    )(places, visible, norm_gain_table, cot, *pieces)
    sums, grad_tokens = chained(sums, grad_tokens)
    other = lat_swap(sums)
    factor = (points * lat_count * lon_count) ** (-0.5)
    g_qkv, g_out, g_gain = call(
        functools.partial(weights_kernel, factor, lon_count),
        (
            struct((2, width, 3 * width), F32),
            struct((2, width, width), F32),
            struct((2, width), F32),
        ),
        in_specs=[scalar()] + [whole()] * 4,
        out_specs=(whole(),) * 3,
        scratch=[pltpu.VMEM((2, 4 * width, width), F32)],
        mib=20,
        us=5,
    )(lat, sums, other, wt, norm_gain_table)
    return grad_tokens.reshape(rows, cols, width), g_qkv, g_out, g_gain


def without(kernel, at, count, *refs):
    kernel(*refs[:at], *[None] * count, *refs[at:])


def solution(mesh):
    return jax.shard_map(
        local,
        mesh=mesh,
        in_specs=(
            P(("group", "lat"), "lon", None),
            P(("group", "lat"), "lon"),
            P(),
            P(),
            P(),
            P(),
            P(("group", "lat"), "lon", None),
        ),
        out_specs=(
            P(("group", "lat"), "lon", None),
            P("group", None, None),
            P("group", None, None),
            P("group", None),
        ),
        check_vma=False,
    )
```

```python
import functools

import jax
import jax.numpy as jnp
import numpy as np
from jax import lax
from jax.experimental import pallas as pl
from jax.experimental.pallas import tpu as pltpu
from jax.sharding import PartitionSpec as P

HEADS = 6
EPS = 1e-05
F32 = jnp.float32
BF16 = jnp.bfloat16
LARGE_MIB = 56
HALO = 112
CORNER = 96
KEYS = 208
RETURNED = 224


def nn(a, b):
    return lax.dot_general(a, b, (((1,), (0,)), ((), ())), preferred_element_type=F32)


def nt(a, b):
    return lax.dot_general(a, b, (((1,), (1,)), ((), ())), preferred_element_type=F32)


def tn(a, b):
    return lax.dot_general(a, b, (((0,), (0,)), ((), ())), preferred_element_type=F32)


def tt(a, b):
    return lax.dot_general(a, b, (((0,), (1,)), ((), ())), preferred_element_type=F32)


def iota(shape, dim):
    return lax.broadcasted_iota(jnp.int32, shape, dim)


def one_hot(condition):
    return jnp.where(condition, 1.0, 0.0).astype(BF16)


def permuted(value, axis, target):
    count = lax.axis_size(axis)
    return lax.ppermute(value, axis, [(i, target(i) % count) for i in range(count)])


def lat_swap(value):
    return permuted(value, "lat", lambda i: i ^ 1)


def lon_swap(value):
    return permuted(value, "lon", lambda i: i ^ 1)


def lon_forward(value):
    return permuted(value, "lon", lambda i: i + 2 if i % 2 == 0 else i - 2)


def lon_backward(value):
    return permuted(value, "lon", lambda i: i - 2 if i % 2 == 0 else i + 2)


def from_left(value):
    return permuted(value, "lon", lambda i: i + 1)


def from_right(value):
    return permuted(value, "lon", lambda i: i - 1)


def chained(value, after):
    return lax.optimization_barrier((value, after))


def exchanged(parts, axis_stride, factor):
    count = lax.axis_size("lon")
    digit = (lax.axis_index("lon") // axis_stride) % factor
    moved = []
    for d in range(1, factor):
        pairs = [(i, shifted(i, axis_stride, factor, d)) for i in range(count)]
        moved.append(lax.ppermute(parts(digit ^ d), "lon", pairs))
    total = parts(digit).astype(F32)
    for piece in moved:
        total = total + piece.astype(F32)
    return total.astype(BF16)


def shifted(i, stride, factor, d):
    digit = (i // stride) % factor
    return i + ((digit ^ d) - digit) * stride


def spread(value, axis_stride, factor):
    count = lax.axis_size("lon")
    digit = (lax.axis_index("lon") // axis_stride) % factor
    rows = value.shape[0]
    full = jnp.zeros((factor * rows,) + value.shape[1:], value.dtype)
    full = lax.dynamic_update_slice(full, value, (digit * rows, 0))
    for d in range(1, factor):
        pairs = [(i, shifted(i, axis_stride, factor, d)) for i in range(count)]
        got = lax.ppermute(value, "lon", pairs)
        at = (digit ^ d) * rows
        full = lax.dynamic_update_slice(full, got, (at, 0))
    return full


def lon_factors():
    left = lax.axis_size("lon")
    stride, out = 1, []
    for factor in [2] + [4] * 10:
        if left == 1:
            break
        factor = min(factor, left)
        out.append((stride, factor))
        stride, left = stride * factor, left // factor
    return out


def halves_summed(mine, other):
    return (mine.astype(F32) + lat_swap(other).astype(F32)).astype(BF16)


def stage_summed(value, stage):
    stride, factor = stage
    size = value.shape[0] // factor
    return exchanged(
        lambda k: lax.dynamic_slice_in_dim(value, k * size, size, 0), stride, factor
    )


def norm_parts(x):
    mean = jnp.mean(x, axis=-1, keepdims=True)
    centred = x - mean
    spread = jnp.mean(centred * centred, axis=-1, keepdims=True)
    rstd = lax.rsqrt(spread + EPS)
    return centred * rstd, rstd


def norm_back(x, gain, grad_normal):
    xhat, rstd = norm_parts(x)
    g = grad_normal * gain
    return rstd * (
        g - jnp.mean(g, axis=-1, keepdims=True) - xhat * jnp.mean(g * xhat, axis=-1, keepdims=True)
    )


def shown_column(visible, token):
    rows, cols = visible.shape
    tile = token.shape[0]
    of_row = nn(one_hot(token // cols == iota((tile, rows), 1)), visible.astype(F32).astype(BF16))
    mine = token % cols == iota((tile, cols), 1)
    return jnp.sum(jnp.where(mine, of_row, 0.0), axis=1, keepdims=True)


def token_order(rows, cols):
    row, col = np.divmod(np.arange(rows * cols), cols)
    border = (row == 0) | (row == rows - 1) | (col == 0) | (col == cols - 1)
    order = np.argsort(~border, kind="stable").astype(np.int32)
    return order, np.argsort(order, kind="stable").astype(np.int32)


def picked(places, values):
    count = values.shape[0]
    return nn(one_hot(places == iota((places.shape[0], count), 1)), values)


def start_kernel(order_ref, tok_ref, vis_ref, mask_ref, gain_ref, start_ref, normal_ref):
    width = tok_ref.shape[1]
    token = order_ref[...]
    shown = shown_column(vis_ref[...], token)
    x = jnp.where(
        shown > 0.5, picked(token, tok_ref[...]), mask_ref[...].astype(F32).reshape(1, width)
    )
    start_ref[...] = x.astype(BF16)
    xhat, _ = norm_parts(x)
    normal_ref[...] = (xhat * gain_ref[0:1, :]).astype(BF16)


def first_kernel(
    lat_ref, order_ref, n0, n1, n2, n3, n4, n5, start_ref,
    wt_ref, wo_ref, gain_ref,
    q_ref, kv_ref, p_ref, mixed_ref, h_ref, normal_ref, row_ref, left_ref, right_ref,
    w_s, pack_s,
):
    width, tile = q_ref.shape
    head = width // HEADS
    blocks = (n0, n1, n2, n3, n4, n5)
    q_ref[...] = nt(wt_ref[0:width], n0[...]).astype(BF16)
    for b, ref in enumerate(blocks):
        kv_ref[b] = nt(wt_ref[width : 3 * width], ref[...]).astype(BF16)
    for h in range(HEADS):
        lo, hi = h * head, (h + 1) * head
        q = q_ref[lo:hi, :].astype(F32) * (head**-0.5)
        total = jnp.zeros((1, tile), F32)
        out = jnp.zeros((head, tile), F32)
        for b in range(len(blocks)):
            k = kv_ref[b, lo:hi, :].astype(F32)
            w = jnp.exp(jnp.sum(q * k, axis=0, keepdims=True))
            w_s[b, h : h + 1, :] = w
            total = total + w
            out = out + w * kv_ref[b, width + lo : width + hi, :].astype(F32)
        inverse = 1.0 / total
        for b in range(len(blocks)):
            p_ref[b, h : h + 1, :] = w_s[b, h : h + 1, :] * inverse
        mixed_ref[lo:hi, :] = (out * inverse).astype(BF16)
    h1 = start_ref[...].astype(F32) + tn(mixed_ref[...], wo_ref[...])
    h1 = h1.astype(BF16)
    h_ref[...] = h1
    xhat, _ = norm_parts(h1.astype(F32))
    normal = (xhat * gain_ref[1:2, :]).astype(BF16)
    normal_ref[...] = normal
    step = pl.program_id(0)
    brow = jnp.where(lat_ref[0] == 0, 31, 0)
    slot = iota((96, tile), 0)
    r, c = order_ref[...] // 32, order_ref[...] % 32
    pick = one_hot(
        ((slot < 32) & (r == brow) & (c == slot))
        | ((slot >= 32) & (slot < 64) & (c == 0) & (r == slot - 32))
        | ((slot >= 64) & (c == 31) & (r == slot - 64))
    )

    @pl.when(step == 0)
    def _():
        pack_s[...] = jnp.zeros_like(pack_s)

    pack_s[...] += nn(pick, normal)

    @pl.when(step == pl.num_programs(0) - 1)
    def _():
        for i, ref in enumerate((row_ref, left_ref, right_ref)):
            ref[...] = pack_s[i * 32 : i * 32 + 32, :].astype(BF16)


def write_halves(lat, total_ref, mine_ref, other_ref):
    half = mine_ref.shape[0]
    for band in range(2):

        @pl.when(lat == band)
        def _():
            mine_ref[...] = total_ref[band * half : (band + 1) * half, :].astype(BF16)
            other_ref[...] = total_ref[(1 - band) * half : (2 - band) * half, :].astype(BF16)


def second_kernel(
    lat_ref, place_ref, na_ref, nb_ref, row_ref, left_ref, right_ref, dleft_ref, dright_ref,
    w_all, wo_all, cot_ref,
    both_ref, dw_ref, brow_ref, bleft_ref, bright_ref,
    dq_ref, dk_ref, dv_ref, mixed_s, dkh_ref, dvh_ref, halo_s,
    q_s, k_s, v_s, kc_s, vc_s, dk_s, dv_s, dkc_s, dvc_s, do_s, mask_s, normal_s,
):
    points, width = cot_ref.shape
    head = width // HEADS
    w_ref, wo_ref = w_all.at[1], wo_all.at[1]
    upper = lat_ref[0] == 0
    halo_s[0:32, :] = row_ref[...]
    halo_s[32:64, :] = left_ref[...]
    halo_s[64:96, :] = right_ref[...]
    a, b = iota((16, 32), 0), iota((16, 32), 1)
    sent = b == jnp.where(upper, 0, 31)
    corners = nn(one_hot(sent & (a == 0)), dleft_ref[...])
    corners += nn(one_hot(sent & (a == 1)), dright_ref[...])
    halo_s[CORNER:HALO, :] = corners.astype(BF16)
    halo = halo_s[...]
    ordered = jnp.concatenate([na_ref[...], nb_ref[...]], 0)
    @pl.loop(0, points // 256)
    def _(step):
        rows = pl.ds(pl.multiple_of(step * 256, 256), 256)
        normal_s[rows, :] = picked(place_ref[rows, :], ordered).astype(BF16)
    normal = normal_s[...]
    scale = head**-0.5
    q_s[...] = (nn(normal, w_ref[:, 0:width]).astype(BF16).astype(F32) * scale).astype(BF16)
    k_s[32 : 32 + points, :] = nn(normal, w_ref[:, width : 2 * width]).astype(BF16)
    v_s[32 : 32 + points, :] = nn(normal, w_ref[:, 2 * width : 3 * width]).astype(BF16)
    kh = nn(halo, w_ref[:, width : 2 * width]).astype(BF16)
    vh = nn(halo, w_ref[:, 2 * width : 3 * width]).astype(BF16)
    for at in (0, 32 + points):
        k_s[at : at + 32, :] = kh[0:32]
        v_s[at : at + 32, :] = vh[0:32]
    tiles = points // 128
    slots = tiles * 16
    a, b = iota((slots, HALO - 32), 0), iota((slots, HALO - 32), 1)
    place, is_right = a % 16, jnp.where(a % 16 >= 6, 1, 0)
    ext_row = 4 * (a // 16) + place - 6 * is_right
    inner = (ext_row >= 1) & (ext_row <= 32)
    source = jnp.where(inner, 32 * is_right + ext_row - 1, 64 + is_right)
    spread_cols = one_hot((place < 12) & (b == source))
    kc_s[...] = nn(spread_cols, kh[32:HALO]).astype(BF16)
    vc_s[...] = nn(spread_cols, vh[32:HALO]).astype(BF16)
    dk_s[...] = jnp.zeros_like(dk_s)
    dv_s[...] = jnp.zeros_like(dv_s)
    cot = cot_ref[...].astype(BF16)
    both_ref[:, width : 2 * width] = cot
    do_s[...] = nt(cot, wo_ref[...]).astype(BF16)

    key, query = iota((KEYS, 256), 0), iota((KEYS, 256), 1) % 128
    place = key - 192
    right = place >= 6
    row = jnp.where(place < 0, key // 32, jnp.where(right, place - 6, place))
    col = jnp.where(place < 0, key % 32, jnp.where(right, 32, -1))
    near = (jnp.abs(row - 1 - query // 32) <= 1) & (jnp.abs(col - query % 32) <= 1)
    mask_s[...] = jnp.where(near & (place < 12), row, 9)

    def tile_step(t, carry):
        base = pl.multiple_of(t * 128, 128)
        first = jnp.where(upper & (t == 0), 1, 0)
        last = jnp.where(jnp.logical_not(upper) & (t == tiles - 1), 4, 5)
        mask = (mask_s[...] >= first) & (mask_s[...] <= last)
        even = iota((128, 128), 1) < 64
        top = iota((128, 128), 0) < 64
        win, here = pl.ds(base, 192), pl.ds(base, 128)
        side = pl.ds(pl.multiple_of(t * 16, 16), 16)
        for pair in range(HEADS // 2):
            lanes = slice(pair * 128, pair * 128 + 128)
            q = q_s[here, lanes]
            do = do_s[here, lanes]
            zero = jnp.zeros_like(q)
            qm = jnp.concatenate([jnp.where(even, q, zero), jnp.where(even, zero, q)], 0)
            dom = jnp.concatenate([jnp.where(even, do, zero), jnp.where(even, zero, do)], 0)
            k = jnp.concatenate([k_s[win, lanes], kc_s[side, lanes]], 0)
            v = jnp.concatenate([v_s[win, lanes], vc_s[side, lanes]], 0)
            w = jnp.where(mask, jnp.exp(nt(k, qm)), 0.0)
            p = w * (1.0 / jnp.sum(w, axis=0, keepdims=True))
            dp = nt(v, dom)
            delta = jnp.sum(p * dp, axis=0, keepdims=True)
            ds = (p * (dp - delta)).astype(BF16)
            p = p.astype(BF16)
            out = tn(v, p)
            mixed_s[lanes, here] = jnp.where(top, out[:, 0:128], out[:, 128:256]).astype(BF16)
            dq = tn(k, ds) * scale
            dq_ref[lanes, here] = jnp.where(top, dq[:, 0:128], dq[:, 128:256]).astype(BF16)
            dk, dv = nn(ds, qm), nn(p, dom)
            dk_s[win, lanes] += dk[0:192]
            dv_s[win, lanes] += dv[0:192]
            dkc_s[side, lanes] = dk[192:KEYS].astype(BF16)
            dvc_s[side, lanes] = dv[192:KEYS].astype(BF16)
        return carry

    lax.fori_loop(0, tiles, tile_step, 0)

    row_at = pl.multiple_of(jnp.where(upper, 32 + points, 0), 32)
    dkh = jnp.concatenate([dk_s[pl.ds(row_at, 32), :], tn(spread_cols, dkc_s[...])], 0).astype(BF16)
    dvh = jnp.concatenate([dv_s[pl.ds(row_at, 32), :], tn(spread_cols, dvc_s[...])], 0).astype(BF16)
    dkh_ref[...] = dkh
    dvh_ref[...] = dvh
    dk_ref[...] = dk_s[32 : 32 + points, :].astype(BF16)
    dv_ref[...] = dv_s[32 : 32 + points, :].astype(BF16)
    wk, wv = (w_ref[:, i * width : (i + 1) * width] for i in (1, 2))
    back = (nt(dkh, wk) + nt(dvh, wv)).astype(BF16)
    brow_ref[...] = back[0:32]
    for ref, at in ((bleft_ref, 32), (bright_ref, 64)):
        ref[0:32, :] = back[at : at + 32]
        ref[32:48, :] = back[CORNER:HALO]
    wq, wk, wv = (w_all[1, :, i * width : (i + 1) * width] for i in range(3))
    dw_ref[0:width, :] = nn(dq_ref[...], normal).astype(BF16)
    dw_ref[width : 2 * width, :] = (tn(dk_ref[...], normal) + tn(dkh_ref[...], halo)).astype(BF16)
    dw_ref[2 * width : 3 * width, :] = (
        tn(dv_ref[...], normal) + tn(dvh_ref[...], halo)
    ).astype(BF16)
    dw_ref[3 * width : 4 * width, :] = nn(mixed_s[...], cot).astype(BF16)
    both_ref[:, 0:width] = (tt(dq_ref[...], wq) + nt(dk_ref[...], wk) + nt(dv_ref[...], wv)).astype(BF16)


def third_kernel(
    lat_ref, order_ref, n0, n1, n2, n3, n4, n5, q_ref, kv_ref, p_ref, mixed_ref, h_ref, both_ref,
    packs_ref, wt_ref, wo_ref, gain_ref, dw_in,
    dh_ref, d0, d1, d2, d3, d4, d5, dw_ref, other_ref,
    dw_s, dmix_s, dkv_s, dq_s, dp_s, n_s,
):
    width, tile = q_ref.shape
    head = width // HEADS
    scale = head**-0.5
    blocks = (n0, n1, n2, n3, n4, n5)
    outs = (d0, d1, d2, d3, d4, d5)
    step = pl.program_id(0)

    @pl.when(step == 0)
    def _():
        dw_s[...] = jnp.zeros_like(dw_s) if dw_in is None else dw_in[...]

    token = order_ref[...]
    both = picked(token, both_ref[...])
    dn = both[:, 0:width]
    if packs_ref is not None:
        brow = jnp.where(lat_ref[0] == 0, 31, 0)
        r, c, slot = token // 32, token % 32, iota((tile, RETURNED), 1)
        border = r == brow
        place = one_hot(
            (border & (slot < 32) & (slot == c))
            | ((c == 0) & (slot < 64) & (slot == 32 + r))
            | ((c == 31) & (slot < 112) & (slot == 80 + r))
            | (border & (c == 0) & (slot == 128 + 33))
            | (border & (c == 31) & (slot == 176 + 32))
        )
        dn = dn + nn(place, packs_ref[...])
    dh = norm_back(h_ref[...].astype(F32), gain_ref[1:2, :], dn)
    dh_ref[...] = dh
    dh = dh + both[:, width : 2 * width]
    dhb = dh.astype(BF16)
    dmix_s[...] = nt(wo_ref[...], dhb)
    dw_s[3 * width : 4 * width, :] += nn(mixed_ref[...], dhb)
    for h in range(HEADS):
        lo, hi = h * head, (h + 1) * head
        dmix = dmix_s[lo:hi, :]
        delta = jnp.zeros((1, tile), F32)
        for b in range(len(blocks)):
            dp = jnp.sum(
                dmix * kv_ref[b, width + lo : width + hi, :].astype(F32), axis=0, keepdims=True
            )
            dp_s[b : b + 1, :] = dp
            delta = delta + p_ref[b, h : h + 1, :] * dp
        q = q_ref[lo:hi, :].astype(F32)
        dq = jnp.zeros((head, tile), F32)
        for b in range(len(blocks)):
            p = p_ref[b, h : h + 1, :]
            ds = p * (dp_s[b : b + 1, :] - delta) * scale
            dq = dq + ds * kv_ref[b, lo:hi, :].astype(F32)
            here = slice(b * tile, (b + 1) * tile)
            dkv_s[lo:hi, here] = (ds * q).astype(BF16)
            dkv_s[width + lo : width + hi, here] = (p * dmix).astype(BF16)
        dq_s[lo:hi, :] = dq.astype(BF16)
    dq = dq_s[...]
    dw_s[0:width, :] += nn(dq, n0[...])
    for b, ref in enumerate(blocks):
        n_s[b * tile : (b + 1) * tile, :] = ref[...]
    dw_s[width : 3 * width, :] += nn(dkv_s[...], n_s[...])
    grads = tn(dkv_s[...], wt_ref[width : 3 * width])
    outs[0][...] = (grads[0:tile] + tn(dq, wt_ref[0:width])).astype(BF16)
    for b in range(1, len(blocks)):
        outs[b][...] = grads[b * tile : (b + 1) * tile].astype(BF16)

    @pl.when(step == pl.num_programs(0) - 1)
    def _():
        if other_ref is None:
            dw_ref[...] = dw_s[...]
        else:
            write_halves(lat_ref[0], dw_s, dw_ref, other_ref)


def last_kernel(place_ref, vis_ref, gain_ref, cot_ref, *refs):
    inputs, out_ref, high_s, low_s = refs[:-3], refs[-3], refs[-2], refs[-1]
    points, width = cot_ref.shape
    tile = 256
    at = 0
    while inputs:
        start_ref, dh_ref, own_ref, far_ref, near_ref = inputs[:5]
        for lo in range(0, start_ref.shape[0], tile):
            rows = slice(lo, lo + tile)
            dn = own_ref[rows].astype(F32) + far_ref[rows].astype(F32) + near_ref[rows].astype(F32)
            back = norm_back(start_ref[rows].astype(F32), gain_ref[0:1, :], dn)
            grad = dh_ref[rows] + back
            high = grad.astype(BF16)
            high_s[at : at + tile, :] = high
            low_s[at : at + tile, :] = (grad - high.astype(F32)).astype(BF16)
            at += tile
        inputs = inputs[5:]
    for lo in range(0, points, tile):
        rows = slice(lo, lo + tile)
        place = place_ref[rows, :]
        shown = shown_column(vis_ref[...], lo + iota((tile, 1), 0))
        grad = picked(place, high_s[...]) + picked(place, low_s[...]) + cot_ref[rows]
        out_ref[rows] = jnp.where(shown > 0.5, grad, 0.0)


def weights_kernel(
    factor, pieces, lat_ref, mine_ref, other_ref, wt_ref, gain_ref,
    qkv_ref, out_ref, gain_out_ref, rows_s,
):
    total, width = mine_ref.shape
    piece = total // pieces // 2
    lat = lat_ref[0]
    for ref, band in ((mine_ref, lat), (other_ref, 1 - lat)):
        for k in range(pieces):
            at = pl.multiple_of(band * (total // 2) + k * piece, 8)
            for layer in range(2):
                lo = (2 * k + layer) * piece
                rows_s[layer, pl.ds(at, piece), :] = ref[lo : lo + piece, :].astype(F32) * factor
    for layer in range(2):
        acc = jnp.zeros((1, width), F32)
        for i in range(3):
            lo, hi = i * width, (i + 1) * width
            grad = rows_s[layer, lo:hi, :]
            weight = wt_ref[layer, lo:hi, :].astype(F32)
            acc = acc + jnp.sum(weight * grad, axis=0, keepdims=True)
            qkv_ref[layer, :, lo:hi] = grad.T
        out_ref[layer] = rows_s[layer, 3 * width : 4 * width, :]
        gain_out_ref[layer : layer + 1, :] = acc / gain_ref[layer : layer + 1, :]


def call(
    kernel, out_shape, scratch=(), grid=None, in_specs=None, out_specs=None, us=1, aliases=None, mib=12
):
    return pl.pallas_call(
        kernel,
        out_shape=out_shape,
        grid_spec=pltpu.PrefetchScalarGridSpec(
            num_scalar_prefetch=0,
            grid=grid or (),
            in_specs=in_specs,
            out_specs=out_specs,
            scratch_shapes=list(scratch),
        ),
        input_output_aliases=aliases or {},
        cost_estimate=pl.CostEstimate(
            flops=int(us * 1e6 * 800), bytes_accessed=int(us * 1e6), transcendentals=0
        ),
        compiler_params=pltpu.CompilerParams(vmem_limit_bytes=mib * 1024 * 1024),
    )


def whole():
    return pl.BlockSpec(memory_space=pltpu.VMEM)


def scalar():
    return pl.BlockSpec(memory_space=pltpu.SMEM)


def fixed(shape):
    return pl.BlockSpec(shape, lambda i: (0,) * len(shape))


def token_spec(tile, width, first=0):
    at = first // tile
    return pl.BlockSpec((tile, width), lambda i: (i + at, 0))


def layer_spec(layer, rows, width):
    return pl.BlockSpec((None, rows, width), lambda i: (layer, 0, 0))


CHUNKS = 2
FORWARD_TILE = 256
BACKWARD_TILE = 256


def run_first(first, lat, order, blocks, start, wt, output_weight, norm_gain_table):
    size, width = start.shape
    tile = min(FORWARD_TILE, size)
    struct = jax.ShapeDtypeStruct
    part = struct((size, width), BF16)
    tok_spec = token_spec(tile, width)
    feat_spec = pl.BlockSpec((width, tile), lambda i: (0, i))
    at = first // tile
    return call(
        first_kernel,
        (
            struct((width, size), BF16),
            struct((6, 2 * width, size), BF16),
            struct((6, 8, size), F32),
            struct((width, size), BF16),
            part,
            part,
            *[struct((32, width), BF16)] * 3,
        ),
        grid=(size // tile,),
        in_specs=[scalar(), pl.BlockSpec((1, tile), lambda i: (0, i + at))]
        + [tok_spec] * 7
        + [
            layer_spec(0, 3 * width, width),
            layer_spec(0, width, width),
            fixed((2, width)),
        ],
        out_specs=(
            feat_spec,
            pl.BlockSpec((6, 2 * width, tile), lambda i: (0, 0, i)),
            pl.BlockSpec((6, 8, tile), lambda i: (0, 0, i)),
            feat_spec,
            tok_spec,
            tok_spec,
            *[fixed((32, width))] * 3,
        ),
        scratch=[pltpu.VMEM((6, 8, tile), F32), pltpu.VMEM((96, width), F32)],
        mib=LARGE_MIB,
        us=8,
    )(lat, order, *blocks, start, wt, output_weight, norm_gain_table)


def run_second(lat, places, normals, halos, query_key_value_weight, output_weight, cot):
    points, width = cot.shape
    struct = jax.ShapeDtypeStruct
    ext, slots = points + 64, points // 8
    across = pltpu.VMEM((width, points), BF16)
    every, halo = pltpu.VMEM((points, width), BF16), pltpu.VMEM((HALO, width), BF16)
    return call(
        second_kernel,
        (
            struct((points, 2 * width), BF16),
            struct((4 * width, width), BF16),
            struct((32, width), BF16),
            struct((48, width), BF16),
            struct((48, width), BF16),
        ),
        in_specs=[scalar()] + [whole()] * 11,
        out_specs=(whole(),) * 5,
        scratch=[
            across, every, every, across,
            *[halo] * 3,
            every,
            pltpu.VMEM((ext, width), BF16),
            pltpu.VMEM((ext, width), BF16),
            *[pltpu.VMEM((slots, width), BF16)] * 2,
            pltpu.VMEM((ext, width), F32),
            pltpu.VMEM((ext, width), F32),
            *[pltpu.VMEM((slots, width), BF16)] * 2,
            every,
            pltpu.VMEM((KEYS, 256), jnp.int32),
            every,
        ],
        mib=LARGE_MIB,
        us=22,
    )(lat, places, *normals, *halos, query_key_value_weight, output_weight, cot)


def inner_third_kernel(*refs):
    third_kernel(*refs[:14], None, *refs[14:17], None, *refs[17:25], None, *refs[25:])


def run_third(
    first, lat, order, blocks, kept, both, packs, wt, output_weight, norm_gain_table, weights
):
    q0, kv0, p0, mixed0, h1 = kept
    size, width = h1.shape
    points = both.shape[0]
    tile = min(BACKWARD_TILE, size)
    struct = jax.ShapeDtypeStruct
    part = struct((size, width), BF16)
    tok_spec = token_spec(tile, width)
    feat_spec = pl.BlockSpec((width, tile), lambda i: (0, i))
    final = packs is not None
    whole_dw, half_dw = (4 * width, width), (2 * width, width)
    return call(
        third_kernel if final else inner_third_kernel,
        (
            struct((size, width), F32),
            *[part] * 6,
            *([struct(half_dw, BF16)] * 2 if final else [struct(whole_dw, F32)]),
        ),
        grid=(size // tile,),
        in_specs=[scalar(), token_spec(tile, 1, first)]
        + [tok_spec] * 6
        + [
            feat_spec,
            pl.BlockSpec((6, 2 * width, tile), lambda i: (0, 0, i)),
            pl.BlockSpec((6, 8, tile), lambda i: (0, 0, i)),
            feat_spec,
            tok_spec,
        ]
        + [fixed((points, 2 * width))]
        + [fixed((RETURNED, width))] * final
        + [
            layer_spec(0, 3 * width, width),
            layer_spec(0, width, width),
            fixed((2, width)),
        ]
        + [fixed(whole_dw)] * final,
        out_specs=(*[tok_spec] * 7, *([fixed(half_dw)] * 2 if final else [fixed(whole_dw)])),
        scratch=[
            pltpu.VMEM(whole_dw, F32),
            pltpu.VMEM((width, tile), F32),
            pltpu.VMEM((2 * width, 6 * tile), BF16),
            pltpu.VMEM((width, tile), BF16),
            pltpu.VMEM((8, tile), F32),
            pltpu.VMEM((6 * tile, width), BF16),
        ],
        mib=LARGE_MIB,
        us=13,
    )(
        lat, order, *blocks, q0, kv0, p0, mixed0, h1, both, *([packs] if final else []), wt,
        output_weight, norm_gain_table, *([weights] if final else []),
    )


def local(
    tokens, visible, mask_token, norm_gain_table, query_key_value_weight, output_weight, cotangent
):
    rows, cols, width = tokens.shape
    points = rows * cols
    size = points // CHUNKS
    firsts = [c * size for c in range(CHUNKS)]
    lat_count, lon_count = lax.axis_size("lat"), lax.axis_size("lon")
    lat = lax.axis_index("lat").astype(jnp.int32).reshape(1)
    wt = jnp.swapaxes(query_key_value_weight, 1, 2)
    struct = jax.ShapeDtypeStruct
    tokens = tokens.reshape(points, width)
    cot = cotangent.reshape(points, width)
    part = struct((size, width), BF16)
    gain_spec = fixed((2, width))
    wt_spec, wo_spec = layer_spec(0, 3 * width, width), layer_spec(0, width, width)

    order, places = token_order(rows, cols)
    order_row = jnp.asarray(order.reshape(1, points))
    order, places = jnp.asarray(order.reshape(points, 1)), jnp.asarray(places.reshape(points, 1))

    small = 512
    starts, normals = [], []
    for first in firsts:
        start, normal = call(
            start_kernel,
            (part, part),
            grid=(size // small,),
            in_specs=[
                token_spec(small, 1, first),
                fixed((points, width)),
                fixed((rows, cols)),
                fixed((width,)),
                gain_spec,
            ],
            out_specs=(token_spec(small, width),) * 2,
            mib=LARGE_MIB,
            us=2,
        )(order, tokens, visible, mask_token, norm_gain_table)
        starts.append(start)
        normals.append(normal)

    swapped0 = lon_swap(normals[0])
    own1, swapped0, wt = lax.optimization_barrier((normals[1], swapped0, wt))
    swapped1 = lon_swap(own1)
    beyond0, beyond1 = lon_forward(swapped0), lon_forward(swapped1)
    near0, near1 = lat_swap(normals[0]), lat_swap(own1)

    def blocks_of(own, near, swapped, beyond):
        return [own, near, swapped, beyond, lat_swap(swapped), lat_swap(beyond)]

    blocks = [blocks_of(normals[0], near0, swapped0, beyond0), None]

    kept = []
    for c in range(CHUNKS):
        *keep, normal1, row, left, right = run_first(
            firsts[c], lat, order_row, blocks[c], starts[c], wt, output_weight, norm_gain_table
        )
        if c == 1:
            keep, normal1, halos = lax.optimization_barrier((keep, normal1, halos))
            halos = [*halos, lat_swap(halos[1]), lat_swap(halos[2])]
        kept.append((keep, normal1))
        if c == 0:
            beyond1, row, left, right = lax.optimization_barrier((beyond1, row, left, right))
            halos = [lat_swap(row), from_left(right), from_right(left)]
            blocks[1] = blocks_of(own1, near1, swapped1, beyond1)

    both1, dw1, brow, bleft, bright = run_second(
        lat, places, [kept[0][1], kept[1][1]], halos, query_key_value_weight, output_weight, cot
    )

    from_l, from_r, brow = from_left(bright), from_right(bleft), lat_swap(brow)
    stages = lon_factors()
    sum1 = halves_summed(
        lax.dynamic_slice_in_dim(dw1, lat[0] * 2 * width, 2 * width, 0),
        lax.dynamic_slice_in_dim(dw1, (1 - lat[0]) * 2 * width, 2 * width, 0),
    )
    both1, sum1 = chained(both1, sum1)
    border = (brow, from_l, from_r)

    def plus(a, b):
        return (a.astype(F32) + b.astype(F32)).astype(BF16)

    weights = packs = None
    sum_stages = list(stages)
    ends = []
    coming = returned = None
    for n, c in enumerate(range(CHUNKS)[::-1]):
        dh1, d0, d1, d2, d3, d4, d5, *weights = run_third(
            firsts[c], lat, order, blocks[c], kept[c][0], both1, packs, wt,
            output_weight, norm_gain_table, weights,
        )
        if n == 0:
            sum1 = stage_summed(sum1, sum_stages.pop(0))
        border, weights, sum1, d1, d2, d3, d4, d5, coming, returned = lax.optimization_barrier(
            (border, weights, sum1, d1, d2, d3, d4, d5, coming, returned)
        )
        if n == 0:
            brow, from_l, from_r = border
            packs = jnp.concatenate([brow, from_l, from_r, lat_swap(from_l), lat_swap(from_r)], 0)
        d3 = plus(d3, lat_swap(d5))
        d2 = plus(d2, lat_swap(d4))
        d1 = lat_swap(d1)
        if n == CHUNKS - 1:
            weights = [halves_summed(*weights)]
        weights, d1, d2, d3 = lax.optimization_barrier((weights, d1, d2, d3))
        if returned is not None:
            ends[-2][-1] = returned
        returned = None
        if coming is not None:
            returned = lon_swap(coming)
        coming = plus(d2, lon_backward(d3))
        weights = weights[0]
        ends.append([c, dh1, d0, d1, None])

    sum0 = stage_summed(weights, stages[0])
    for stage in sum_stages:
        sum1 = stage_summed(sum1, stage)
    sum0, sum1, coming, returned = lax.optimization_barrier((sum0, sum1, coming, returned))
    ends[-2][-1] = returned
    returned = lon_swap(coming)
    sum0 = stage_summed(sum0, stages[1])
    sum0, returned = lax.optimization_barrier((sum0, returned))
    ends[-1][-1] = returned
    for stage in stages[2:]:
        sum0 = stage_summed(sum0, stage)
    sums = jnp.concatenate([sum0, sum1], 0)
    for stage in stages[::-1]:
        sums = spread(sums, *stage)

    pieces = []
    for c, dh1, d0, near, far in ends:
        pieces.append((c, [starts[c], dh1, d0, far, near]))
    pieces = [array for _, arrays in sorted(pieces, key=lambda p: p[0]) for array in arrays]
    grad_tokens = call(
        last_kernel,
        struct((points, width), F32),
        in_specs=[whole()] * (4 + len(pieces)),
        out_specs=whole(),
        scratch=[pltpu.VMEM((points, width), BF16)] * 2,
        mib=LARGE_MIB,
        us=6,
    )(places, visible, norm_gain_table, cot, *pieces)
    sums, grad_tokens = chained(sums, grad_tokens)
    other = lat_swap(sums)
    factor = (points * lat_count * lon_count) ** (-0.5)
    g_qkv, g_out, g_gain = call(
        functools.partial(weights_kernel, factor, lon_count),
        (
            struct((2, width, 3 * width), F32),
            struct((2, width, width), F32),
            struct((2, width), F32),
        ),
        in_specs=[scalar()] + [whole()] * 4,
        out_specs=(whole(),) * 3,
        scratch=[pltpu.VMEM((2, 4 * width, width), F32)],
        mib=20,
        us=5,
    )(lat, sums, other, wt, norm_gain_table)
    return grad_tokens.reshape(rows, cols, width), g_qkv, g_out, g_gain


def without(kernel, at, count, *refs):
    kernel(*refs[:at], *[None] * count, *refs[at:])


def solution(mesh):
    return jax.shard_map(
        local,
        mesh=mesh,
        in_specs=(
            P(("group", "lat"), "lon", None),
            P(("group", "lat"), "lon"),
            P(),
            P(),
            P(),
            P(),
            P(("group", "lat"), "lon", None),
        ),
        out_specs=(
            P(("group", "lat"), "lon", None),
            P("group", None, None),
            P("group", None, None),
            P("group", None),
        ),
        check_vma=False,
    )
```
